128 devices in a mesh: req: 8 (over z, core), tok: 16 (over y, x).
Axes of the slice: x: 4, y: 4, z: 4, core: 2. Of those that a mesh axis runs over, the one named last changes fastest.
Arguments:
- draft_ids: int32 [32, 16], replicated, may hold values from 0 to 65535
- lengths: int32 [32], replicated, may hold values from 1 to 16384, as said below
- current_slot: int32 [32], replicated, may hold values from 0 to 31, as said below
- new_slot: int32 [32], replicated, may hold values from 0 to 31, as said below
- accepted: int32 [32], replicated, may hold values from 1 to 16, as said below
- embed_table: bfloat16 [65536, 3072], P(('req', 'tok')), may hold values from -6.5 to 6.5
- mixer_gain: float32 [3072], replicated, may hold values from 0.5 to 1.5
- query_weight: bfloat16 [3072, 768], replicated, may hold values from -0.3049512 to 0.3049512
- keyvalue_weight: bfloat16 [3072, 256], replicated, may hold values from -0.109375 to 0.109375
- key_cache: bfloat16 [32, 16384, 128], P('req', 'tok'), may hold values from -6 to 6
- value_cache: bfloat16 [32, 16384, 128], P('req', 'tok'), may hold values from -6 to 6
- attention_out: bfloat16 [768, 3072], P(None, 'tok'), may hold values from -0.21875 to 0.21875
- mamba_input: bfloat16 [3072, 2048], P(None, 'tok'), may hold values from -0.109375 to 0.109375
- mamba_gate: bfloat16 [3072, 2048], P(None, 'tok'), may hold values from -0.109375 to 0.109375
- state_proj: bfloat16 [3072, 512], replicated, may hold values from -0.02734375 to 0.02734375
- mamba_step: bfloat16 [3072, 16], P(None, 'tok'), may hold values from -0.109375 to 0.109375
- step_bias: float32 [16], P('tok'), may hold values from -4 to 0
- decay_log: float32 [16], P('tok'), may hold values from -2 to 1.5
- skip_gain: float32 [16], P('tok'), may hold values from 0.5 to 1.5
- states: float32 [32, 16, 128, 256], P('req', 'tok'), may hold values from -1.5 to 1.5
- mamba_out: bfloat16 [2048, 3072], P('tok'), may hold values from -0.125 to 0.125
- mlp_gain: float32 [3072], replicated, may hold values from 0.5 to 1.5
- gate_weight: bfloat16 [3072, 12288], P(None, ('req', 'tok')), may hold values from -0.109375 to 0.109375
- up_weight: bfloat16 [3072, 12288], P(None, ('req', 'tok')), may hold values from -0.109375 to 0.109375
- down_weight: bfloat16 [3072, 12288], P(None, ('req', 'tok')), may hold values from -0.0546875 to 0.0546875
Outputs:
- hidden_out: bfloat16 [512, 3072], P(('req', 'tok'))
- new_states: float32 [32, 16, 128, 256], P('req', 'tok')
The draws below stay inside these ranges and needn't reach their ends.
Inputs may be any that keep to these rules, and one draw needn't show every extreme that they name: `lengths`: some request has exactly 16384 cached positions and some exactly one. `current_slot`: a permutation: each slot holds one request. `new_slot`: a permutation: each slot receives one request. `accepted`: some request accepts all 16 drafts and some exactly one.
All inputs are finite; a program needn't handle non-finite values.
Results may differ from the reference program's by a relative error of at most 0.02.
Values may be sent and summed in bfloat16 or wider, within the bound.
No kernel may reach another device: no remote copies, remote signals or barrier semaphores. Data moves between devices by JAX's collectives and lax.ppermute only.
A program may use at most 128 MiB of HBM per device.

```python
import math
import jax
import jax.numpy as jnp
import numpy as np
from jax import lax

D = 3072
FF = 12288
HEAD = 128
MHEAD = 128
MSTATE = 256
QHEADS = 6
MHEADS = 16
DRAFT = 16
REQ = 32
TOKENS = 512
CACHE = 16384
VOCAB = 65536


def mark_ends(key, values, top_value, low_value):
    shuffled = jax.random.permutation(key, values.shape[0])
    return values.at[shuffled[0]].set(top_value).at[shuffled[1]].set(low_value)


def draw_lengths(key, part):
    first_key, second_key = jax.random.split(jax.random.fold_in(key, 5))
    values = jax.random.randint(first_key, (REQ,), 1, CACHE + 1, dtype=jnp.int32)
    return mark_ends(second_key, values, CACHE, 1)


def draw_accepted(key, part):
    first_key, second_key = jax.random.split(jax.random.fold_in(key, 7))
    values = jax.random.randint(first_key, (REQ,), 1, DRAFT + 1, dtype=jnp.int32)
    return mark_ends(second_key, values, DRAFT, 1)


def draw_current_slot(key, part):
    return jax.random.permutation(jax.random.fold_in(key, 11), REQ).astype(jnp.int32)


def draw_new_slot(key, part):
    return jax.random.permutation(jax.random.fold_in(key, 23), REQ).astype(jnp.int32)


def sign_vector(key, salt, count):
    picks = jax.random.randint(jax.random.fold_in(key, salt), (count,), 0, 2, dtype=jnp.int32)
    return (picks * 2 - 1).astype(jnp.float32)


def draw_embed_table(key, part):
    common_dir = sign_vector(key, 41, D)
    noise = jax.random.truncated_normal(jax.random.fold_in(key, 43), -6.0, 6.0, (VOCAB, D), jnp.float32)
    level = 0.5
    return (noise + level * common_dir[None, :]).astype(jnp.bfloat16)


def draw_query_weight(key, part):
    base = jax.random.truncated_normal(jax.random.fold_in(key, 47), -4.0, 4.0, (D, QHEADS * HEAD), jnp.float32) * (D // 16) ** (-0.5)
    common_dir = sign_vector(key, 41, D)
    key_dir = sign_vector(key, 31, HEAD)
    order = jax.random.permutation(jax.random.fold_in(key, 37), QHEADS)
    marked = (order < max(1, QHEADS // 3)).astype(jnp.float32)
    column_sign = (marked[:, None] * key_dir[None, :]).reshape(-1)
    return (base + 50.0 / D * common_dir[:, None] * column_sign[None, :]).astype(jnp.bfloat16)


def draw_key_cache(key, part):
    base = jax.random.truncated_normal(jax.random.fold_in(key, 53), -6.0, 6.0, (REQ, CACHE, HEAD), jnp.float32)
    lengths = draw_lengths(key, part)
    slots = draw_current_slot(key, part)
    owners = jnp.zeros((REQ,), jnp.int32).at[slots].set(jnp.arange(REQ, dtype=jnp.int32))
    slot_len = jnp.take(lengths, owners)
    first_pos = jax.random.randint(jax.random.fold_in(key, 59), (REQ,), 0, slot_len, dtype=jnp.int32)
    second_pos = jax.random.randint(jax.random.fold_in(key, 61), (REQ,), 0, slot_len, dtype=jnp.int32)
    strength = jnp.exp(jax.random.uniform(jax.random.fold_in(key, 67), (REQ,), jnp.float32, -0.6931, 0.4055))
    key_dir = sign_vector(key, 31, HEAD)
    planted = strength[:, None] * key_dir[None, :]
    gap_index = jax.random.randint(jax.random.fold_in(key, 71), (REQ,), 0, HEAD, dtype=jnp.int32)
    keep = (jnp.arange(HEAD, dtype=jnp.int32)[None, :] != gap_index[:, None]).astype(jnp.float32)
    rows = jnp.arange(REQ, dtype=jnp.int32)
    return base.at[rows, first_pos].set(planted).at[rows, second_pos].set(planted * keep).astype(jnp.bfloat16)


def set_ends(drawn, own_key, least, high):
    longest = drawn.shape.index(max(drawn.shape))
    spots = []
    for shift in (0, 1):
        where = [jax.random.randint(jax.random.fold_in(own_key, axis), (), 0, length) for axis, length in enumerate(drawn.shape)]
        where[longest] = (where[longest] + shift) % drawn.shape[longest]
        spots.append(tuple(where))
    return drawn.at[spots[0]].set(least).at[spots[1]].set(high)


def levels(own_key, shape, pieces, smallest, high):
    gain, own = 1.0, jax.random.fold_in(own_key, 6)
    for dim, shards_of in pieces:
        steps = jnp.exp(jax.random.uniform(jax.random.fold_in(own, dim), (shards_of,), jnp.float32, smallest / len(pieces), high / len(pieces)))
        gain = gain * jnp.repeat(steps, shape[dim] // shards_of).reshape([-1 if axis == dim else 1 for axis in range(len(shape))])
    return gain


def cumulative_ranks(amount, slope):
    portions = [(1 << 20) // math.isqrt(grade ** slope) + 1 for grade in range(1, amount + 1)]
    width = 1 + sum(portions) // (1 << 30)
    return np.cumsum(np.array([max(1, weight // width) for weight in portions]))


def ranked(rng, extent, count, lean):
    table = cumulative_ranks(count, lean)
    lot = jax.random.randint(jax.random.fold_in(rng, 1), extent, 0, int(table[count - 1]))
    grade = jnp.searchsorted(jnp.asarray(table, jnp.int32), lot, side="right")
    return jax.random.permutation(jax.random.fold_in(rng, 2), count)[grade].astype(jnp.int32)


def centred(stream_key, shape, width, limit, shards=(), kind=jnp.bfloat16):
    loudness = levels(stream_key, shape, shards, -0.22, 0.18) if shards else 1.0
    entries = jax.random.normal(stream_key, shape, jnp.float32) * width * loudness
    return jnp.minimum(jnp.maximum(entries, -limit), limit).astype(kind)


def setup_inputs(seed: int = 0) -> dict:
    key_list = jax.random.split(jax.random.key(seed), 26)
    draft_ids = set_ends(ranked(key_list[0], (REQ, DRAFT), VOCAB, 2), jax.random.fold_in(key_list[0], 3), 0, VOCAB - 1).astype(jnp.int32)
    lengths = draw_lengths(jax.random.fold_in(key_list[25], 71), 0)
    current_slot = draw_current_slot(jax.random.fold_in(key_list[25], 71), 0)
    new_slot = draw_new_slot(jax.random.fold_in(key_list[25], 71), 0)
    accepted = draw_accepted(jax.random.fold_in(key_list[25], 71), 0)
    embed_table = draw_embed_table(jax.random.fold_in(key_list[25], 71), 0)
    mixer_gain = jnp.clip(1.0 + 0.1 * jax.random.normal(key_list[6], (D,), jnp.float32), 0.5, 1.5)
    query_weight = draw_query_weight(jax.random.fold_in(key_list[25], 71), 0)
    keyvalue_weight = centred(key_list[8], (D, 2 * HEAD), D ** -0.5, 0.109375)
    key_cache = draw_key_cache(jax.random.fold_in(key_list[25], 71), 0)
    value_cache = centred(key_list[10], (REQ, CACHE, HEAD), 1.0, 6.0, ((0, 8), (1, 16)))
    attention_out = centred(key_list[11], (QHEADS * HEAD, D), (QHEADS * HEAD) ** -0.5, 0.21875, ((1, 16),))
    mamba_input = centred(key_list[12], (D, MHEADS * MHEAD), D ** -0.5, 0.109375, ((1, 16),))
    mamba_gate = centred(key_list[13], (D, MHEADS * MHEAD), D ** -0.5, 0.109375, ((1, 16),))
    state_proj = centred(key_list[14], (D, 2 * MSTATE), (16 * D) ** -0.5, 0.02734375)
    mamba_step = centred(key_list[15], (D, MHEADS), D ** -0.5, 0.109375, ((1, 16),))
    step_bias = jnp.clip(-4.0 + 4.0 * jax.random.uniform(key_list[16], (MHEADS,), jnp.float32) ** levels(key_list[16], (MHEADS,), ((0, 16),), -0.2, 0.2), -4.0, 0.0)
    decay_log = jnp.clip(-2.0 + 3.5 * jax.random.uniform(key_list[17], (MHEADS,), jnp.float32) ** levels(key_list[17], (MHEADS,), ((0, 16),), -0.2, 0.2), -2.0, 1.5)
    skip_gain = jnp.clip(0.5 + 1.0 * jax.random.uniform(key_list[18], (MHEADS,), jnp.float32) ** levels(key_list[18], (MHEADS,), ((0, 16),), -0.2, 0.2), 0.5, 1.5)
    states = centred(key_list[19], (REQ, MHEADS, MHEAD, MSTATE), 0.25, 1.5, ((0, 8), (1, 16)), jnp.float32)
    mamba_out = centred(key_list[20], (MHEADS * MHEAD, D), (MHEADS * MHEAD) ** -0.5, 0.125, ((0, 16),))
    mlp_gain = jnp.clip(1.0 + 0.1 * jax.random.normal(key_list[21], (D,), jnp.float32), 0.5, 1.5)
    gate_weight = centred(key_list[22], (D, FF), D ** -0.5, 0.109375, ((1, 128),))
    up_weight = centred(key_list[23], (D, FF), D ** -0.5, 0.109375, ((1, 128),))
    down_weight = centred(key_list[24], (D, FF), FF ** -0.5, 0.0546875, ((1, 128),))
    return dict(draft_ids=draft_ids, lengths=lengths, current_slot=current_slot, new_slot=new_slot, accepted=accepted, embed_table=embed_table, mixer_gain=mixer_gain, query_weight=query_weight, keyvalue_weight=keyvalue_weight, key_cache=key_cache, value_cache=value_cache, attention_out=attention_out, mamba_input=mamba_input, mamba_gate=mamba_gate, state_proj=state_proj, mamba_step=mamba_step, step_bias=step_bias, decay_log=decay_log, skip_gain=skip_gain, states=states, mamba_out=mamba_out, mlp_gain=mlp_gain, gate_weight=gate_weight, up_weight=up_weight, down_weight=down_weight)


def rms_rows(table_rows, norm_gain):
    values = table_rows.astype(jnp.float32)
    factor = lax.rsqrt(lax.optimization_barrier(jnp.mean(values * values, axis=-1, keepdims=True)) + 1e-05)
    return (values * factor * norm_gain.astype(jnp.float32)).astype(jnp.bfloat16)

def inverse_of(mapping):
    places = jnp.arange(mapping.shape[0], dtype=jnp.int32)
    matches = mapping[None, :] == places[:, None]
    return lax.optimization_barrier(jnp.sum(jnp.where(matches, places[None, :], 0), axis=1)).astype(jnp.int32)

def recurrence(start_states, decay_rate, inputs, state_in, state_read, accept_count):

    def advance(state_pair, step_items):
        current, chosen = state_pair
        step_decay, step_input, step_in, step_read, step_index = step_items
        current = step_decay[:, :, None, None] * current + step_input[..., None] * step_in[:, None, None, :]
        readout = lax.optimization_barrier(jnp.sum(current * step_read[:, None, None, :], axis=-1))
        chosen = jnp.where((accept_count == step_index + 1)[:, None, None, None], current, chosen)
        return ((current, chosen), readout)
    sequence = (jnp.swapaxes(decay_rate, 0, 1), jnp.swapaxes(inputs, 0, 1), jnp.swapaxes(state_in, 0, 1), jnp.swapaxes(state_read, 0, 1), jnp.arange(decay_rate.shape[1], dtype=jnp.int32))
    (current, chosen), readouts = lax.scan(advance, (start_states, start_states), sequence)
    return (jnp.swapaxes(readouts, 0, 1), chosen)

def reference(draft_ids, lengths, current_slot, new_slot, accepted, embed_table, mixer_gain, query_weight, keyvalue_weight, key_cache, value_cache, attention_out, mamba_input, mamba_gate, state_proj, mamba_step, step_bias, decay_log, skip_gain, states, mamba_out, mlp_gain, gate_weight, up_weight, down_weight):
    slot_owner = inverse_of(current_slot)
    token_ids = jnp.take(draft_ids, slot_owner, axis=0).reshape(-1)
    embedded = jnp.take(embed_table, token_ids, axis=0)
    normed = rms_rows(embedded, mixer_gain)
    queries = lax.optimization_barrier(jnp.dot(normed, query_weight, preferred_element_type=jnp.float32).astype(jnp.bfloat16))
    keyvalue = lax.optimization_barrier(jnp.dot(normed, keyvalue_weight, preferred_element_type=jnp.float32).astype(jnp.bfloat16))
    queries = queries.reshape(REQ, DRAFT, QHEADS, HEAD)
    keyvalue = keyvalue.reshape(REQ, DRAFT, 2, HEAD)
    slot_length = jnp.take(lengths, slot_owner)
    slot_accept = jnp.take(accepted, slot_owner)
    score_scale = HEAD ** (-0.5)
    positions = jnp.arange(CACHE, dtype=jnp.int32)
    causal = jnp.arange(DRAFT)[None, :] <= jnp.arange(DRAFT)[:, None]

    def attend(slot_items):
        slot_queries, slot_keys, slot_values, slot_new, slot_len = slot_items
        query_full = slot_queries.astype(jnp.float32)
        cache_scores = jnp.einsum('thd,pd->thp', query_full, slot_keys.astype(jnp.float32)) * score_scale
        draft_scores = jnp.einsum('thd,ud->thu', query_full, slot_new[:, 0].astype(jnp.float32)) * score_scale
        visible = (positions < slot_len)[None, None, :]
        draft_mask = causal[:, None, :]
        top_score = jnp.maximum(lax.optimization_barrier(jnp.max(jnp.where(visible, cache_scores, -1e+30), axis=-1)), lax.optimization_barrier(jnp.max(jnp.where(draft_mask, draft_scores, -1e+30), axis=-1)))
        cache_probs = jnp.where(visible, jnp.exp(cache_scores - top_score[..., None]), 0.0)
        draft_probs = jnp.where(draft_mask, jnp.exp(draft_scores - top_score[..., None]), 0.0)
        prob_total = lax.optimization_barrier(jnp.sum(cache_probs, axis=-1)) + lax.optimization_barrier(jnp.sum(draft_probs, axis=-1))
        cache_round = lax.optimization_barrier(cache_probs.astype(jnp.bfloat16)).astype(jnp.float32)
        draft_round = lax.optimization_barrier(draft_probs.astype(jnp.bfloat16)).astype(jnp.float32)
        summed = jnp.einsum('thp,pd->thd', cache_round, slot_values.astype(jnp.float32))
        summed = summed + jnp.einsum('thu,ud->thd', draft_round, slot_new[:, 1].astype(jnp.float32))
        return (summed / prob_total[..., None]).astype(jnp.bfloat16)
    attended = lax.map(attend, (queries, key_cache, value_cache, keyvalue, slot_length))
    attended = attended.reshape(TOKENS, QHEADS * HEAD)
    attn_proj = jnp.dot(attended, attention_out, preferred_element_type=jnp.float32)
    mamba_x = jnp.dot(normed, mamba_input, preferred_element_type=jnp.float32).reshape(REQ, DRAFT, MHEADS, MHEAD)
    mamba_z = jnp.dot(normed, mamba_gate, preferred_element_type=jnp.float32).reshape(REQ, DRAFT, MHEADS, MHEAD)
    both_proj = jnp.dot(normed, state_proj, preferred_element_type=jnp.float32).reshape(REQ, DRAFT, 2, MSTATE)
    step_size = jax.nn.softplus(jnp.dot(normed, mamba_step, preferred_element_type=jnp.float32) + step_bias.astype(jnp.float32)).reshape(REQ, DRAFT, MHEADS)
    decay_rate = jnp.exp(-jnp.exp(decay_log.astype(jnp.float32)) * step_size)
    readout, chosen = recurrence(states, decay_rate, step_size[..., None] * mamba_x, both_proj[:, :, 0], both_proj[:, :, 1], slot_accept)
    readout = readout + skip_gain.astype(jnp.float32)[None, None, :, None] * mamba_x
    gated = (readout * jax.nn.silu(mamba_z)).astype(jnp.bfloat16).reshape(TOKENS, MHEADS * MHEAD)
    mamba_proj = jnp.dot(gated, mamba_out, preferred_element_type=jnp.float32)
    mixed_rows = (embedded.astype(jnp.float32) + attn_proj + mamba_proj).astype(jnp.bfloat16)
    second = rms_rows(mixed_rows, mlp_gain)
    gate_part = jnp.dot(second, gate_weight, preferred_element_type=jnp.float32)
    up_part = jnp.dot(second, up_weight, preferred_element_type=jnp.float32)
    hidden = (jax.nn.silu(gate_part) * up_part).astype(jnp.bfloat16)
    mlp_sum = lax.dot_general(hidden, down_weight, (((1,), (1,)), ((), ())), preferred_element_type=jnp.float32)
    hidden_out = (mixed_rows.astype(jnp.float32) + mlp_sum).astype(jnp.bfloat16)
    sources = jnp.take(current_slot, inverse_of(new_slot))
    new_states = jnp.take(chosen, sources, axis=0)
    return (hidden_out, new_states)
```

```python
import functools

import jax
import jax.numpy as jnp
from jax import lax
from jax.experimental import pallas as pl
from jax.experimental.pallas import tpu as pltpu
from jax.sharding import PartitionSpec as P

BF = jnp.bfloat16
F32 = jnp.float32
NEG = -1e30
AUX = 128


def rms_rows(table_rows, norm_gain):
    values = table_rows.astype(F32)
    factor = lax.rsqrt(jnp.mean(values * values, axis=-1, keepdims=True) + 1e-05)
    return (values * factor * norm_gain).astype(BF)


def inverse_of(mapping):
    places = jnp.arange(mapping.shape[0], dtype=jnp.int32)
    matches = mapping[None, :] == places[:, None]
    return jnp.sum(jnp.where(matches, places[None, :], 0), axis=1)


def dot_nn(a, b, precision=None):
    return lax.dot_general(
        a, b, (((1,), (0,)), ((), ())), precision=precision, preferred_element_type=F32
    )


def dot_nt(a, b, precision=None):
    return lax.dot_general(
        a, b, (((1,), (1,)), ((), ())), precision=precision, preferred_element_type=F32
    )


def dot_tn(a, b, precision=None):
    return lax.dot_general(
        a, b, (((0,), (0,)), ((), ())), precision=precision, preferred_element_type=F32
    )


HI = lax.Precision.HIGHEST


def mixer_kernel(
    ints,
    reals,
    queries,
    keyvalue,
    keys,
    values,
    mamba_x,
    mamba_z,
    both,
    step,
    states,
    mamba_out,
    payload,
    chosen,
    *,
    heads,
):
    slot = pl.program_id(0)
    drafts = queries.shape[0]
    size = keys.shape[2]
    cache = keys.shape[1]
    length = ints[slot]
    member = ints[8]
    accept = ints[4 + slot]
    scale = size ** (-0.5)
    query = jnp.concatenate([queries[:, h * size : (h + 1) * size] for h in range(heads)], axis=0)
    rows = heads * drafts
    scores = dot_nt(query, keys[0]) * scale
    position = lax.broadcasted_iota(jnp.int32, (rows, cache), 1) + member * cache
    scores = jnp.where(position < length, scores, NEG)
    draft_scores = dot_nt(query, keyvalue[:, :size]) * scale
    token = lax.broadcasted_iota(jnp.int32, (heads, drafts, drafts), 1).reshape(rows, drafts)
    other = lax.broadcasted_iota(jnp.int32, (rows, drafts), 1)
    limit = jnp.where(member == 0, token, -1)
    draft_scores = jnp.where(other <= limit, draft_scores, NEG)
    top = jnp.maximum(
        jnp.max(scores, axis=-1, keepdims=True), jnp.max(draft_scores, axis=-1, keepdims=True)
    )
    probs = jnp.where(position < length, jnp.exp(scores - top), 0.0)
    draft_probs = jnp.where(other <= limit, jnp.exp(draft_scores - top), 0.0)
    total = jnp.sum(probs, axis=-1, keepdims=True) + jnp.sum(draft_probs, axis=-1, keepdims=True)
    summed = dot_nn(probs.astype(BF), values[0]) + dot_nn(
        draft_probs.astype(BF), keyvalue[:, size:]
    )
    for h in range(heads):
        payload[:, h * size : (h + 1) * size] = summed[h * drafts : (h + 1) * drafts].astype(BF)
    top_a = top.astype(BF).astype(F32)
    top_b = (top - top_a).astype(BF).astype(F32)
    top_c = top - top_a - top_b
    total_a = total.astype(BF).astype(F32)
    total_b = total - total_a
    lane = lax.broadcasted_iota(jnp.int32, (drafts, AUX), 1)
    aux = jnp.zeros((drafts, AUX), F32)
    for k, piece in enumerate((top_a, top_b, top_c, total_a, total_b)):
        for h in range(heads):
            part = piece[h * drafts : (h + 1) * drafts]
            aux = jnp.where(lane == k * heads + h, part, aux)
    payload[:, heads * size : heads * size + AUX] = aux.astype(BF)
    step_in = step[...] + reals[0]
    size_t = jnp.maximum(step_in, 0.0) + jnp.log1p(jnp.exp(-jnp.abs(step_in)))
    row = lax.broadcasted_iota(jnp.int32, (drafts, drafts), 0)
    col = lax.broadcasted_iota(jnp.int32, (drafts, drafts), 1)
    size_row = jnp.sum(jnp.where(row == col, size_t, 0.0), axis=0, keepdims=True)
    log_decay = -reals[1] * jnp.sum(
        jnp.where(col <= row, size_row, 0.0), axis=1, keepdims=True
    )
    log_row = jnp.sum(jnp.where(row == col, log_decay, 0.0), axis=0, keepdims=True)
    between = jnp.exp(jnp.where(col <= row, log_decay - log_row, NEG))
    state_size = both.shape[1] // 2
    state_in = both[:, :state_size]
    state_read = both[:, state_size:]
    x = mamba_x[...]
    inputs = size_t * x
    start = states[0, 0]
    weights = dot_nt(state_read, state_in, HI) * between
    readout = dot_nn(weights, inputs, HI) + jnp.exp(log_decay) * dot_nt(state_read, start, HI)
    readout = readout + reals[2] * x
    rows_in = lax.broadcasted_iota(jnp.int32, (drafts, 1), 0)
    last = jnp.sum(jnp.where(rows_in == accept - 1, log_decay, 0.0), axis=0, keepdims=True)
    remain = jnp.exp(jnp.where(rows_in < accept, last - log_decay, NEG))
    chosen[0, 0] = (jnp.exp(last) * start + dot_tn(remain * inputs, state_in, HI)).astype(BF)
    z = mamba_z[...]
    gated = (readout * (z / (1.0 + jnp.exp(-z)))).astype(BF)
    payload[:, heads * size + AUX :] = dot_nn(gated, mamba_out[...]).astype(BF)


def mixer(ints, reals, queries, keyvalue, keys, values, x, z, both, step, states, mamba_out):
    slots, cache, size = keys.shape
    tokens = queries.shape[0]
    drafts = tokens // slots
    heads = queries.shape[1] // size
    width = heads * size + AUX + mamba_out.shape[1]
    rows = lambda a: pl.BlockSpec((drafts, a.shape[1]), lambda s: (s, 0))
    smem = pl.BlockSpec(memory_space=pltpu.SMEM)
    return pl.pallas_call(
        functools.partial(mixer_kernel, heads=heads),
        grid=(slots,),
        in_specs=[
            smem,
            smem,
            rows(queries),
            rows(keyvalue),
            pl.BlockSpec((1, cache, size), lambda s: (s, 0, 0)),
            pl.BlockSpec((1, cache, size), lambda s: (s, 0, 0)),
            rows(x),
            rows(z),
            rows(both),
            rows(step),
            pl.BlockSpec((1, 1) + states.shape[2:], lambda s: (s, 0, 0, 0)),
            pl.BlockSpec(mamba_out.shape, lambda s: (0, 0)),
        ],
        out_specs=[
            pl.BlockSpec((drafts, width), lambda s: (s, 0)),
            pl.BlockSpec((1, 1) + states.shape[2:], lambda s: (s, 0, 0, 0)),
        ],
        out_shape=[
            jax.ShapeDtypeStruct((tokens, width), BF),
            jax.ShapeDtypeStruct(states.shape, BF),
        ],
        compiler_params=pltpu.CompilerParams(vmem_limit_bytes=40 << 20),
        name="mixer",
    )(ints, reals, queries, keyvalue, keys, values, x, z, both, step, states, mamba_out)


def join_kernel(parts, embedded, out_weight, gain, mixed, second, *, heads, size):
    aux = parts[:, :, heads * size : heads * size + AUX].astype(F32)
    pieces = []
    for h in range(heads):
        get = lambda k: aux[:, :, k * heads + h : k * heads + h + 1]
        top = get(0) + get(1) + get(2)
        total = get(3) + get(4)
        factor = jnp.exp(top - jnp.max(top, axis=0, keepdims=True))
        whole = jnp.sum(factor * total, axis=0)
        value = parts[:, :, h * size : (h + 1) * size].astype(F32)
        summed = jnp.sum(factor * value, axis=0)
        pieces.append((summed / whole).astype(BF))
    attended = jnp.concatenate(pieces, axis=1)
    attn = dot_nt(attended, out_weight[...])
    mamba = jnp.sum(parts[:, :, heads * size + AUX :].astype(F32), axis=0)
    rows = (embedded[...].astype(F32) + attn + mamba).astype(BF)
    mixed[...] = rows
    wide = rows.astype(F32)
    factor = lax.rsqrt(jnp.mean(wide * wide, axis=-1, keepdims=True) + 1e-05)
    normed = (wide * factor * gain[...]).astype(BF)
    for j in range(second.shape[0]):
        second[j] = normed


def join(parts, embedded, out_weight, gain, heads, size):
    vm = pl.BlockSpec(memory_space=pltpu.VMEM)
    return pl.pallas_call(
        functools.partial(join_kernel, heads=heads, size=size),
        in_specs=[vm] * 4,
        out_specs=[vm] * 2,
        out_shape=[
            jax.ShapeDtypeStruct(embedded.shape, BF),
            jax.ShapeDtypeStruct((parts.shape[0],) + embedded.shape, BF),
        ],
        compiler_params=pltpu.CompilerParams(vmem_limit_bytes=40 << 20),
        name="join",
    )(parts, embedded, out_weight, gain)


def pick_kernel(sources, states, out):
    out[...] = states[...].astype(F32)


def pick_states(sources, states, count):
    block = (1,) + states.shape[1:]
    zeros = (0,) * (len(block) - 1)
    return pl.pallas_call(
        pick_kernel,
        grid_spec=pltpu.PrefetchScalarGridSpec(
            num_scalar_prefetch=1,
            grid=(count,),
            in_specs=[pl.BlockSpec(block, lambda i, src: (src[i],) + zeros)],
            out_specs=pl.BlockSpec(block, lambda i, src: (i,) + zeros),
        ),
        out_shape=jax.ShapeDtypeStruct((count,) + states.shape[1:], F32),
        name="pick",
    )(sources, states)


def local(
    draft_ids,
    lengths,
    current_slot,
    new_slot,
    accepted,
    embed_table,
    mixer_gain,
    query_weight,
    keyvalue_weight,
    key_cache,
    value_cache,
    attention_out,
    mamba_input,
    mamba_gate,
    state_proj,
    mamba_step,
    step_bias,
    decay_log,
    skip_gain,
    states,
    mamba_out,
    mlp_gain,
    gate_weight,
    up_weight,
    down_weight,
):
    members = lax.axis_size("tok")
    groups = lax.axis_size("req")
    group_index = lax.axis_index("req")
    member = lax.axis_index("tok")
    slots_dev, cache_dev, head_size = key_cache.shape
    draft_len = draft_ids.shape[1]
    vocab_dev, width = embed_table.shape
    query_heads = query_weight.shape[1] // head_size
    own = slots_dev * draft_len // members

    out_all = lax.all_gather(attention_out.T, "tok", axis=0, tiled=True)
    gate_all = lax.all_gather(gate_weight.T, "req", axis=0, tiled=True)
    up_all = lax.all_gather(up_weight.T, "req", axis=0, tiled=True)
    down_all = lax.all_gather(down_weight.T, "req", axis=0, tiled=True)

    slot_owner = inverse_of(current_slot)
    token_ids = jnp.take(draft_ids, slot_owner, axis=0).reshape(-1)
    vocab_start = (group_index * members + member) * vocab_dev
    wanted = token_ids - vocab_start
    inside = (wanted >= 0) & (wanted < vocab_dev)
    picked = jnp.take(embed_table, jnp.clip(wanted, 0, vocab_dev - 1), axis=0)
    picked = jnp.where(inside[:, None], picked, jnp.zeros_like(picked))
    arrived = lax.all_to_all(
        picked.reshape(groups * members, own, width), ("req", "tok"), 0, 0, tiled=True
    )
    embedded = jnp.sum(arrived.astype(F32), axis=0).astype(BF)
    normed = rms_rows(embedded, mixer_gain)
    gathered = lax.all_to_all(
        jnp.broadcast_to(normed[None], (members, own, width)), "tok", 0, 0, tiled=True
    ).reshape(members * own, width)

    queries = jnp.dot(gathered, query_weight, preferred_element_type=F32).astype(BF)
    keyvalue = jnp.dot(gathered, keyvalue_weight, preferred_element_type=F32).astype(BF)
    x = jnp.dot(gathered, mamba_input, preferred_element_type=F32)
    z = jnp.dot(gathered, mamba_gate, preferred_element_type=F32)
    both = jnp.dot(gathered, state_proj, preferred_element_type=F32)
    step = jnp.dot(gathered, mamba_step, preferred_element_type=F32)

    local_owner = lax.dynamic_slice_in_dim(slot_owner, group_index * slots_dev, slots_dev)
    ints = jnp.concatenate(
        [jnp.take(lengths, local_owner), jnp.take(accepted, local_owner), member[None]]
    )
    reals = jnp.concatenate([step_bias, jnp.exp(decay_log), skip_gain])
    payload, chosen = mixer(
        ints,
        reals,
        queries,
        keyvalue,
        key_cache,
        value_cache,
        x,
        z,
        both,
        step,
        states,
        mamba_out,
    )
    every_state = lax.all_gather(chosen, "req", axis=0, tiled=True)
    parts = lax.all_to_all(
        payload.reshape(members, own, payload.shape[1]), "tok", 0, 0, tiled=True
    )
    mixed, second = join(parts, embedded, out_all, mlp_gain[None], query_heads, head_size)
    everything = lax.all_to_all(second, "tok", 0, 0, tiled=True).reshape(members * own, width)
    gate_part = dot_nt(everything, gate_all)
    up_part = dot_nt(everything, up_all)
    hidden = (jax.nn.silu(gate_part) * up_part).astype(BF)
    mlp_part = dot_nn(hidden, down_all).astype(BF)
    mlp_rows = lax.all_to_all(mlp_part.reshape(members, own, width), "tok", 0, 0, tiled=True)
    hidden_out = (
        mixed.astype(F32) + jnp.sum(mlp_rows.astype(F32), axis=0)
    ).astype(BF)

    incoming = inverse_of(new_slot)
    local_targets = lax.dynamic_slice_in_dim(incoming, group_index * slots_dev, slots_dev)
    sources = jnp.take(current_slot, local_targets)
    new_states = pick_states(sources, every_state, slots_dev)
    return (hidden_out, new_states)


def solution(mesh):
    return jax.shard_map(
        local,
        mesh=mesh,
        in_specs=(
            P(),
            P(),
            P(),
            P(),
            P(),
            P(("req", "tok"), None),
            P(),
            P(),
            P(),
            P("req", "tok", None),
            P("req", "tok", None),
            P(None, "tok"),
            P(None, "tok"),
            P(None, "tok"),
            P(),
            P(None, "tok"),
            P("tok"),
            P("tok"),
            P("tok"),
            P("req", "tok", None, None),
            P("tok", None),
            P(),
            P(None, ("req", "tok")),
            P(None, ("req", "tok")),
            P(None, ("req", "tok")),
        ),
        out_specs=(P(("req", "tok"), None), P("req", "tok", None, None)),
        check_vma=False,
    )
```

```python
import functools

import jax
import jax.numpy as jnp
from jax import lax
from jax.experimental import pallas as pl
from jax.experimental.pallas import tpu as pltpu
from jax.sharding import PartitionSpec as P

BF = jnp.bfloat16
F32 = jnp.float32
NEG = -1e30
AUX = 128
ROOM = 12


def inverse_of(mapping):
    places = jnp.arange(mapping.shape[0], dtype=jnp.int32)
    matches = mapping[None, :] == places[:, None]
    return jnp.sum(jnp.where(matches, places[None, :], 0), axis=1)


def dot_nn(a, b, precision=None):
    return lax.dot_general(
        a, b, (((1,), (0,)), ((), ())), precision=precision, preferred_element_type=F32
    )


def dot_nt(a, b, precision=None):
    return lax.dot_general(
        a, b, (((1,), (1,)), ((), ())), precision=precision, preferred_element_type=F32
    )


def dot_tn(a, b, precision=None):
    return lax.dot_general(
        a, b, (((0,), (0,)), ((), ())), precision=precision, preferred_element_type=F32
    )


HI = lax.Precision.HIGHEST


def cost(flops, moved, special=0):
    return pl.CostEstimate(flops=flops, bytes_accessed=moved, transcendentals=special)


def whole(count):
    return [pl.BlockSpec(memory_space=pltpu.VMEM)] * count


def scalars(count):
    return [pl.BlockSpec(memory_space=pltpu.SMEM)] * count


PARAMS = pltpu.CompilerParams(vmem_limit_bytes=48 << 20)


def fetch_kernel(ints, slots_row, draft_ids, table, payload, places, most, *, members):
    groups, room, width = payload.shape
    requests, drafts = draft_ids.shape
    vocab = table.shape[0]
    count = requests * drafts // groups
    slots = requests // groups
    group, member, base = ints[0], ints[1], ints[2]
    me = group * members + member
    sub = lax.broadcasted_iota(jnp.int32, (count, count), 0)
    lane = lax.broadcasted_iota(jnp.int32, (count, count), 1)
    ids = draft_ids[...]
    ids_hi = (ids // 256).astype(F32).astype(BF)
    ids_lo = (ids % 256).astype(F32).astype(BF)
    row_slot = lax.broadcasted_iota(jnp.int32, (count, requests), 0) // drafts
    token = lax.broadcasted_iota(jnp.int32, (count, drafts), 0) % drafts
    token_lane = lax.broadcasted_iota(jnp.int32, (count, drafts), 1)
    slot_iota = lax.broadcasted_iota(jnp.int32, (room, count), 0) + base
    local_iota = lax.broadcasted_iota(jnp.int32, (room, vocab), 1)
    hots = []
    own_place = jnp.zeros((count, 1), jnp.int32)
    peak = jnp.zeros((1, count), jnp.int32)
    for g in range(groups):
        pick = jnp.where(slots_row[...] == row_slot + g * slots, 1.0, 0.0).astype(BF)
        mixed_ids = dot_nn(pick, ids_hi) * 256.0 + dot_nn(pick, ids_lo)
        id_c = jnp.sum(
            jnp.where(token == token_lane, mixed_ids, 0.0), axis=1, keepdims=True
        ).astype(jnp.int32)
        id_r = jnp.sum(jnp.where(sub == lane, id_c, 0), axis=0, keepdims=True)
        same = id_c == id_r
        first_c = jnp.min(jnp.where(same, lane, count), axis=1, keepdims=True)
        first_r = jnp.min(jnp.where(same, sub, count), axis=0, keepdims=True)
        sub_c = sub[:, :1]
        lane_r = lane[:1, :]
        owner_c = id_c // vocab
        owner_r = id_r // vocab
        column_c = owner_c % members
        column_r = owner_r % members
        alike = column_c == column_r
        before_r = jnp.where(alike & (first_c == sub_c) & (sub < first_r), 1, 0)
        rank_r = jnp.sum(before_r, axis=0, keepdims=True)
        peak = jnp.maximum(peak, rank_r + 1)
        before_c = jnp.where(alike & (first_r == lane_r) & (lane < first_c), 1, 0)
        rank_c = jnp.sum(before_c, axis=1, keepdims=True)
        inside = (rank_c >= base) & (rank_c < base + room)
        place = jnp.where(inside, column_c * room + rank_c - base, -1)
        own_place = jnp.where(group == g, place, own_place)
        mine = (first_r == lane_r) & (owner_r == me)
        asked = jnp.where(mine & (rank_r == slot_iota), id_r % vocab + 1, 0)
        row = jnp.sum(asked, axis=1, keepdims=True) - 1
        hots.append(jnp.where(local_iota == row, 1.0, 0.0))
    hot = jnp.concatenate(hots, axis=0).astype(BF)
    rows = dot_nn(hot, table[...])
    for g in range(groups):
        payload[g] = rows[g * room : (g + 1) * room].astype(BF)
    places[...] = jnp.broadcast_to(own_place, places.shape)
    most[...] = jnp.broadcast_to(jnp.max(peak, axis=1, keepdims=True), most.shape)


def fetch(ints, slots_row, draft_ids, table, groups, members, room):
    count = draft_ids.size // groups
    width = table.shape[1]
    return pl.pallas_call(
        functools.partial(fetch_kernel, members=members),
        in_specs=scalars(1) + whole(3),
        out_specs=whole(3),
        out_shape=[
            jax.ShapeDtypeStruct((groups, room, width), BF),
            jax.ShapeDtypeStruct((count, AUX), jnp.int32),
            jax.ShapeDtypeStruct((8, AUX), jnp.int32),
        ],
        compiler_params=PARAMS,
        cost_estimate=cost(2 * groups * room * table.size, 2 * table.size),
        name="fetch",
    )(ints, slots_row, draft_ids, table)


def rows_of(arrived, places):
    peers, room, width = arrived.shape
    count = places.shape[0]
    slot = lax.broadcasted_iota(jnp.int32, (count, peers * room), 1)
    hot = jnp.where(slot == places[:, :1], 1.0, 0.0).astype(BF)
    slots = jnp.concatenate([arrived[j] for j in range(peers)], axis=0)
    return dot_nn(hot, slots)


def place_kernel(arrived, places, before, out):
    out[...] = (before[...].astype(F32) + rows_of(arrived, places)).astype(BF)


def place(arrived, places, before):
    return pl.pallas_call(
        place_kernel,
        in_specs=whole(3),
        out_specs=whole(1)[0],
        out_shape=jax.ShapeDtypeStruct(before.shape, BF),
        compiler_params=PARAMS,
        name="place",
    )(arrived, places, before)


def attend_kernel(
    ints,
    arrived,
    places,
    extra,
    gain,
    query_weight,
    keyvalue_weight,
    keys,
    values,
    payload,
    embedded,
    normed,
):
    slots, cache, size = keys.shape
    tokens = extra.shape[0]
    drafts = tokens // slots
    heads = query_weight.shape[1] // size
    own = payload.shape[1]
    rows_in = (rows_of(arrived, places) + extra[...].astype(F32)).astype(BF)
    embedded[...] = rows_in
    wide = rows_in.astype(F32)
    factor = lax.rsqrt(jnp.mean(wide * wide, axis=-1, keepdims=True) + 1e-05)
    normed[...] = (wide * factor * gain[...]).astype(BF)
    queries = dot_nn(normed[...], query_weight[...]).astype(BF)
    keyvalue = dot_nn(normed[...], keyvalue_weight[...]).astype(BF)
    member = ints[8]
    scale = size ** (-0.5)
    rows = heads * drafts
    position = lax.broadcasted_iota(jnp.int32, (rows, cache), 1) + member * cache
    token = lax.broadcasted_iota(jnp.int32, (rows, drafts), 0) % drafts
    other = lax.broadcasted_iota(jnp.int32, (rows, drafts), 1)
    seen = other <= jnp.where(member == 0, token, -1)
    lane = lax.broadcasted_iota(jnp.int32, (drafts, AUX), 1)
    for slot in range(slots):
        span = slice(slot * drafts, (slot + 1) * drafts)
        length = ints[slot]
        query = jnp.concatenate(
            [queries[span, h * size : (h + 1) * size] for h in range(heads)], axis=0
        )
        scores = dot_nt(query, keys[slot]) * scale
        scores = jnp.where(position < length, scores, NEG)
        draft_scores = dot_nt(query, keyvalue[span, :size]) * scale
        draft_scores = jnp.where(seen, draft_scores, NEG)
        top = jnp.maximum(
            jnp.max(scores, axis=-1, keepdims=True),
            jnp.max(draft_scores, axis=-1, keepdims=True),
        )
        probs = jnp.where(position < length, jnp.exp(scores - top), 0.0)
        draft_probs = jnp.where(seen, jnp.exp(draft_scores - top), 0.0)
        total = jnp.sum(probs, axis=-1, keepdims=True) + jnp.sum(
            draft_probs, axis=-1, keepdims=True
        )
        summed = dot_nn(probs.astype(BF), values[slot]) + dot_nn(
            draft_probs.astype(BF), keyvalue[span, size:]
        )
        top_a = top.astype(BF).astype(F32)
        top_b = (top - top_a).astype(BF).astype(F32)
        top_c = top - top_a - top_b
        total_a = total.astype(BF).astype(F32)
        total_b = total - total_a
        aux = jnp.zeros((drafts, AUX), F32)
        for k, piece in enumerate((top_a, top_b, top_c, total_a, total_b)):
            for h in range(heads):
                part = piece[h * drafts : (h + 1) * drafts]
                aux = jnp.where(lane == k * heads + h, part, aux)
        flat = jnp.concatenate(
            [summed[h * drafts : (h + 1) * drafts] for h in range(heads)] + [aux], axis=1
        ).astype(BF)
        for q in range(drafts // own):
            payload[slot * (drafts // own) + q] = flat[q * own : (q + 1) * own]


def attend(ints, arrived, places, extra, gain, query_weight, keyvalue_weight, keys, values):
    tokens, width = extra.shape
    members = arrived.shape[0]
    wide = query_weight.shape[1] + AUX
    return pl.pallas_call(
        attend_kernel,
        in_specs=scalars(1) + whole(8),
        out_specs=whole(3),
        out_shape=[
            jax.ShapeDtypeStruct((members, tokens // members, wide), BF),
            jax.ShapeDtypeStruct((tokens, width), BF),
            jax.ShapeDtypeStruct((tokens, width), BF),
        ],
        compiler_params=PARAMS,
        cost_estimate=cost(
            2 * tokens * query_weight.size * 2, 2 * (query_weight.size + keys.size * 2), keys.size
        ),
        name="attend",
    )(ints, arrived, places, extra, gain, query_weight, keyvalue_weight, keys, values)


def mamba_kernel(
    ints,
    reals,
    normed,
    input_weight,
    gate_weight,
    state_proj,
    step_row,
    states,
    mamba_out,
    blocks,
    chosen,
):
    slots = states.shape[0]
    tokens = normed.shape[0]
    drafts = tokens // slots
    rows = normed[...]
    x_all = dot_nn(rows, input_weight[...])
    z_all = dot_nn(rows, gate_weight[...])
    both = dot_nn(rows, state_proj[...])
    step_in = (
        jnp.sum(rows.astype(F32) * step_row[...].astype(F32), axis=1, keepdims=True) + reals[0]
    )
    sizes = jnp.maximum(step_in, 0.0) + jnp.log1p(jnp.exp(-jnp.abs(step_in)))
    state_size = both.shape[1] // 2
    row = lax.broadcasted_iota(jnp.int32, (drafts, drafts), 0)
    col = lax.broadcasted_iota(jnp.int32, (drafts, drafts), 1)
    rows_in = lax.broadcasted_iota(jnp.int32, (drafts, 1), 0)
    gated = []
    for slot in range(slots):
        span = slice(slot * drafts, (slot + 1) * drafts)
        accept = ints[4 + slot]
        size_t = sizes[span]
        size_row = jnp.sum(jnp.where(row == col, size_t, 0.0), axis=0, keepdims=True)
        log_decay = -reals[1] * jnp.sum(
            jnp.where(col <= row, size_row, 0.0), axis=1, keepdims=True
        )
        log_row = jnp.sum(jnp.where(row == col, log_decay, 0.0), axis=0, keepdims=True)
        between = jnp.exp(jnp.where(col <= row, log_decay - log_row, NEG))
        state_in = both[span, :state_size]
        state_read = both[span, state_size:]
        x = x_all[span]
        z = z_all[span]
        inputs = size_t * x
        start = states[slot, 0]
        weights = dot_nt(state_read, state_in, HI) * between
        readout = dot_nn(weights, inputs, HI) + jnp.exp(log_decay) * dot_nt(
            state_read, start, HI
        )
        readout = readout + reals[2] * x
        last = jnp.sum(jnp.where(rows_in == accept - 1, log_decay, 0.0), axis=0, keepdims=True)
        remain = jnp.exp(jnp.where(rows_in < accept, last - log_decay, NEG))
        chosen[slot, 0] = (
            jnp.exp(last) * start + dot_tn(remain * inputs, state_in, HI)
        ).astype(BF)
        gated.append((readout * (z / (1.0 + jnp.exp(-z)))).astype(BF))
    part = dot_nn(jnp.concatenate(gated, axis=0), mamba_out[...])
    share = blocks.shape[2]
    for j in range(blocks.shape[0]):
        blocks[j] = part[:, j * share : (j + 1) * share].astype(BF)


def mamba(ints, reals, normed, input_weight, gate_weight, state_proj, step_row, states, mamba_out, members):
    tokens = normed.shape[0]
    share = mamba_out.shape[1] // members
    return pl.pallas_call(
        mamba_kernel,
        in_specs=scalars(2) + whole(7),
        out_specs=whole(2),
        out_shape=[
            jax.ShapeDtypeStruct((members, tokens, share), BF),
            jax.ShapeDtypeStruct(states.shape, BF),
        ],
        compiler_params=PARAMS,
        cost_estimate=cost(2 * tokens * state_proj.size * 2, 4 * state_proj.size),
        name="mamba",
    )(ints, reals, normed, input_weight, gate_weight, state_proj, step_row, states, mamba_out)


def join_kernel(parts, blocks, payload, *, heads, size):
    peers, tokens, share = blocks.shape
    own = parts.shape[1]
    aux = parts[:, :, heads * size : heads * size + AUX].astype(F32)
    payload[:, :tokens, :] = blocks[...]
    for h in range(heads):
        get = lambda k: aux[:, :, k * heads + h : k * heads + h + 1]
        top = get(0) + get(1) + get(2)
        total = get(3) + get(4)
        factor = jnp.exp(top - jnp.max(top, axis=0, keepdims=True))
        norm = jnp.sum(factor * total, axis=0)
        value = parts[:, :, h * size : (h + 1) * size].astype(F32)
        summed = jnp.sum(factor * value, axis=0)
        piece = (summed / norm).astype(BF)
        for j in range(peers):
            payload[j, tokens + h * own : tokens + (h + 1) * own, :size] = piece


def join(parts, blocks, heads, size):
    members, tokens, share = blocks.shape
    own = parts.shape[1]
    return pl.pallas_call(
        functools.partial(join_kernel, heads=heads, size=size),
        in_specs=whole(2),
        out_specs=whole(1)[0],
        out_shape=jax.ShapeDtypeStruct((members, tokens + heads * own, share), BF),
        compiler_params=PARAMS,
        name="join",
    )(parts, blocks)


def project_kernel(parts, out_weight, spread, *, heads, size):
    peers, tokens, share = spread.shape
    own = (parts.shape[1] - tokens) // heads
    acc = jnp.sum(parts[:, :tokens, :].astype(F32), axis=0)
    for h in range(heads):
        attended = jnp.concatenate(
            [parts[j, tokens + h * own : tokens + (h + 1) * own, :size] for j in range(peers)],
            axis=0,
        )
        acc = acc + dot_nt(attended, out_weight[:, h * size : (h + 1) * size])
    out = acc.astype(BF)
    for j in range(peers):
        spread[j] = out


def project(parts, out_weight, tokens, heads, size):
    members, _, share = parts.shape
    return pl.pallas_call(
        functools.partial(project_kernel, heads=heads, size=size),
        in_specs=whole(2),
        out_specs=whole(1)[0],
        out_shape=jax.ShapeDtypeStruct((members, tokens, share), BF),
        compiler_params=PARAMS,
        name="project",
    )(parts, out_weight)


def feed_kernel(spread, embedded, gain, weights, out, mixed, second, acc):
    step = pl.program_id(0)
    peers, own, width = out.shape
    units = weights.shape[1] // 3

    @pl.when(step == 0)
    def _():
        added = jnp.concatenate([spread[j] for j in range(peers)], axis=1)
        rows = (embedded[...].astype(F32) + added.astype(F32)).astype(BF)
        mixed[...] = rows
        wide = rows.astype(F32)
        factor = lax.rsqrt(jnp.mean(wide * wide, axis=-1, keepdims=True) + 1e-05)
        second[...] = (wide * factor * gain[...]).astype(BF)
        acc[...] = jnp.zeros_like(acc)

    rows = second[...]
    gate = dot_nt(rows, weights[0, :units, :])
    up = dot_nt(rows, weights[0, units : 2 * units, :])
    hidden = (gate / (1.0 + jnp.exp(-gate)) * up).astype(BF)
    acc[...] += dot_nn(hidden, weights[0, 2 * units :, :])

    @pl.when(step == pl.num_programs(0) - 1)
    def _():
        for j in range(peers):
            out[j] = acc[j * own : (j + 1) * own, :].astype(BF)


def feed(spread, embedded, gain, weights):
    members, tokens, share = spread.shape
    width = embedded.shape[1]
    groups, packed, _ = weights.shape
    fixed = lambda a: pl.BlockSpec(a.shape, lambda g: (0,) * a.ndim)
    return pl.pallas_call(
        feed_kernel,
        grid=(groups,),
        in_specs=[
            fixed(spread),
            fixed(embedded),
            fixed(gain),
            pl.BlockSpec((1, packed, width), lambda g: (g, 0, 0)),
        ],
        out_specs=[
            pl.BlockSpec((members, tokens // members, width), lambda g: (0, 0, 0)),
            pl.BlockSpec((tokens, width), lambda g: (0, 0)),
        ],
        out_shape=[
            jax.ShapeDtypeStruct((members, tokens // members, width), BF),
            jax.ShapeDtypeStruct((tokens, width), BF),
        ],
        scratch_shapes=[pltpu.VMEM((tokens, width), BF), pltpu.VMEM((tokens, width), F32)],
        compiler_params=PARAMS,
        cost_estimate=cost(2 * tokens * weights.size, 2 * weights.size),
        name="feed",
    )(spread, embedded, gain, weights)


def pick_kernel(sources, states, out):
    out[...] = states[...].astype(F32)


def pick_states(sources, states, count):
    block = (1,) + states.shape[1:]
    zeros = (0,) * (len(block) - 1)
    return pl.pallas_call(
        pick_kernel,
        grid_spec=pltpu.PrefetchScalarGridSpec(
            num_scalar_prefetch=1,
            grid=(count,),
            in_specs=[pl.BlockSpec(block, lambda i, src: (src[i],) + zeros)],
            out_specs=pl.BlockSpec(block, lambda i, src: (i,) + zeros),
        ),
        out_shape=jax.ShapeDtypeStruct((count,) + states.shape[1:], F32),
        name="pick",
    )(sources, states)


def local(
    draft_ids,
    lengths,
    current_slot,
    new_slot,
    accepted,
    embed_table,
    mixer_gain,
    query_weight,
    keyvalue_weight,
    key_cache,
    value_cache,
    attention_out,
    mamba_input,
    mamba_gate,
    state_proj,
    mamba_step,
    step_bias,
    decay_log,
    skip_gain,
    states,
    mamba_out,
    mlp_gain,
    gate_weight,
    up_weight,
    down_weight,
):
    members = lax.axis_size("tok")
    groups = lax.axis_size("req")
    group_index = lax.axis_index("req")
    member = lax.axis_index("tok")
    slots_dev, cache_dev, head_size = key_cache.shape
    draft_len = draft_ids.shape[1]
    width = embed_table.shape[1]
    query_heads = query_weight.shape[1] // head_size
    own = slots_dev * draft_len // members

    packed = jnp.concatenate([gate_weight.T, up_weight.T, down_weight.T], axis=0)
    weights = lax.all_gather(packed, "req", axis=0, tiled=False)

    def exchange(base):
        where = jnp.stack([group_index, member, base]).astype(jnp.int32)
        payload, places, most = fetch(
            where, current_slot[None], draft_ids, embed_table, groups, members, ROOM
        )
        slots = lax.all_to_all(payload, "req", 0, 0, tiled=True)
        held = jnp.sum(slots.astype(F32), axis=0).astype(BF)
        spread = jnp.broadcast_to(held[None], (members,) + held.shape)
        return lax.all_to_all(spread, "tok", 0, 0, tiled=True), places, most[0, 0]

    arrived, places, most = exchange(jnp.int32(0))

    def more(carry):
        return carry[0] < most

    def round_of(carry):
        base, rows = carry
        later, spots, _ = exchange(base)
        return base + ROOM, place(later, spots, rows)

    _, extra = lax.while_loop(
        more, round_of, (jnp.int32(ROOM), jnp.zeros((members * own, width), BF))
    )

    slot_owner = inverse_of(current_slot)
    local_owner = lax.dynamic_slice_in_dim(slot_owner, group_index * slots_dev, slots_dev)
    ints = jnp.concatenate(
        [jnp.take(lengths, local_owner), jnp.take(accepted, local_owner), member[None]]
    )
    reals = jnp.concatenate([step_bias, jnp.exp(decay_log), skip_gain])
    payload, embedded, normed = attend(
        ints,
        arrived,
        places,
        extra,
        mixer_gain[None],
        query_weight,
        keyvalue_weight,
        key_cache,
        value_cache,
    )
    parts = lax.all_to_all(payload, "tok", 0, 0, tiled=True)
    blocks, chosen = mamba(
        ints,
        reals,
        normed,
        mamba_input,
        mamba_gate,
        state_proj,
        mamba_step.T,
        states,
        mamba_out,
        members,
    )
    every_state = lax.all_gather(chosen, "req", axis=0, tiled=True)
    joined = lax.all_to_all(join(parts, blocks, query_heads, head_size), "tok", 0, 0, tiled=True)
    spread = project(joined, attention_out.T, members * own, query_heads, head_size)
    added = lax.all_to_all(spread, "tok", 0, 0, tiled=True)
    mlp_part, mixed = feed(added, embedded, mlp_gain[None], weights)
    mlp_rows = lax.all_to_all(mlp_part, "tok", 0, 0, tiled=True)
    own_rows = lax.dynamic_slice_in_dim(mixed, member * own, own)
    hidden_out = (own_rows.astype(F32) + jnp.sum(mlp_rows.astype(F32), axis=0)).astype(BF)

    incoming = inverse_of(new_slot)
    local_targets = lax.dynamic_slice_in_dim(incoming, group_index * slots_dev, slots_dev)
    sources = jnp.take(current_slot, local_targets)
    new_states = pick_states(sources, every_state, slots_dev)
    return (hidden_out, new_states)


def solution(mesh):
    return jax.shard_map(
        local,
        mesh=mesh,
        in_specs=(
            P(),
            P(),
            P(),
            P(),
            P(),
            P(("req", "tok"), None),
            P(),
            P(),
            P(),
            P("req", "tok", None),
            P("req", "tok", None),
            P(None, "tok"),
            P(None, "tok"),
            P(None, "tok"),
            P(),
            P(None, "tok"),
            P("tok"),
            P("tok"),
            P("tok"),
            P("req", "tok", None, None),
            P("tok", None),
            P(),
            P(None, ("req", "tok")),
            P(None, ("req", "tok")),
            P(None, ("req", "tok")),
        ),
        out_specs=(P(("req", "tok"), None), P("req", "tok", None, None)),
        check_vma=False,
    )
```

```python
import functools

import jax
import jax.numpy as jnp
from jax import lax
from jax.experimental import pallas as pl
from jax.experimental.pallas import tpu as pltpu
from jax.sharding import PartitionSpec as P

BF = jnp.bfloat16
F32 = jnp.float32
NEG = -1e30
AUX = 128
ROOM = 16


def inverse_of(mapping):
    places = jnp.arange(mapping.shape[0], dtype=jnp.int32)
    matches = mapping[None, :] == places[:, None]
    return jnp.sum(jnp.where(matches, places[None, :], 0), axis=1)


def dot_nn(a, b, precision=None):
    return lax.dot_general(
        a, b, (((1,), (0,)), ((), ())), precision=precision, preferred_element_type=F32
    )


def dot_nt(a, b, precision=None):
    return lax.dot_general(
        a, b, (((1,), (1,)), ((), ())), precision=precision, preferred_element_type=F32
    )


def dot_tn(a, b, precision=None):
    return lax.dot_general(
        a, b, (((0,), (0,)), ((), ())), precision=precision, preferred_element_type=F32
    )


HI = lax.Precision.HIGHEST


def cost(flops, moved, special=0):
    return pl.CostEstimate(flops=flops, bytes_accessed=moved, transcendentals=special)


def whole(count):
    return [pl.BlockSpec(memory_space=pltpu.VMEM)] * count


def streamed(count):
    return [pl.BlockSpec(memory_space=pltpu.HBM)] * count


def scalars(count):
    return [pl.BlockSpec(memory_space=pltpu.SMEM)] * count


PARAMS = pltpu.CompilerParams(vmem_limit_bytes=16 << 20)


def fetch_kernel(ints, slots_row, draft_ids, table, payload, places, most, *, members):
    groups, room, width = payload.shape
    requests, drafts = draft_ids.shape
    vocab = table.shape[0]
    count = requests * drafts // groups
    slots = requests // groups
    group, member, base = ints[0], ints[1], ints[2]
    me = group * members + member
    sub = lax.broadcasted_iota(jnp.int32, (count, count), 0)
    lane = lax.broadcasted_iota(jnp.int32, (count, count), 1)
    ids = draft_ids[...]
    ids_hi = (ids // 256).astype(F32).astype(BF)
    ids_lo = (ids % 256).astype(F32).astype(BF)
    row_slot = lax.broadcasted_iota(jnp.int32, (count, requests), 0) // drafts
    token = lax.broadcasted_iota(jnp.int32, (count, drafts), 0) % drafts
    token_lane = lax.broadcasted_iota(jnp.int32, (count, drafts), 1)
    slot_iota = lax.broadcasted_iota(jnp.int32, (room, count), 0) + base
    local_iota = lax.broadcasted_iota(jnp.int32, (room, vocab), 1)
    hots = []
    own_place = jnp.zeros((count, 1), jnp.int32)
    peak = jnp.zeros((1, count), jnp.int32)
    for g in range(groups):
        pick = jnp.where(slots_row[...] == row_slot + g * slots, 1.0, 0.0).astype(BF)
        mixed_ids = dot_nn(pick, ids_hi) * 256.0 + dot_nn(pick, ids_lo)
        id_c = jnp.sum(
            jnp.where(token == token_lane, mixed_ids, 0.0), axis=1, keepdims=True
        ).astype(jnp.int32)
        id_r = jnp.sum(jnp.where(sub == lane, id_c, 0), axis=0, keepdims=True)
        same = id_c == id_r
        first_c = jnp.min(jnp.where(same, lane, count), axis=1, keepdims=True)
        first_r = jnp.min(jnp.where(same, sub, count), axis=0, keepdims=True)
        sub_c = sub[:, :1]
        lane_r = lane[:1, :]
        owner_c = id_c // vocab
        owner_r = id_r // vocab
        column_c = owner_c % members
        column_r = owner_r % members
        alike = column_c == column_r
        before_r = jnp.where(alike & (first_c == sub_c) & (sub < first_r), 1, 0)
        rank_r = jnp.sum(before_r, axis=0, keepdims=True)
        peak = jnp.maximum(peak, rank_r + 1)
        before_c = jnp.where(alike & (first_r == lane_r) & (lane < first_c), 1, 0)
        rank_c = jnp.sum(before_c, axis=1, keepdims=True)
        inside = (rank_c >= base) & (rank_c < base + room)
        place = jnp.where(inside, column_c * room + rank_c - base, -1)
        own_place = jnp.where(group == g, place, own_place)
        mine = (first_r == lane_r) & (owner_r == me)
        asked = jnp.where(mine & (rank_r == slot_iota), id_r % vocab + 1, 0)
        row = jnp.sum(asked, axis=1, keepdims=True) - 1
        hots.append(jnp.where(local_iota == row, 1.0, 0.0))
    hot = jnp.concatenate(hots, axis=0).astype(BF)
    rows = dot_nn(hot, table[...])
    for g in range(groups):
        payload[g] = rows[g * room : (g + 1) * room].astype(BF)
    places[...] = jnp.broadcast_to(own_place, places.shape)
    most[...] = jnp.broadcast_to(jnp.max(peak, axis=1, keepdims=True), most.shape)


def fetch(ints, slots_row, draft_ids, table, groups, members, room):
    count = draft_ids.size // groups
    width = table.shape[1]
    return pl.pallas_call(
        functools.partial(fetch_kernel, members=members),
        in_specs=scalars(1) + whole(3),
        out_specs=whole(3),
        out_shape=[
            jax.ShapeDtypeStruct((groups, room, width), BF),
            jax.ShapeDtypeStruct((count, AUX), jnp.int32),
            jax.ShapeDtypeStruct((8, AUX), jnp.int32),
        ],
        compiler_params=PARAMS,
        cost_estimate=cost(2 * groups * room * table.size, 2 * table.size),
        name="fetch",
    )(ints, slots_row, draft_ids, table)


def rows_of(arrived, places):
    peers, room, width = arrived.shape
    count = places.shape[0]
    slot = lax.broadcasted_iota(jnp.int32, (count, peers * room), 1)
    hot = jnp.where(slot == places[:, :1], 1.0, 0.0).astype(BF)
    slots = jnp.concatenate([arrived[j] for j in range(peers)], axis=0)
    return dot_nn(hot, slots)


def place_kernel(arrived, places, before, out):
    out[...] = (before[...].astype(F32) + rows_of(arrived, places)).astype(BF)


def place(arrived, places, before):
    return pl.pallas_call(
        place_kernel,
        in_specs=whole(3),
        out_specs=whole(1)[0],
        out_shape=jax.ShapeDtypeStruct(before.shape, BF),
        compiler_params=PARAMS,
        name="place",
    )(arrived, places, before)


def attend_kernel(
    ints,
    arrived,
    places,
    extra,
    gain,
    query_weight,
    keyvalue_weight,
    keys,
    values,
    payload,
    embedded,
    normed,
    query_in,
    keyvalue_in,
    keys_in,
    values_in,
    sems,
):
    moves = []
    third = query_weight.shape[0] // 3
    for k in range(3):
        span = pl.ds(k * third, third)
        moves.append((query_weight.at[span, :], query_in.at[span, :]))
    moves += [(keyvalue_weight, keyvalue_in), (keys, keys_in), (values, values_in)]
    copies = [pltpu.make_async_copy(a, b, sems.at[n]) for n, (a, b) in enumerate(moves)]
    for copy in copies:
        copy.start()
    slots, cache, size = keys.shape
    tokens = extra.shape[0]
    drafts = tokens // slots
    heads = query_weight.shape[1] // size
    own = payload.shape[1]
    rows_in = (rows_of(arrived, places) + extra[...].astype(F32)).astype(BF)
    embedded[...] = rows_in
    wide = rows_in.astype(F32)
    factor = lax.rsqrt(jnp.mean(wide * wide, axis=-1, keepdims=True) + 1e-05)
    rows_norm = (wide * factor * gain[...]).astype(BF)
    normed[...] = rows_norm
    queries = None
    for k in range(3):
        copies[k].wait()
        span = slice(k * third, (k + 1) * third)
        part = dot_nn(rows_norm[:, span], query_in[span, :])
        queries = part if queries is None else queries + part
    queries = queries.astype(BF)
    copies[3].wait()
    keyvalue = dot_nn(rows_norm, keyvalue_in[...]).astype(BF)
    copies[4].wait()
    copies[5].wait()
    member = ints[8]
    scale = size ** (-0.5)
    rows = heads * drafts
    position = lax.broadcasted_iota(jnp.int32, (rows, cache), 1) + member * cache
    token = lax.broadcasted_iota(jnp.int32, (rows, drafts), 0) % drafts
    other = lax.broadcasted_iota(jnp.int32, (rows, drafts), 1)
    seen = other <= jnp.where(member == 0, token, -1)
    lane = lax.broadcasted_iota(jnp.int32, (drafts, AUX), 1)
    for slot in range(slots):
        span = slice(slot * drafts, (slot + 1) * drafts)
        length = ints[slot]
        query = jnp.concatenate(
            [queries[span, h * size : (h + 1) * size] for h in range(heads)], axis=0
        )
        scores = dot_nt(query, keys_in[slot]) * scale
        scores = jnp.where(position < length, scores, NEG)
        draft_scores = dot_nt(query, keyvalue[span, :size]) * scale
        draft_scores = jnp.where(seen, draft_scores, NEG)
        top = jnp.maximum(
            jnp.max(scores, axis=-1, keepdims=True),
            jnp.max(draft_scores, axis=-1, keepdims=True),
        )
        probs = jnp.where(position < length, jnp.exp(scores - top), 0.0)
        draft_probs = jnp.where(seen, jnp.exp(draft_scores - top), 0.0)
        total = jnp.sum(probs, axis=-1, keepdims=True) + jnp.sum(
            draft_probs, axis=-1, keepdims=True
        )
        summed = dot_nn(probs.astype(BF), values_in[slot]) + dot_nn(
            draft_probs.astype(BF), keyvalue[span, size:]
        )
        top_a = top.astype(BF).astype(F32)
        top_b = (top - top_a).astype(BF).astype(F32)
        top_c = top - top_a - top_b
        total_a = total.astype(BF).astype(F32)
        total_b = total - total_a
        aux = jnp.zeros((drafts, AUX), F32)
        for k, piece in enumerate((top_a, top_b, top_c, total_a, total_b)):
            for h in range(heads):
                part = piece[h * drafts : (h + 1) * drafts]
                aux = jnp.where(lane == k * heads + h, part, aux)
        flat = jnp.concatenate(
            [summed[h * drafts : (h + 1) * drafts] for h in range(heads)] + [aux], axis=1
        ).astype(BF)
        for q in range(drafts // own):
            payload[slot * (drafts // own) + q] = flat[q * own : (q + 1) * own]


def attend(ints, arrived, places, extra, gain, query_weight, keyvalue_weight, keys, values):
    tokens, width = extra.shape
    members = arrived.shape[0]
    wide = query_weight.shape[1] + AUX
    return pl.pallas_call(
        attend_kernel,
        in_specs=scalars(1) + whole(4) + streamed(4),
        out_specs=whole(3),
        out_shape=[
            jax.ShapeDtypeStruct((members, tokens // members, wide), BF),
            jax.ShapeDtypeStruct((tokens, width), BF),
            jax.ShapeDtypeStruct((tokens, width), BF),
        ],
        scratch_shapes=[
            pltpu.VMEM(a.shape, a.dtype) for a in (query_weight, keyvalue_weight, keys, values)
        ]
        + [pltpu.SemaphoreType.DMA((6,))],
        compiler_params=pltpu.CompilerParams(vmem_limit_bytes=28 << 20),
        cost_estimate=cost(
            2 * tokens * query_weight.size * 2, 2 * (query_weight.size + keys.size * 2), keys.size
        ),
        name="attend",
    )(ints, arrived, places, extra, gain, query_weight, keyvalue_weight, keys, values)


def fold(block):
    half = block.shape[0] // 2
    rest = jnp.concatenate([block[:half, AUX:], block[half:, AUX:]], axis=1)
    return jnp.concatenate([block[:, :AUX], rest], axis=0)


def unfold(block, tokens):
    half = AUX // 2
    rest = jnp.concatenate([block[tokens:, :half], block[tokens:, half:]], axis=0)
    return jnp.concatenate([block[:tokens], rest], axis=1)


def mamba_kernel(
    ints,
    reals,
    normed,
    input_weight,
    gate_weight,
    state_proj,
    step_row,
    states,
    mamba_out,
    blocks,
    chosen,
):
    slots = states.shape[0]
    tokens = normed.shape[0]
    drafts = tokens // slots
    rows = normed[...]
    x_all = dot_nn(rows, input_weight[...])
    z_all = dot_nn(rows, gate_weight[...])
    both = dot_nn(rows, state_proj[...])
    step_in = (
        jnp.sum(rows.astype(F32) * step_row[...].astype(F32), axis=1, keepdims=True) + reals[0]
    )
    sizes = jnp.maximum(step_in, 0.0) + jnp.log1p(jnp.exp(-jnp.abs(step_in)))
    state_size = both.shape[1] // 2
    row = lax.broadcasted_iota(jnp.int32, (drafts, drafts), 0)
    col = lax.broadcasted_iota(jnp.int32, (drafts, drafts), 1)
    rows_in = lax.broadcasted_iota(jnp.int32, (drafts, 1), 0)
    gated = []
    for slot in range(slots):
        span = slice(slot * drafts, (slot + 1) * drafts)
        accept = ints[4 + slot]
        size_t = sizes[span]
        size_row = jnp.sum(jnp.where(row == col, size_t, 0.0), axis=0, keepdims=True)
        log_decay = -reals[1] * jnp.sum(
            jnp.where(col <= row, size_row, 0.0), axis=1, keepdims=True
        )
        log_row = jnp.sum(jnp.where(row == col, log_decay, 0.0), axis=0, keepdims=True)
        between = jnp.exp(jnp.where(col <= row, log_decay - log_row, NEG))
        state_in = both[span, :state_size]
        state_read = both[span, state_size:]
        x = x_all[span]
        z = z_all[span]
        inputs = size_t * x
        start = states[slot, 0]
        weights = dot_nt(state_read, state_in, HI) * between
        readout = dot_nn(weights, inputs, HI) + jnp.exp(log_decay) * dot_nt(
            state_read, start, HI
        )
        readout = readout + reals[2] * x
        last = jnp.sum(jnp.where(rows_in == accept - 1, log_decay, 0.0), axis=0, keepdims=True)
        remain = jnp.exp(jnp.where(rows_in < accept, last - log_decay, NEG))
        chosen[slot, 0] = (
            jnp.exp(last) * start + dot_tn(remain * inputs, state_in, HI)
        ).astype(BF)
        gated.append((readout * (z / (1.0 + jnp.exp(-z)))).astype(BF))
    part = dot_nn(jnp.concatenate(gated, axis=0), mamba_out[...])
    share = part.shape[1] // blocks.shape[0]
    for j in range(blocks.shape[0]):
        blocks[j] = fold(part[:, j * share : (j + 1) * share]).astype(BF)


def mamba(ints, reals, normed, input_weight, gate_weight, state_proj, step_row, states, mamba_out, members):
    tokens = normed.shape[0]
    share = mamba_out.shape[1] // members
    return pl.pallas_call(
        mamba_kernel,
        in_specs=scalars(2) + whole(7),
        out_specs=whole(2),
        out_shape=[
            jax.ShapeDtypeStruct((members, tokens * share // AUX, AUX), BF),
            jax.ShapeDtypeStruct(states.shape, BF),
        ],
        compiler_params=PARAMS,
        cost_estimate=cost(2 * tokens * state_proj.size * 2, 4 * state_proj.size, tokens * 4096),
        name="mamba",
    )(ints, reals, normed, input_weight, gate_weight, state_proj, step_row, states, mamba_out)


def join_kernel(parts, blocks, payload, *, heads, size):
    peers, tokens, _ = blocks.shape
    own = parts.shape[1]
    aux = parts[:, :, heads * size : heads * size + AUX].astype(F32)
    payload[:, :tokens, :] = blocks[...]
    for h in range(heads):
        get = lambda k: aux[:, :, k * heads + h : k * heads + h + 1]
        top = get(0) + get(1) + get(2)
        total = get(3) + get(4)
        factor = jnp.exp(top - jnp.max(top, axis=0, keepdims=True))
        norm = jnp.sum(factor * total, axis=0)
        value = parts[:, :, h * size : (h + 1) * size].astype(F32)
        summed = jnp.sum(factor * value, axis=0)
        piece = (summed / norm).astype(BF)
        for j in range(peers):
            payload[j, tokens + h * own : tokens + (h + 1) * own, :size] = piece


def join(parts, blocks, heads, size):
    members, tokens, share = blocks.shape
    own = parts.shape[1]
    return pl.pallas_call(
        functools.partial(join_kernel, heads=heads, size=size),
        in_specs=whole(2),
        out_specs=whole(1)[0],
        out_shape=jax.ShapeDtypeStruct((members, tokens + heads * own, share), BF),
        compiler_params=PARAMS,
        name="join",
    )(parts, blocks)


def project_kernel(parts, out_weight, spread, *, heads, size):
    peers, packed, _ = spread.shape
    own = (parts.shape[1] - packed) // heads
    tokens = own * peers
    acc = unfold(jnp.sum(parts[:, :packed, :].astype(F32), axis=0), tokens)
    for h in range(heads):
        attended = jnp.concatenate(
            [parts[j, packed + h * own : packed + (h + 1) * own, :size] for j in range(peers)],
            axis=0,
        )
        acc = acc + dot_nt(attended, out_weight[:, h * size : (h + 1) * size])
    out = fold(acc).astype(BF)
    for j in range(peers):
        spread[j] = out


def project(parts, out_weight, packed, heads, size):
    members = parts.shape[0]
    return pl.pallas_call(
        functools.partial(project_kernel, heads=heads, size=size),
        in_specs=whole(2),
        out_specs=whole(1)[0],
        out_shape=jax.ShapeDtypeStruct((members, packed, AUX), BF),
        compiler_params=PARAMS,
        name="project",
    )(parts, out_weight)


def feed_kernel(spread, embedded, gain, *refs, count):
    weights = refs[:count]
    out, mixed, gates, ups, downs, sems = refs[count:]
    peers, own, width = out.shape
    tokens = embedded.shape[0]
    total = gates.shape[0]
    pieces = []
    begin = 0
    units = min(w.shape[0] for w in weights) // 3
    for w in weights:
        for first in range(0, w.shape[0], 3 * units):
            pieces.append((w, first, begin))
            begin += units
    copies = []
    for n, (w, first, at) in enumerate(pieces):
        trio = []
        for k, to in enumerate((gates, ups, downs)):
            copy = pltpu.make_async_copy(
                w.at[pl.ds(first + k * units, units), :], to.at[pl.ds(at, units), :], sems.at[n, k]
            )
            copy.start()
            trio.append(copy)
        copies.append((at + units, trio))
    added = jnp.concatenate([unfold(spread[j].astype(F32), tokens) for j in range(peers)], axis=1)
    rows = (embedded[...].astype(F32) + added).astype(BF)
    mixed[...] = rows
    wide = rows.astype(F32)
    factor = lax.rsqrt(jnp.mean(wide * wide, axis=-1, keepdims=True) + 1e-05)
    second = (wide * factor * gain[...]).astype(BF)
    chunk = 256
    waited = 0
    ready = 0
    acc = None
    for c in range(total // chunk):
        while ready < (c + 1) * chunk:
            ready, trio = copies[waited]
            for copy in trio:
                copy.wait()
            waited += 1
        span = slice(c * chunk, (c + 1) * chunk)
        gate = dot_nt(second, gates[span, :])
        up = dot_nt(second, ups[span, :])
        hidden = (gate / (1.0 + jnp.exp(-gate)) * up).astype(BF)
        part = dot_nn(hidden, downs[span, :])
        acc = part if acc is None else acc + part
    for j in range(peers):
        out[j] = acc[j * own : (j + 1) * own, :].astype(BF)


def feed(spread, embedded, gain, weights):
    members = spread.shape[0]
    tokens, width = embedded.shape
    units = sum(w.shape[0] for w in weights) // 3
    count = 3 * units // min(w.shape[0] for w in weights)
    return pl.pallas_call(
        functools.partial(feed_kernel, count=len(weights)),
        in_specs=whole(3) + streamed(len(weights)),
        out_specs=whole(2),
        out_shape=[
            jax.ShapeDtypeStruct((members, tokens // members, width), BF),
            jax.ShapeDtypeStruct((tokens, width), BF),
        ],
        scratch_shapes=[pltpu.VMEM((units, width), BF)] * 3
        + [pltpu.SemaphoreType.DMA((count, 3))],
        compiler_params=pltpu.CompilerParams(vmem_limit_bytes=36 << 20),
        cost_estimate=cost(6 * tokens * units * width, 6 * units * width),
        name="feed",
    )(spread, embedded, gain, *weights)


def pick_kernel(turns, rows, *refs):
    held = refs[:-1]
    out = refs[-1]
    for i in range(out.shape[0]):
        for n, ref in enumerate(held):

            @pl.when(turns[i] == n)
            def _():
                out[i] = ref[rows[i]].astype(F32)


def pick_states(turns, rows, held, count):
    shape = (count,) + held[0].shape[1:]
    return pl.pallas_call(
        pick_kernel,
        in_specs=scalars(2) + whole(len(held)),
        out_specs=whole(1)[0],
        out_shape=jax.ShapeDtypeStruct(shape, F32),
        compiler_params=PARAMS,
        name="pick",
    )(turns, rows, *held)


def local(
    draft_ids,
    lengths,
    current_slot,
    new_slot,
    accepted,
    embed_table,
    mixer_gain,
    query_weight,
    keyvalue_weight,
    key_cache,
    value_cache,
    attention_out,
    mamba_input,
    mamba_gate,
    state_proj,
    mamba_step,
    step_bias,
    decay_log,
    skip_gain,
    states,
    mamba_out,
    mlp_gain,
    gate_weight,
    up_weight,
    down_weight,
):
    members = lax.axis_size("tok")
    groups = lax.axis_size("req")
    group_index = lax.axis_index("req")
    member = lax.axis_index("tok")
    slots_dev, cache_dev, head_size = key_cache.shape
    draft_len = draft_ids.shape[1]
    width = embed_table.shape[1]
    query_heads = query_weight.shape[1] // head_size
    own = slots_dev * draft_len // members

    cores = 2
    chips = groups // cores

    def turn(value, by):
        return lax.ppermute(
            value, "req", [(g, (g + by * cores) % groups) for g in range(groups)]
        )

    def across(value):
        return lax.ppermute(value, "req", [(g, g ^ 1) for g in range(groups)])

    def exchange(base):
        where = jnp.stack([group_index, member, base]).astype(jnp.int32)
        payload, places, most = fetch(
            where, current_slot[None], draft_ids, embed_table, groups, members, ROOM
        )
        slots = lax.all_to_all(payload, "req", 0, 0, tiled=True)
        return payload, slots, places, most[0, 0]

    def spread_slots(slots):
        held = jnp.sum(slots.astype(F32), axis=0).astype(BF)
        spread = jnp.broadcast_to(held[None], (members,) + held.shape)
        return lax.all_to_all(spread, "tok", 0, 0, tiled=True)

    sent, slots, places, most = exchange(jnp.int32(0))

    half = gate_weight.shape[1] // 2
    *trio, _ = lax.optimization_barrier((gate_weight.T, up_weight.T, down_weight.T, sent))
    low = jnp.concatenate([w[:half] for w in trio], axis=0)
    high = jnp.concatenate([w[half:] for w in trio], axis=0)
    own_weights = jnp.concatenate([low, high], axis=0)
    own_weights, slots = lax.optimization_barrier((own_weights, slots))
    arrived = spread_slots(slots)
    from_below = turn(own_weights, 1)
    from_above = turn(own_weights, -1)
    weights = [own_weights, from_below, from_above]

    def more(carry):
        return carry[0] < most

    def round_of(carry):
        base, rows = carry
        _, later, spots, _ = exchange(base)
        return base + ROOM, place(spread_slots(later), spots, rows)

    _, extra = lax.while_loop(
        more, round_of, (jnp.int32(ROOM), jnp.zeros((members * own, width), BF))
    )

    slot_owner = inverse_of(current_slot)
    local_owner = lax.dynamic_slice_in_dim(slot_owner, group_index * slots_dev, slots_dev)
    ints = jnp.concatenate(
        [jnp.take(lengths, local_owner), jnp.take(accepted, local_owner), member[None]]
    )
    reals = jnp.concatenate([step_bias, jnp.exp(decay_log), skip_gain])
    payload, embedded, normed = attend(
        ints,
        arrived,
        places,
        extra,
        mixer_gain[None],
        query_weight,
        keyvalue_weight,
        key_cache,
        value_cache,
    )
    parts = lax.all_to_all(payload, "tok", 0, 0, tiled=True)
    blocks, chosen = mamba(
        ints,
        reals,
        normed,
        mamba_input,
        mamba_gate,
        state_proj,
        mamba_step.T,
        states,
        mamba_out,
        members,
    )
    from_below, from_above, parts, chosen = lax.optimization_barrier(
        (from_below, from_above, parts, chosen)
    )
    far = [turn(from_below[: 3 * half], 1), turn(from_above[3 * half :], -1)]
    weights += [across(w) for w in weights]
    joined = lax.all_to_all(join(parts, blocks, query_heads, head_size), "tok", 0, 0, tiled=True)
    *far, joined = lax.optimization_barrier((*far, joined))
    weights += far + [across(w) for w in far]
    spread = project(joined, attention_out.T, blocks.shape[1], query_heads, head_size)
    added = lax.all_to_all(spread, "tok", 0, 0, tiled=True)
    mlp_part, mixed = feed(added, embedded, mlp_gain[None], weights)
    mlp_rows = lax.all_to_all(mlp_part, "tok", 0, 0, tiled=True)
    own_rows = lax.dynamic_slice_in_dim(mixed, member * own, own)
    hidden_out = (own_rows.astype(F32) + jnp.sum(mlp_rows.astype(F32), axis=0)).astype(BF)

    incoming = inverse_of(new_slot)
    local_targets = lax.dynamic_slice_in_dim(incoming, group_index * slots_dev, slots_dev)
    sources = jnp.take(current_slot, local_targets)
    chosen = chosen[:, 0]
    pair = jnp.concatenate([chosen, across(chosen)], axis=0)
    held = [pair] + [turn(pair, by) for by in range(1, chips)]
    source_group = sources // slots_dev
    turns = (group_index // cores - source_group // cores) % chips
    other_core = (source_group % cores) != (group_index % cores)
    rows = sources % slots_dev + jnp.where(other_core, slots_dev, 0)
    new_states = pick_states(turns, rows, held, slots_dev)[:, None]
    return (hidden_out, new_states)


def solution(mesh):
    return jax.shard_map(
        local,
        mesh=mesh,
        in_specs=(
            P(),
            P(),
            P(),
            P(),
            P(),
            P(("req", "tok"), None),
            P(),
            P(),
            P(),
            P("req", "tok", None),
            P("req", "tok", None),
            P(None, "tok"),
            P(None, "tok"),
            P(None, "tok"),
            P(),
            P(None, "tok"),
            P("tok"),
            P("tok"),
            P("tok"),
            P("req", "tok", None, None),
            P("tok", None),
            P(),
            P(None, ("req", "tok")),
            P(None, ("req", "tok")),
            P(None, ("req", "tok")),
        ),
        out_specs=(P(("req", "tok"), None), P("req", "tok", None, None)),
        check_vma=False,
    )
```

```python
import functools

import jax
import jax.numpy as jnp
from jax import lax
from jax.experimental import pallas as pl
from jax.experimental.pallas import tpu as pltpu
from jax.sharding import PartitionSpec as P

BF = jnp.bfloat16
F32 = jnp.float32
NEG = -1e30
AUX = 128
ROOM = 16


def inverse_of(mapping):
    places = jnp.arange(mapping.shape[0], dtype=jnp.int32)
    matches = mapping[None, :] == places[:, None]
    return jnp.sum(jnp.where(matches, places[None, :], 0), axis=1)


def dot_nn(a, b, precision=None):
    return lax.dot_general(
        a, b, (((1,), (0,)), ((), ())), precision=precision, preferred_element_type=F32
    )


def dot_nt(a, b, precision=None):
    return lax.dot_general(
        a, b, (((1,), (1,)), ((), ())), precision=precision, preferred_element_type=F32
    )


def dot_tn(a, b, precision=None):
    return lax.dot_general(
        a, b, (((0,), (0,)), ((), ())), precision=precision, preferred_element_type=F32
    )


HI = lax.Precision.HIGHEST


def cost(flops, moved, special=0):
    return pl.CostEstimate(flops=flops, bytes_accessed=moved, transcendentals=special)


def whole(shapes):
    return [pl.BlockSpec(a.shape, lambda i, n=len(a.shape): (0,) * n) for a in shapes]


def streamed(count):
    return [pl.BlockSpec(memory_space=pltpu.HBM)] * count


def scalars(count):
    return [pl.BlockSpec(memory_space=pltpu.SMEM)] * count


PARAMS = pltpu.CompilerParams(vmem_limit_bytes=60 << 20)


def fetch_kernel(
    ints, slots_row, draft_ids, table_far, payload, places, most, table, sem, *, members
):
    load = pltpu.make_async_copy(table_far, table, sem)
    load.start()
    groups, room, width = payload.shape
    requests, drafts = draft_ids.shape
    vocab = table.shape[0]
    count = requests * drafts // groups
    slots = requests // groups
    group, member, base = ints[0], ints[1], ints[2]
    me = group * members + member
    sub = lax.broadcasted_iota(jnp.int32, (count, count), 0)
    lane = lax.broadcasted_iota(jnp.int32, (count, count), 1)
    ids = draft_ids[...]
    ids_hi = (ids // 256).astype(F32).astype(BF)
    ids_lo = (ids % 256).astype(F32).astype(BF)
    row_slot = lax.broadcasted_iota(jnp.int32, (count, requests), 0) // drafts
    token = lax.broadcasted_iota(jnp.int32, (count, drafts), 0) % drafts
    token_lane = lax.broadcasted_iota(jnp.int32, (count, drafts), 1)
    slot_iota = lax.broadcasted_iota(jnp.int32, (room, count), 0) + base
    local_iota = lax.broadcasted_iota(jnp.int32, (room, vocab), 1)
    hots = []
    own_place = jnp.zeros((count, 1), jnp.int32)
    peak = jnp.zeros((1, count), jnp.int32)
    for g in range(groups):
        pick = jnp.where(slots_row[...] == row_slot + g * slots, 1.0, 0.0).astype(BF)
        mixed_ids = dot_nn(pick, ids_hi) * 256.0 + dot_nn(pick, ids_lo)
        id_c = jnp.sum(
            jnp.where(token == token_lane, mixed_ids, 0.0), axis=1, keepdims=True
        ).astype(jnp.int32)
        id_r = jnp.sum(jnp.where(sub == lane, id_c, 0), axis=0, keepdims=True)
        same = id_c == id_r
        first_c = jnp.min(jnp.where(same, lane, count), axis=1, keepdims=True)
        first_r = jnp.min(jnp.where(same, sub, count), axis=0, keepdims=True)
        sub_c = sub[:, :1]
        lane_r = lane[:1, :]
        owner_c = id_c // vocab
        owner_r = id_r // vocab
        column_c = owner_c % members
        column_r = owner_r % members
        alike = column_c == column_r
        before_r = jnp.where(alike & (first_c == sub_c) & (sub < first_r), 1, 0)
        rank_r = jnp.sum(before_r, axis=0, keepdims=True)
        peak = jnp.maximum(peak, rank_r + 1)
        before_c = jnp.where(alike & (first_r == lane_r) & (lane < first_c), 1, 0)
        rank_c = jnp.sum(before_c, axis=1, keepdims=True)
        inside = (rank_c >= base) & (rank_c < base + room)
        place = jnp.where(inside, column_c * room + rank_c - base, -1)
        own_place = jnp.where(group == g, place, own_place)
        mine = (first_r == lane_r) & (owner_r == me)
        asked = jnp.where(mine & (rank_r == slot_iota), id_r % vocab + 1, 0)
        row = jnp.sum(asked, axis=1, keepdims=True) - 1
        hots.append(jnp.where(local_iota == row, 1.0, 0.0))
    hot = jnp.concatenate(hots, axis=0).astype(BF)
    load.wait()
    rows = dot_nn(hot, table[...])
    for g in range(groups):
        payload[g] = rows[g * room : (g + 1) * room].astype(BF)
    places[...] = jnp.broadcast_to(own_place, places.shape)
    most[...] = jnp.broadcast_to(jnp.max(peak, axis=1, keepdims=True), most.shape)


def fetch(ints, slots_row, draft_ids, table, groups, members, room):
    count = draft_ids.size // groups
    width = table.shape[1]
    outs = [
        jax.ShapeDtypeStruct((groups, room, width), BF),
        jax.ShapeDtypeStruct((count, AUX), jnp.int32),
        jax.ShapeDtypeStruct((8, AUX), jnp.int32),
    ]
    return pl.pallas_call(
        functools.partial(fetch_kernel, members=members),
        grid=(1,),
        in_specs=scalars(1) + whole([slots_row, draft_ids]) + streamed(1),
        out_specs=whole(outs),
        out_shape=outs,
        scratch_shapes=[pltpu.VMEM(table.shape, table.dtype), pltpu.SemaphoreType.DMA],
        compiler_params=PARAMS,
        cost_estimate=cost(2 * groups * room * table.size, 2 * table.size),
        name="fetch",
    )(ints, slots_row, draft_ids, table)


def rows_of(arrived, places):
    peers, room, width = arrived.shape
    count = places.shape[0]
    slot = lax.broadcasted_iota(jnp.int32, (count, peers * room), 1)
    hot = jnp.where(slot == places[:, :1], 1.0, 0.0).astype(BF)
    slots = jnp.concatenate([arrived[j] for j in range(peers)], axis=0)
    return dot_nn(hot, slots)


def place_kernel(arrived, places, before, out):
    out[...] = (before[...].astype(F32) + rows_of(arrived, places)).astype(BF)


def place(arrived, places, before):
    return pl.pallas_call(
        place_kernel,
        grid=(1,),
        in_specs=whole([arrived, places, before]),
        out_specs=whole([before])[0],
        out_shape=jax.ShapeDtypeStruct(before.shape, BF),
        compiler_params=PARAMS,
        name="place",
    )(arrived, places, before)


def attend_kernel(
    ints,
    arrived,
    places,
    extra,
    gain,
    query_weight,
    keyvalue_weight,
    keys,
    values,
    payload,
    embedded,
    normed,
    arrived_in,
    query_in,
    keyvalue_in,
    keys_in,
    values_in,
    sems,
):
    moves = [(arrived, arrived_in)]
    third = query_weight.shape[0] // 3
    for k in range(3):
        span = pl.ds(k * third, third)
        moves.append((query_weight.at[span, :], query_in.at[span, :]))
    moves += [(keyvalue_weight, keyvalue_in), (keys, keys_in), (values, values_in)]
    copies = [pltpu.make_async_copy(a, b, sems.at[n]) for n, (a, b) in enumerate(moves)]
    for copy in copies:
        copy.start()
    slots, cache, size = keys.shape
    tokens = extra.shape[0]
    drafts = tokens // slots
    heads = query_weight.shape[1] // size
    own = payload.shape[1]
    copies[0].wait()
    rows_in = (rows_of(arrived_in, places) + extra[...].astype(F32)).astype(BF)
    embedded[...] = rows_in
    wide = rows_in.astype(F32)
    factor = lax.rsqrt(jnp.mean(wide * wide, axis=-1, keepdims=True) + 1e-05)
    rows_norm = (wide * factor * gain[...]).astype(BF)
    normed[...] = rows_norm
    queries = None
    for k in range(3):
        copies[k + 1].wait()
        span = slice(k * third, (k + 1) * third)
        part = dot_nn(rows_norm[:, span], query_in[span, :])
        queries = part if queries is None else queries + part
    queries = queries.astype(BF)
    copies[4].wait()
    keyvalue = dot_nn(rows_norm, keyvalue_in[...]).astype(BF)
    copies[5].wait()
    copies[6].wait()
    member = ints[8]
    scale = size ** (-0.5)
    rows = heads * drafts
    position = lax.broadcasted_iota(jnp.int32, (rows, cache), 1) + member * cache
    token = lax.broadcasted_iota(jnp.int32, (rows, drafts), 0) % drafts
    other = lax.broadcasted_iota(jnp.int32, (rows, drafts), 1)
    seen = other <= jnp.where(member == 0, token, -1)
    lane = lax.broadcasted_iota(jnp.int32, (drafts, AUX), 1)
    for slot in range(slots):
        span = slice(slot * drafts, (slot + 1) * drafts)
        length = ints[slot]
        query = jnp.concatenate(
            [queries[span, h * size : (h + 1) * size] for h in range(heads)], axis=0
        )
        scores = dot_nt(query, keys_in[slot]) * scale
        scores = jnp.where(position < length, scores, NEG)
        draft_scores = dot_nt(query, keyvalue[span, :size]) * scale
        draft_scores = jnp.where(seen, draft_scores, NEG)
        top = jnp.maximum(
            jnp.max(scores, axis=-1, keepdims=True),
            jnp.max(draft_scores, axis=-1, keepdims=True),
        )
        probs = jnp.where(position < length, jnp.exp(scores - top), 0.0)
        draft_probs = jnp.where(seen, jnp.exp(draft_scores - top), 0.0)
        total = jnp.sum(probs, axis=-1, keepdims=True) + jnp.sum(
            draft_probs, axis=-1, keepdims=True
        )
        summed = dot_nn(probs.astype(BF), values_in[slot]) + dot_nn(
            draft_probs.astype(BF), keyvalue[span, size:]
        )
        top_a = top.astype(BF).astype(F32)
        top_b = (top - top_a).astype(BF).astype(F32)
        top_c = top - top_a - top_b
        total_a = total.astype(BF).astype(F32)
        total_b = total - total_a
        aux = jnp.zeros((drafts, AUX), F32)
        for k, piece in enumerate((top_a, top_b, top_c, total_a, total_b)):
            for h in range(heads):
                part = piece[h * drafts : (h + 1) * drafts]
                aux = jnp.where(lane == k * heads + h, part, aux)
        flat = jnp.concatenate(
            [summed[h * drafts : (h + 1) * drafts] for h in range(heads)] + [aux], axis=1
        ).astype(BF)
        for q in range(drafts // own):
            payload[slot * (drafts // own) + q] = flat[q * own : (q + 1) * own]


def attend(ints, arrived, places, extra, gain, query_weight, keyvalue_weight, keys, values):
    tokens, width = extra.shape
    members = arrived.shape[0]
    wide = query_weight.shape[1] + AUX
    far = (arrived, query_weight, keyvalue_weight, keys, values)
    outs = [
        jax.ShapeDtypeStruct((members, tokens // members, wide), BF),
        jax.ShapeDtypeStruct((tokens, width), BF),
        jax.ShapeDtypeStruct((tokens, width), BF),
    ]
    return pl.pallas_call(
        attend_kernel,
        grid=(1,),
        in_specs=scalars(1) + streamed(1) + whole([places, extra, gain]) + streamed(4),
        out_specs=whole(outs),
        out_shape=outs,
        scratch_shapes=[pltpu.VMEM(a.shape, a.dtype) for a in far]
        + [pltpu.SemaphoreType.DMA((7,))],
        compiler_params=PARAMS,
        cost_estimate=cost(
            2 * tokens * query_weight.size * 2, 2 * (query_weight.size + keys.size * 2), keys.size
        ),
        name="attend",
    )(ints, arrived, places, extra, gain, query_weight, keyvalue_weight, keys, values)


def fold(block):
    half = block.shape[0] // 2
    rest = jnp.concatenate([block[:half, AUX:], block[half:, AUX:]], axis=1)
    return jnp.concatenate([block[:, :AUX], rest], axis=0)


def unfold(block, tokens):
    half = AUX // 2
    rest = jnp.concatenate([block[tokens:, :half], block[tokens:, half:]], axis=0)
    return jnp.concatenate([block[:tokens], rest], axis=1)


def mamba_kernel(
    ints,
    reals,
    normed,
    input_weight,
    gate_weight,
    state_proj,
    step_row,
    states,
    mamba_out,
    blocks,
    chosen,
    proj_in,
    input_in,
    gate_in,
    states_in,
    out_in,
    sems,
):
    moves = (
        (state_proj, proj_in),
        (input_weight, input_in),
        (gate_weight, gate_in),
        (states, states_in),
        (mamba_out, out_in),
    )
    copies = [pltpu.make_async_copy(a, b, sems.at[n]) for n, (a, b) in enumerate(moves)]
    for copy in copies:
        copy.start()
    slots = states.shape[0]
    tokens = normed.shape[0]
    drafts = tokens // slots
    rows = normed[...]
    step_in = (
        jnp.sum(rows.astype(F32) * step_row[...].astype(F32), axis=1, keepdims=True) + reals[0]
    )
    sizes = jnp.maximum(step_in, 0.0) + jnp.log1p(jnp.exp(-jnp.abs(step_in)))
    copies[0].wait()
    both = dot_nn(rows, proj_in[...])
    copies[1].wait()
    x_all = dot_nn(rows, input_in[...])
    copies[2].wait()
    z_all = dot_nn(rows, gate_in[...])
    copies[3].wait()
    state_size = both.shape[1] // 2
    row = lax.broadcasted_iota(jnp.int32, (drafts, drafts), 0)
    col = lax.broadcasted_iota(jnp.int32, (drafts, drafts), 1)
    rows_in = lax.broadcasted_iota(jnp.int32, (drafts, 1), 0)
    gated = []
    for slot in range(slots):
        span = slice(slot * drafts, (slot + 1) * drafts)
        accept = ints[4 + slot]
        size_t = sizes[span]
        size_row = jnp.sum(jnp.where(row == col, size_t, 0.0), axis=0, keepdims=True)
        log_decay = -reals[1] * jnp.sum(
            jnp.where(col <= row, size_row, 0.0), axis=1, keepdims=True
        )
        log_row = jnp.sum(jnp.where(row == col, log_decay, 0.0), axis=0, keepdims=True)
        between = jnp.exp(jnp.where(col <= row, log_decay - log_row, NEG))
        state_in = both[span, :state_size]
        state_read = both[span, state_size:]
        x = x_all[span]
        z = z_all[span]
        inputs = size_t * x
        start = states_in[slot, 0]
        weights = dot_nt(state_read, state_in, HI) * between
        readout = dot_nn(weights, inputs, HI) + jnp.exp(log_decay) * dot_nt(
            state_read, start, HI
        )
        readout = readout + reals[2] * x
        last = jnp.sum(jnp.where(rows_in == accept - 1, log_decay, 0.0), axis=0, keepdims=True)
        remain = jnp.exp(jnp.where(rows_in < accept, last - log_decay, NEG))
        chosen[slot, 0] = (
            jnp.exp(last) * start + dot_tn(remain * inputs, state_in, HI)
        ).astype(BF)
        gated.append((readout * (z / (1.0 + jnp.exp(-z)))).astype(BF))
    copies[4].wait()
    part = dot_nn(jnp.concatenate(gated, axis=0), out_in[...])
    share = part.shape[1] // blocks.shape[0]
    for j in range(blocks.shape[0]):
        blocks[j] = fold(part[:, j * share : (j + 1) * share]).astype(BF)


def mamba(ints, reals, normed, input_weight, gate_weight, state_proj, step_row, states, mamba_out, members):
    tokens = normed.shape[0]
    share = mamba_out.shape[1] // members
    outs = [
        jax.ShapeDtypeStruct((members, tokens * share // AUX, AUX), BF),
        jax.ShapeDtypeStruct(states.shape, BF),
    ]
    far = (state_proj, input_weight, gate_weight, states, mamba_out)
    return pl.pallas_call(
        mamba_kernel,
        grid=(1,),
        in_specs=scalars(2)
        + whole([normed])
        + streamed(3)
        + whole([step_row])
        + streamed(2),
        out_specs=whole(outs),
        out_shape=outs,
        scratch_shapes=[pltpu.VMEM(a.shape, a.dtype) for a in far]
        + [pltpu.SemaphoreType.DMA((5,))],
        compiler_params=PARAMS,
        cost_estimate=cost(2 * tokens * state_proj.size * 2, 4 * state_proj.size, tokens * 4096),
        name="mamba",
    )(ints, reals, normed, input_weight, gate_weight, state_proj, step_row, states, mamba_out)


def join_kernel(parts, blocks, payload, *, heads, size):
    peers, tokens, _ = blocks.shape
    own = parts.shape[1]
    aux = parts[:, :, heads * size : heads * size + AUX].astype(F32)
    payload[:, :tokens, :] = blocks[...]
    for h in range(heads):
        get = lambda k: aux[:, :, k * heads + h : k * heads + h + 1]
        top = get(0) + get(1) + get(2)
        total = get(3) + get(4)
        factor = jnp.exp(top - jnp.max(top, axis=0, keepdims=True))
        norm = jnp.sum(factor * total, axis=0)
        value = parts[:, :, h * size : (h + 1) * size].astype(F32)
        summed = jnp.sum(factor * value, axis=0)
        piece = (summed / norm).astype(BF)
        for j in range(peers):
            payload[j, tokens + h * own : tokens + (h + 1) * own, :size] = piece


def join(parts, blocks, heads, size):
    members, tokens, share = blocks.shape
    own = parts.shape[1]
    out = jax.ShapeDtypeStruct((members, tokens + heads * own, share), BF)
    return pl.pallas_call(
        functools.partial(join_kernel, heads=heads, size=size),
        grid=(1,),
        in_specs=whole([parts, blocks]),
        out_specs=whole([out])[0],
        out_shape=out,
        compiler_params=PARAMS,
        name="join",
    )(parts, blocks)


def project_kernel(parts, out_weight, spread, *, heads, size):
    peers, packed, _ = spread.shape
    own = (parts.shape[1] - packed) // heads
    tokens = own * peers
    acc = unfold(jnp.sum(parts[:, :packed, :].astype(F32), axis=0), tokens)
    for h in range(heads):
        attended = jnp.concatenate(
            [parts[j, packed + h * own : packed + (h + 1) * own, :size] for j in range(peers)],
            axis=0,
        )
        acc = acc + dot_nt(attended, out_weight[:, h * size : (h + 1) * size])
    out = fold(acc).astype(BF)
    for j in range(peers):
        spread[j] = out


def project(parts, out_weight, packed, heads, size):
    members = parts.shape[0]
    out = jax.ShapeDtypeStruct((members, packed, AUX), BF)
    return pl.pallas_call(
        functools.partial(project_kernel, heads=heads, size=size),
        grid=(1,),
        in_specs=whole([parts, out_weight]),
        out_specs=whole([out])[0],
        out_shape=out,
        compiler_params=PARAMS,
        name="project",
    )(parts, out_weight)


def feed_kernel(spread, embedded, gain, *refs, count):
    weights = refs[:count]
    out, mixed, gates, ups, downs, sems = refs[count:]
    peers, own, width = out.shape
    tokens = embedded.shape[0]
    total = gates.shape[0]
    pieces = []
    begin = 0
    units = min(w.shape[0] for w in weights) // 3
    for w in weights:
        for first in range(0, w.shape[0], 3 * units):
            pieces.append((w, first, begin))
            begin += units
    copies = []
    for n, (w, first, at) in enumerate(pieces):
        trio = []
        for k, to in enumerate((gates, ups, downs)):
            copy = pltpu.make_async_copy(
                w.at[pl.ds(first + k * units, units), :], to.at[pl.ds(at, units), :], sems.at[n, k]
            )
            copy.start()
            trio.append(copy)
        copies.append((at + units, trio))
    added = jnp.concatenate([unfold(spread[j].astype(F32), tokens) for j in range(peers)], axis=1)
    rows = (embedded[...].astype(F32) + added).astype(BF)
    mixed[...] = rows
    wide = rows.astype(F32)
    factor = lax.rsqrt(jnp.mean(wide * wide, axis=-1, keepdims=True) + 1e-05)
    second = (wide * factor * gain[...]).astype(BF)
    chunk = 256
    waited = 0
    ready = 0
    acc = None
    for c in range(total // chunk):
        while ready < (c + 1) * chunk:
            ready, trio = copies[waited]
            for copy in trio:
                copy.wait()
            waited += 1
        span = slice(c * chunk, (c + 1) * chunk)
        gate = dot_nt(second, gates[span, :])
        up = dot_nt(second, ups[span, :])
        hidden = (gate / (1.0 + jnp.exp(-gate)) * up).astype(BF)
        part = dot_nn(hidden, downs[span, :])
        acc = part if acc is None else acc + part
    for j in range(peers):
        out[j] = acc[j * own : (j + 1) * own, :].astype(BF)


def feed(spread, embedded, gain, weights):
    members = spread.shape[0]
    tokens, width = embedded.shape
    units = sum(w.shape[0] for w in weights) // 3
    count = 3 * units // min(w.shape[0] for w in weights)
    outs = [
        jax.ShapeDtypeStruct((members, tokens // members, width), BF),
        jax.ShapeDtypeStruct((tokens, width), BF),
    ]
    return pl.pallas_call(
        functools.partial(feed_kernel, count=len(weights)),
        grid=(1,),
        in_specs=whole([spread, embedded, gain]) + streamed(len(weights)),
        out_specs=whole(outs),
        out_shape=outs,
        scratch_shapes=[pltpu.VMEM((units, width), BF)] * 3
        + [pltpu.SemaphoreType.DMA((count, 3))],
        compiler_params=PARAMS,
        cost_estimate=cost(6 * tokens * units * width, 6 * units * width),
        name="feed",
    )(spread, embedded, gain, *weights)


def pack_kernel(gate, up, down, ready, low, high, sems):
    half = low.shape[0] // 3
    copies = []
    for k, part in enumerate((gate, up, down)):
        for h, out in enumerate((low, high)):
            copy = pltpu.make_async_copy(
                part.at[pl.ds(h * half, half), :],
                out.at[pl.ds(k * half, half), :],
                sems.at[k, h],
            )
            copy.start()
            copies.append(copy)
    for copy in copies:
        copy.wait()


def pack(gate, up, down, ready):
    units, width = gate.shape
    out = jax.ShapeDtypeStruct((3 * units // 2, width), gate.dtype)
    return pl.pallas_call(
        pack_kernel,
        in_specs=streamed(4),
        out_specs=streamed(2),
        out_shape=[out, out],
        scratch_shapes=[pltpu.SemaphoreType.DMA((3, 2))],
        compiler_params=PARAMS,
        cost_estimate=cost(0, 1024),
        name="pack",
    )(gate, up, down, ready)


def pick_kernel(turns, rows, *refs):
    held = refs[:-1]
    out = refs[-1]
    for i in range(out.shape[0]):
        for n, ref in enumerate(held):

            @pl.when(turns[i] == n)
            def _():
                out[i] = ref[rows[i]].astype(F32)


def pick_states(turns, rows, held, count):
    shape = (count,) + held[0].shape[1:]
    out = jax.ShapeDtypeStruct(shape, F32)
    return pl.pallas_call(
        pick_kernel,
        grid=(1,),
        in_specs=scalars(2) + whole(held),
        out_specs=whole([out])[0],
        out_shape=out,
        compiler_params=PARAMS,
        name="pick",
    )(turns, rows, *held)


def local(
    draft_ids,
    lengths,
    current_slot,
    new_slot,
    accepted,
    embed_table,
    mixer_gain,
    query_weight,
    keyvalue_weight,
    key_cache,
    value_cache,
    attention_out,
    mamba_input,
    mamba_gate,
    state_proj,
    mamba_step,
    step_bias,
    decay_log,
    skip_gain,
    states,
    mamba_out,
    mlp_gain,
    gate_weight,
    up_weight,
    down_weight,
):
    members = lax.axis_size("tok")
    groups = lax.axis_size("req")
    group_index = lax.axis_index("req")
    member = lax.axis_index("tok")
    slots_dev, cache_dev, head_size = key_cache.shape
    draft_len = draft_ids.shape[1]
    width = embed_table.shape[1]
    query_heads = query_weight.shape[1] // head_size
    own = slots_dev * draft_len // members

    cores = 2
    chips = groups // cores

    def turn(value, by):
        return lax.ppermute(
            value, "req", [(g, (g + by * cores) % groups) for g in range(groups)]
        )

    def across(value):
        return lax.ppermute(value, "req", [(g, g ^ 1) for g in range(groups)])

    def exchange(base):
        where = jnp.stack([group_index, member, base]).astype(jnp.int32)
        payload, places, most = fetch(
            where, current_slot[None], draft_ids, embed_table, groups, members, ROOM
        )
        slots = lax.all_to_all(payload, "req", 0, 0, tiled=True)
        return payload, slots, places, most[0, 0]

    def spread_slots(slots):
        held = jnp.sum(slots.astype(F32), axis=0).astype(BF)
        spread = jnp.broadcast_to(held[None], (members,) + held.shape)
        return lax.all_to_all(spread, "tok", 0, 0, tiled=True)

    sent, slots, places, most = exchange(jnp.int32(0))

    low, high = pack(gate_weight.T, up_weight.T, down_weight.T, sent)
    low, high, _ = lax.optimization_barrier((low, high, slots))
    arrived = spread_slots(slots)
    near = [turn(low, 1), turn(high, -1), turn(high, 1), turn(low, -1)]

    def more(carry):
        return carry[0] < most

    def round_of(carry):
        base, rows = carry
        _, later, spots, _ = exchange(base)
        return base + ROOM, place(spread_slots(later), spots, rows)

    _, extra = lax.while_loop(
        more, round_of, (jnp.int32(ROOM), jnp.zeros((members * own, width), BF))
    )

    slot_owner = inverse_of(current_slot)
    local_owner = lax.dynamic_slice_in_dim(slot_owner, group_index * slots_dev, slots_dev)
    ints = jnp.concatenate(
        [jnp.take(lengths, local_owner), jnp.take(accepted, local_owner), member[None]]
    )
    reals = jnp.concatenate([step_bias, jnp.exp(decay_log), skip_gain])
    payload, embedded, normed = attend(
        ints,
        arrived,
        places,
        extra,
        mixer_gain[None],
        query_weight,
        keyvalue_weight,
        key_cache,
        value_cache,
    )
    parts = lax.all_to_all(payload, "tok", 0, 0, tiled=True)
    blocks, chosen = mamba(
        ints,
        reals,
        normed,
        mamba_input,
        mamba_gate,
        state_proj,
        mamba_step.T,
        states,
        mamba_out,
        members,
    )
    *near, chosen, _ = lax.optimization_barrier((*near, chosen, parts))
    far = [turn(near[0], 1), turn(near[1], -1)]
    weights = [low, high] + near
    weights += [across(w) for w in weights]
    joined = lax.all_to_all(join(parts, blocks, query_heads, head_size), "tok", 0, 0, tiled=True)
    spread = project(joined, attention_out.T, blocks.shape[1], query_heads, head_size)
    *far, _ = lax.optimization_barrier((*far, spread))
    weights += far + [across(w) for w in far]
    added = lax.all_to_all(spread, "tok", 0, 0, tiled=True)
    mlp_part, mixed = feed(added, embedded, mlp_gain[None], weights)
    mlp_rows = lax.all_to_all(mlp_part, "tok", 0, 0, tiled=True)
    own_rows = lax.dynamic_slice_in_dim(mixed, member * own, own)
    hidden_out = (own_rows.astype(F32) + jnp.sum(mlp_rows.astype(F32), axis=0)).astype(BF)

    incoming = inverse_of(new_slot)
    local_targets = lax.dynamic_slice_in_dim(incoming, group_index * slots_dev, slots_dev)
    sources = jnp.take(current_slot, local_targets)
    chosen = chosen[:, 0]
    pair = jnp.concatenate([chosen, across(chosen)], axis=0)
    held = [pair] + [turn(pair, by) for by in range(1, chips)]
    source_group = sources // slots_dev
    turns = (group_index // cores - source_group // cores) % chips
    other_core = (source_group % cores) != (group_index % cores)
    rows = sources % slots_dev + jnp.where(other_core, slots_dev, 0)
    new_states = pick_states(turns, rows, held, slots_dev)[:, None]
    return (hidden_out, new_states)


def solution(mesh):
    return jax.shard_map(
        local,
        mesh=mesh,
        in_specs=(
            P(),
            P(),
            P(),
            P(),
            P(),
            P(("req", "tok"), None),
            P(),
            P(),
            P(),
            P("req", "tok", None),
            P("req", "tok", None),
            P(None, "tok"),
            P(None, "tok"),
            P(None, "tok"),
            P(),
            P(None, "tok"),
            P("tok"),
            P("tok"),
            P("tok"),
            P("req", "tok", None, None),
            P("tok", None),
            P(),
            P(None, ("req", "tok")),
            P(None, ("req", "tok")),
            P(None, ("req", "tok")),
        ),
        out_specs=(P(("req", "tok"), None), P("req", "tok", None, None)),
        check_vma=False,
    )
```

```python
import functools

import jax
import jax.numpy as jnp
from jax import lax
from jax.experimental import pallas as pl
from jax.experimental.pallas import tpu as pltpu
from jax.sharding import PartitionSpec as P

BF = jnp.bfloat16
F32 = jnp.float32
NEG = -1e30
AUX = 128
ROOM = 16


def inverse_of(mapping):
    places = jnp.arange(mapping.shape[0], dtype=jnp.int32)
    matches = mapping[None, :] == places[:, None]
    return jnp.sum(jnp.where(matches, places[None, :], 0), axis=1)


def dot_nn(a, b, precision=None):
    return lax.dot_general(
        a, b, (((1,), (0,)), ((), ())), precision=precision, preferred_element_type=F32
    )


def dot_nt(a, b, precision=None):
    return lax.dot_general(
        a, b, (((1,), (1,)), ((), ())), precision=precision, preferred_element_type=F32
    )


def dot_tn(a, b, precision=None):
    return lax.dot_general(
        a, b, (((0,), (0,)), ((), ())), precision=precision, preferred_element_type=F32
    )


HI = lax.Precision.HIGHEST


def cost(flops, moved, special=0):
    return pl.CostEstimate(flops=flops, bytes_accessed=moved, transcendentals=special)


def whole(shapes):
    return [pl.BlockSpec(a.shape, lambda i, n=len(a.shape): (0,) * n) for a in shapes]


def streamed(count):
    return [pl.BlockSpec(memory_space=pltpu.HBM)] * count


def scalars(count):
    return [pl.BlockSpec(memory_space=pltpu.SMEM)] * count


PARAMS = pltpu.CompilerParams(vmem_limit_bytes=60 << 20)


def fetch_kernel(
    ints, slots_row, draft_ids, table_far, payload, places, most, table, sem, *, members
):
    load = pltpu.make_async_copy(table_far, table, sem)
    load.start()
    groups, room, width = payload.shape
    requests, drafts = draft_ids.shape
    vocab = table.shape[0]
    count = requests * drafts // groups
    slots = requests // groups
    group, member, base = ints[0], ints[1], ints[2]
    me = group * members + member
    sub = lax.broadcasted_iota(jnp.int32, (count, count), 0)
    lane = lax.broadcasted_iota(jnp.int32, (count, count), 1)
    ids = draft_ids[...]
    ids_hi = (ids // 256).astype(F32).astype(BF)
    ids_lo = (ids % 256).astype(F32).astype(BF)
    row_slot = lax.broadcasted_iota(jnp.int32, (count, requests), 0) // drafts
    token = lax.broadcasted_iota(jnp.int32, (count, drafts), 0) % drafts
    token_lane = lax.broadcasted_iota(jnp.int32, (count, drafts), 1)
    slot_iota = lax.broadcasted_iota(jnp.int32, (room, count), 0) + base
    local_iota = lax.broadcasted_iota(jnp.int32, (room, vocab), 1)
    hots = []
    own_place = jnp.zeros((count, 1), jnp.int32)
    peak = jnp.zeros((1, count), jnp.int32)
    for g in range(groups):
        pick = jnp.where(slots_row[...] == row_slot + g * slots, 1.0, 0.0).astype(BF)
        mixed_ids = dot_nn(pick, ids_hi) * 256.0 + dot_nn(pick, ids_lo)
        id_c = jnp.sum(
            jnp.where(token == token_lane, mixed_ids, 0.0), axis=1, keepdims=True
        ).astype(jnp.int32)
        id_r = jnp.sum(jnp.where(sub == lane, id_c, 0), axis=0, keepdims=True)
        same = id_c == id_r
        first_c = jnp.min(jnp.where(same, lane, count), axis=1, keepdims=True)
        first_r = jnp.min(jnp.where(same, sub, count), axis=0, keepdims=True)
        sub_c = sub[:, :1]
        lane_r = lane[:1, :]
        owner_c = id_c // vocab
        owner_r = id_r // vocab
        column_c = owner_c % members
        column_r = owner_r % members
        alike = column_c == column_r
        before_r = jnp.where(alike & (first_c == sub_c) & (sub < first_r), 1, 0)
        rank_r = jnp.sum(before_r, axis=0, keepdims=True)
        peak = jnp.maximum(peak, rank_r + 1)
        before_c = jnp.where(alike & (first_r == lane_r) & (lane < first_c), 1, 0)
        rank_c = jnp.sum(before_c, axis=1, keepdims=True)
        inside = (rank_c >= base) & (rank_c < base + room)
        place = jnp.where(inside, column_c * room + rank_c - base, -1)
        own_place = jnp.where(group == g, place, own_place)
        mine = (first_r == lane_r) & (owner_r == me)
        asked = jnp.where(mine & (rank_r == slot_iota), id_r % vocab + 1, 0)
        row = jnp.sum(asked, axis=1, keepdims=True) - 1
        hots.append(jnp.where(local_iota == row, 1.0, 0.0))
    hot = jnp.concatenate(hots, axis=0).astype(BF)
    load.wait()
    rows = dot_nn(hot, table[...])
    for g in range(groups):
        payload[g] = rows[g * room : (g + 1) * room].astype(BF)
    places[...] = jnp.broadcast_to(own_place, places.shape)
    most[...] = jnp.broadcast_to(jnp.max(peak, axis=1, keepdims=True), most.shape)


def fetch(ints, slots_row, draft_ids, table, groups, members, room):
    count = draft_ids.size // groups
    width = table.shape[1]
    outs = [
        jax.ShapeDtypeStruct((groups, room, width), BF),
        jax.ShapeDtypeStruct((count, AUX), jnp.int32),
        jax.ShapeDtypeStruct((8, AUX), jnp.int32),
    ]
    return pl.pallas_call(
        functools.partial(fetch_kernel, members=members),
        grid=(1,),
        in_specs=scalars(1) + whole([slots_row, draft_ids]) + streamed(1),
        out_specs=whole(outs),
        out_shape=outs,
        scratch_shapes=[pltpu.VMEM(table.shape, table.dtype), pltpu.SemaphoreType.DMA],
        compiler_params=PARAMS,
        cost_estimate=cost(2 * groups * room * table.size, 2 * table.size),
        name="fetch",
    )(ints, slots_row, draft_ids, table)


def rows_of(arrived, places):
    peers, room, width = arrived.shape
    count = places.shape[0]
    slot = lax.broadcasted_iota(jnp.int32, (count, peers * room), 1)
    hot = jnp.where(slot == places[:, :1], 1.0, 0.0).astype(BF)
    slots = jnp.concatenate([arrived[j] for j in range(peers)], axis=0)
    return dot_nn(hot, slots)


def place_kernel(arrived, places, before, out):
    out[...] = (before[...].astype(F32) + rows_of(arrived, places)).astype(BF)


def place(arrived, places, before):
    return pl.pallas_call(
        place_kernel,
        grid=(1,),
        in_specs=whole([arrived, places, before]),
        out_specs=whole([before])[0],
        out_shape=jax.ShapeDtypeStruct(before.shape, BF),
        compiler_params=PARAMS,
        name="place",
    )(arrived, places, before)


def attend_kernel(
    ints,
    arrived,
    places,
    extra,
    gain,
    query_weight,
    keyvalue_weight,
    keys,
    values,
    payload,
    embedded,
    normed,
    query_in,
    keyvalue_in,
    keys_in,
    values_in,
    sems,
):
    moves = []
    third = query_weight.shape[0] // 3
    for k in range(3):
        span = pl.ds(k * third, third)
        moves.append((query_weight.at[span, :], query_in.at[span, :]))
    moves += [(keyvalue_weight, keyvalue_in), (keys, keys_in), (values, values_in)]
    copies = [pltpu.make_async_copy(a, b, sems.at[n]) for n, (a, b) in enumerate(moves)]
    for copy in copies:
        copy.start()
    slots, cache, size = keys.shape
    tokens = extra.shape[0]
    drafts = tokens // slots
    heads = query_weight.shape[1] // size
    own = payload.shape[1]
    rows_in = (rows_of(arrived, places) + extra[...].astype(F32)).astype(BF)
    embedded[...] = rows_in
    wide = rows_in.astype(F32)
    factor = lax.rsqrt(jnp.mean(wide * wide, axis=-1, keepdims=True) + 1e-05)
    rows_norm = (wide * factor * gain[...]).astype(BF)
    normed[...] = rows_norm
    queries = None
    for k in range(3):
        copies[k].wait()
        span = slice(k * third, (k + 1) * third)
        part = dot_nn(rows_norm[:, span], query_in[span, :])
        queries = part if queries is None else queries + part
    queries = queries.astype(BF)
    copies[3].wait()
    keyvalue = dot_nn(rows_norm, keyvalue_in[...]).astype(BF)
    copies[4].wait()
    copies[5].wait()
    member = ints[8]
    scale = size ** (-0.5)
    rows = heads * drafts
    position = lax.broadcasted_iota(jnp.int32, (rows, cache), 1) + member * cache
    token = lax.broadcasted_iota(jnp.int32, (rows, drafts), 0) % drafts
    other = lax.broadcasted_iota(jnp.int32, (rows, drafts), 1)
    seen = other <= jnp.where(member == 0, token, -1)
    lane = lax.broadcasted_iota(jnp.int32, (drafts, AUX), 1)
    for slot in range(slots):
        span = slice(slot * drafts, (slot + 1) * drafts)
        length = ints[slot]
        query = jnp.concatenate(
            [queries[span, h * size : (h + 1) * size] for h in range(heads)], axis=0
        )
        scores = dot_nt(query, keys_in[slot]) * scale
        scores = jnp.where(position < length, scores, NEG)
        draft_scores = dot_nt(query, keyvalue[span, :size]) * scale
        draft_scores = jnp.where(seen, draft_scores, NEG)
        top = jnp.maximum(
            jnp.max(scores, axis=-1, keepdims=True),
            jnp.max(draft_scores, axis=-1, keepdims=True),
        )
        probs = jnp.where(position < length, jnp.exp(scores - top), 0.0)
        draft_probs = jnp.where(seen, jnp.exp(draft_scores - top), 0.0)
        total = jnp.sum(probs, axis=-1, keepdims=True) + jnp.sum(
            draft_probs, axis=-1, keepdims=True
        )
        summed = dot_nn(probs.astype(BF), values_in[slot]) + dot_nn(
            draft_probs.astype(BF), keyvalue[span, size:]
        )
        top_a = top.astype(BF).astype(F32)
        top_b = (top - top_a).astype(BF).astype(F32)
        top_c = top - top_a - top_b
        total_a = total.astype(BF).astype(F32)
        total_b = total - total_a
        aux = jnp.zeros((drafts, AUX), F32)
        for k, piece in enumerate((top_a, top_b, top_c, total_a, total_b)):
            for h in range(heads):
                part = piece[h * drafts : (h + 1) * drafts]
                aux = jnp.where(lane == k * heads + h, part, aux)
        flat = jnp.concatenate(
            [summed[h * drafts : (h + 1) * drafts] for h in range(heads)] + [aux], axis=1
        ).astype(BF)
        for q in range(drafts // own):
            payload[slot * (drafts // own) + q] = flat[q * own : (q + 1) * own]


def attend(ints, arrived, places, extra, gain, query_weight, keyvalue_weight, keys, values):
    tokens, width = extra.shape
    members = arrived.shape[0]
    wide = query_weight.shape[1] + AUX
    far = (query_weight, keyvalue_weight, keys, values)
    outs = [
        jax.ShapeDtypeStruct((members, tokens // members, wide), BF),
        jax.ShapeDtypeStruct((tokens, width), BF),
        jax.ShapeDtypeStruct((tokens, width), BF),
    ]
    return pl.pallas_call(
        attend_kernel,
        grid=(1,),
        in_specs=scalars(1) + whole([arrived, places, extra, gain]) + streamed(4),
        out_specs=whole(outs),
        out_shape=outs,
        scratch_shapes=[pltpu.VMEM(a.shape, a.dtype) for a in far]
        + [pltpu.SemaphoreType.DMA((6,))],
        compiler_params=PARAMS,
        cost_estimate=cost(
            2 * tokens * query_weight.size * 2, 2 * (query_weight.size + keys.size * 2), keys.size
        ),
        name="attend",
    )(ints, arrived, places, extra, gain, query_weight, keyvalue_weight, keys, values)


def fold(block):
    half = block.shape[0] // 2
    rest = jnp.concatenate([block[:half, AUX:], block[half:, AUX:]], axis=1)
    return jnp.concatenate([block[:, :AUX], rest], axis=0)


def unfold(block, tokens):
    half = AUX // 2
    rest = jnp.concatenate([block[tokens:, :half], block[tokens:, half:]], axis=0)
    return jnp.concatenate([block[:tokens], rest], axis=1)


def mamba_kernel(
    ints,
    reals,
    normed,
    input_weight,
    gate_weight,
    state_proj,
    step_row,
    states,
    mamba_out,
    blocks,
    chosen,
    proj_in,
    input_in,
    gate_in,
    states_in,
    out_in,
    sems,
):
    moves = (
        (state_proj, proj_in),
        (input_weight, input_in),
        (gate_weight, gate_in),
        (states, states_in),
        (mamba_out, out_in),
    )
    copies = [pltpu.make_async_copy(a, b, sems.at[n]) for n, (a, b) in enumerate(moves)]
    for copy in copies:
        copy.start()
    slots = states.shape[0]
    tokens = normed.shape[0]
    drafts = tokens // slots
    rows = normed[...]
    step_in = (
        jnp.sum(rows.astype(F32) * step_row[...].astype(F32), axis=1, keepdims=True) + reals[0]
    )
    sizes = jnp.maximum(step_in, 0.0) + jnp.log1p(jnp.exp(-jnp.abs(step_in)))
    copies[0].wait()
    both = dot_nn(rows, proj_in[...])
    copies[1].wait()
    x_all = dot_nn(rows, input_in[...])
    copies[2].wait()
    z_all = dot_nn(rows, gate_in[...])
    copies[3].wait()
    state_size = both.shape[1] // 2
    row = lax.broadcasted_iota(jnp.int32, (drafts, drafts), 0)
    col = lax.broadcasted_iota(jnp.int32, (drafts, drafts), 1)
    rows_in = lax.broadcasted_iota(jnp.int32, (drafts, 1), 0)
    gated = []
    for slot in range(slots):
        span = slice(slot * drafts, (slot + 1) * drafts)
        accept = ints[4 + slot]
        size_t = sizes[span]
        size_row = jnp.sum(jnp.where(row == col, size_t, 0.0), axis=0, keepdims=True)
        log_decay = -reals[1] * jnp.sum(
            jnp.where(col <= row, size_row, 0.0), axis=1, keepdims=True
        )
        log_row = jnp.sum(jnp.where(row == col, log_decay, 0.0), axis=0, keepdims=True)
        between = jnp.exp(jnp.where(col <= row, log_decay - log_row, NEG))
        state_in = both[span, :state_size]
        state_read = both[span, state_size:]
        x = x_all[span]
        z = z_all[span]
        inputs = size_t * x
        start = states_in[slot, 0]
        weights = dot_nt(state_read, state_in, HI) * between
        readout = dot_nn(weights, inputs, HI) + jnp.exp(log_decay) * dot_nt(
            state_read, start, HI
        )
        readout = readout + reals[2] * x
        last = jnp.sum(jnp.where(rows_in == accept - 1, log_decay, 0.0), axis=0, keepdims=True)
        remain = jnp.exp(jnp.where(rows_in < accept, last - log_decay, NEG))
        chosen[slot, 0] = (
            jnp.exp(last) * start + dot_tn(remain * inputs, state_in, HI)
        ).astype(BF)
        gated.append((readout * (z / (1.0 + jnp.exp(-z)))).astype(BF))
    copies[4].wait()
    part = dot_nn(jnp.concatenate(gated, axis=0), out_in[...])
    share = part.shape[1] // blocks.shape[0]
    for j in range(blocks.shape[0]):
        blocks[j] = fold(part[:, j * share : (j + 1) * share]).astype(BF)


def mamba(ints, reals, normed, input_weight, gate_weight, state_proj, step_row, states, mamba_out, members):
    tokens = normed.shape[0]
    share = mamba_out.shape[1] // members
    outs = [
        jax.ShapeDtypeStruct((members, tokens * share // AUX, AUX), BF),
        jax.ShapeDtypeStruct(states.shape, BF),
    ]
    far = (state_proj, input_weight, gate_weight, states, mamba_out)
    return pl.pallas_call(
        mamba_kernel,
        grid=(1,),
        in_specs=scalars(2)
        + whole([normed])
        + streamed(3)
        + whole([step_row])
        + streamed(2),
        out_specs=whole(outs),
        out_shape=outs,
        scratch_shapes=[pltpu.VMEM(a.shape, a.dtype) for a in far]
        + [pltpu.SemaphoreType.DMA((5,))],
        compiler_params=PARAMS,
        cost_estimate=cost(2 * tokens * state_proj.size * 2, 4 * state_proj.size, tokens * 4096),
        name="mamba",
    )(ints, reals, normed, input_weight, gate_weight, state_proj, step_row, states, mamba_out)


def join_kernel(parts, blocks, payload, *, heads, size):
    peers, tokens, _ = blocks.shape
    own = parts.shape[1]
    aux = parts[:, :, heads * size : heads * size + AUX].astype(F32)
    payload[:, :tokens, :] = blocks[...]
    for h in range(heads):
        get = lambda k: aux[:, :, k * heads + h : k * heads + h + 1]
        top = get(0) + get(1) + get(2)
        total = get(3) + get(4)
        factor = jnp.exp(top - jnp.max(top, axis=0, keepdims=True))
        norm = jnp.sum(factor * total, axis=0)
        value = parts[:, :, h * size : (h + 1) * size].astype(F32)
        summed = jnp.sum(factor * value, axis=0)
        piece = (summed / norm).astype(BF)
        for j in range(peers):
            payload[j, tokens + h * own : tokens + (h + 1) * own, :size] = piece


def join(parts, blocks, heads, size):
    members, tokens, share = blocks.shape
    own = parts.shape[1]
    out = jax.ShapeDtypeStruct((members, tokens + heads * own, share), BF)
    return pl.pallas_call(
        functools.partial(join_kernel, heads=heads, size=size),
        grid=(1,),
        in_specs=whole([parts, blocks]),
        out_specs=whole([out])[0],
        out_shape=out,
        compiler_params=PARAMS,
        name="join",
    )(parts, blocks)


def project_kernel(parts, out_weight, spread, *, heads, size):
    peers, packed, _ = spread.shape
    own = (parts.shape[1] - packed) // heads
    tokens = own * peers
    acc = unfold(jnp.sum(parts[:, :packed, :].astype(F32), axis=0), tokens)
    for h in range(heads):
        attended = jnp.concatenate(
            [parts[j, packed + h * own : packed + (h + 1) * own, :size] for j in range(peers)],
            axis=0,
        )
        acc = acc + dot_nt(attended, out_weight[:, h * size : (h + 1) * size])
    out = fold(acc).astype(BF)
    for j in range(peers):
        spread[j] = out


def project(parts, out_weight, packed, heads, size):
    members = parts.shape[0]
    out = jax.ShapeDtypeStruct((members, packed, AUX), BF)
    return pl.pallas_call(
        functools.partial(project_kernel, heads=heads, size=size),
        grid=(1,),
        in_specs=whole([parts, out_weight]),
        out_specs=whole([out])[0],
        out_shape=out,
        compiler_params=PARAMS,
        name="project",
    )(parts, out_weight)


def feed_kernel(spread, embedded, gain, *refs, count):
    weights = refs[:count]
    out, mixed, gates, ups, downs, sems = refs[count:]
    peers, own, width = out.shape
    tokens = embedded.shape[0]
    total = gates.shape[0]
    pieces = []
    begin = 0
    units = min(w.shape[0] for w in weights) // 3
    for w in weights:
        for first in range(0, w.shape[0], 3 * units):
            pieces.append((w, first, begin))
            begin += units
    copies = []
    for n, (w, first, at) in enumerate(pieces):
        trio = []
        for k, to in enumerate((gates, ups, downs)):
            copy = pltpu.make_async_copy(
                w.at[pl.ds(first + k * units, units), :], to.at[pl.ds(at, units), :], sems.at[n, k]
            )
            copy.start()
            trio.append(copy)
        copies.append((at + units, trio))
    added = jnp.concatenate([unfold(spread[j].astype(F32), tokens) for j in range(peers)], axis=1)
    rows = (embedded[...].astype(F32) + added).astype(BF)
    mixed[...] = rows
    wide = rows.astype(F32)
    factor = lax.rsqrt(jnp.mean(wide * wide, axis=-1, keepdims=True) + 1e-05)
    second = (wide * factor * gain[...]).astype(BF)
    chunk = 256
    waited = 0
    ready = 0
    acc = None
    for c in range(total // chunk):
        while ready < (c + 1) * chunk:
            ready, trio = copies[waited]
            for copy in trio:
                copy.wait()
            waited += 1
        span = slice(c * chunk, (c + 1) * chunk)
        gate = dot_nt(second, gates[span, :])
        up = dot_nt(second, ups[span, :])
        hidden = (gate / (1.0 + jnp.exp(-gate)) * up).astype(BF)
        part = dot_nn(hidden, downs[span, :])
        acc = part if acc is None else acc + part
    for j in range(peers):
        out[j] = acc[j * own : (j + 1) * own, :].astype(BF)


def feed(spread, embedded, gain, weights):
    members = spread.shape[0]
    tokens, width = embedded.shape
    units = sum(w.shape[0] for w in weights) // 3
    count = 3 * units // min(w.shape[0] for w in weights)
    outs = [
        jax.ShapeDtypeStruct((members, tokens // members, width), BF),
        jax.ShapeDtypeStruct((tokens, width), BF),
    ]
    return pl.pallas_call(
        functools.partial(feed_kernel, count=len(weights)),
        grid=(1,),
        in_specs=whole([spread, embedded, gain]) + streamed(len(weights)),
        out_specs=whole(outs),
        out_shape=outs,
        scratch_shapes=[pltpu.VMEM((units, width), BF)] * 3
        + [pltpu.SemaphoreType.DMA((count, 3))],
        compiler_params=PARAMS,
        cost_estimate=cost(6 * tokens * units * width, 6 * units * width),
        name="feed",
    )(spread, embedded, gain, *weights)


def pack_kernel(gate, up, down, ready, low, high):
    half = low.shape[0] // 3
    for k, part in enumerate((gate, up, down)):
        low[k * half : (k + 1) * half] = part[:half]
        high[k * half : (k + 1) * half] = part[half:]


def pack(gate, up, down, ready):
    units, width = gate.shape
    out = jax.ShapeDtypeStruct((3 * units // 2, width), gate.dtype)
    return pl.pallas_call(
        pack_kernel,
        grid=(1,),
        in_specs=whole([gate, up, down]) + streamed(1),
        out_specs=whole([out, out]),
        out_shape=[out, out],
        compiler_params=PARAMS,
        cost_estimate=cost(0, 1024),
        name="pack",
    )(gate, up, down, ready)


def pick_kernel(turns, rows, *refs):
    held = refs[:-1]
    out = refs[-1]
    for i in range(out.shape[0]):
        for n, ref in enumerate(held):

            @pl.when(turns[i] == n)
            def _():
                out[i] = ref[rows[i]].astype(F32)


def pick_states(turns, rows, held, count):
    shape = (count,) + held[0].shape[1:]
    out = jax.ShapeDtypeStruct(shape, F32)
    return pl.pallas_call(
        pick_kernel,
        grid=(1,),
        in_specs=scalars(2) + whole(held),
        out_specs=whole([out])[0],
        out_shape=out,
        compiler_params=PARAMS,
        name="pick",
    )(turns, rows, *held)


def local(
    draft_ids,
    lengths,
    current_slot,
    new_slot,
    accepted,
    embed_table,
    mixer_gain,
    query_weight,
    keyvalue_weight,
    key_cache,
    value_cache,
    attention_out,
    mamba_input,
    mamba_gate,
    state_proj,
    mamba_step,
    step_bias,
    decay_log,
    skip_gain,
    states,
    mamba_out,
    mlp_gain,
    gate_weight,
    up_weight,
    down_weight,
):
    members = lax.axis_size("tok")
    groups = lax.axis_size("req")
    group_index = lax.axis_index("req")
    member = lax.axis_index("tok")
    slots_dev, cache_dev, head_size = key_cache.shape
    draft_len = draft_ids.shape[1]
    width = embed_table.shape[1]
    query_heads = query_weight.shape[1] // head_size
    own = slots_dev * draft_len // members

    cores = 2
    chips = groups // cores

    def turn(value, by):
        return lax.ppermute(
            value, "req", [(g, (g + by * cores) % groups) for g in range(groups)]
        )

    def across(value):
        return lax.ppermute(value, "req", [(g, g ^ 1) for g in range(groups)])

    def exchange(base):
        where = jnp.stack([group_index, member, base]).astype(jnp.int32)
        payload, places, most = fetch(
            where, current_slot[None], draft_ids, embed_table, groups, members, ROOM
        )
        slots = lax.all_to_all(payload, "req", 0, 0, tiled=True)
        return payload, slots, places, most[0, 0]

    def spread_slots(slots):
        held = jnp.sum(slots.astype(F32), axis=0).astype(BF)
        spread = jnp.broadcast_to(held[None], (members,) + held.shape)
        return lax.all_to_all(spread, "tok", 0, 0, tiled=True)

    sent, slots, places, most = exchange(jnp.int32(0))

    low, high = pack(gate_weight.T, up_weight.T, down_weight.T, sent)
    low, high, slots = lax.optimization_barrier((low, high, slots))
    arrived = spread_slots(slots)
    near = [turn(low, 1), turn(high, -1), turn(high, 1), turn(low, -1)]

    def more(carry):
        return carry[0] < most

    def round_of(carry):
        base, rows = carry
        _, later, spots, _ = exchange(base)
        return base + ROOM, place(spread_slots(later), spots, rows)

    _, extra = lax.while_loop(
        more, round_of, (jnp.int32(ROOM), jnp.zeros((members * own, width), BF))
    )

    slot_owner = inverse_of(current_slot)
    local_owner = lax.dynamic_slice_in_dim(slot_owner, group_index * slots_dev, slots_dev)
    ints = jnp.concatenate(
        [jnp.take(lengths, local_owner), jnp.take(accepted, local_owner), member[None]]
    )
    reals = jnp.concatenate([step_bias, jnp.exp(decay_log), skip_gain])
    payload, embedded, normed = attend(
        ints,
        arrived,
        places,
        extra,
        mixer_gain[None],
        query_weight,
        keyvalue_weight,
        key_cache,
        value_cache,
    )
    parts = lax.all_to_all(payload, "tok", 0, 0, tiled=True)
    blocks, chosen = mamba(
        ints,
        reals,
        normed,
        mamba_input,
        mamba_gate,
        state_proj,
        mamba_step.T,
        states,
        mamba_out,
        members,
    )
    *near, chosen, _ = lax.optimization_barrier((*near, chosen, parts))
    far = [turn(near[0], 1), turn(near[1], -1)]
    weights = [low, high] + near
    weights += [across(w) for w in weights]
    joined = lax.all_to_all(join(parts, blocks, query_heads, head_size), "tok", 0, 0, tiled=True)
    spread = project(joined, attention_out.T, blocks.shape[1], query_heads, head_size)
    *far, _ = lax.optimization_barrier((*far, spread))
    weights += far + [across(w) for w in far]
    added = lax.all_to_all(spread, "tok", 0, 0, tiled=True)
    mlp_part, mixed = feed(added, embedded, mlp_gain[None], weights)
    mlp_rows = lax.all_to_all(mlp_part, "tok", 0, 0, tiled=True)
    own_rows = lax.optimization_barrier(lax.dynamic_slice_in_dim(mixed, member * own, own))
    hidden_out = (own_rows.astype(F32) + jnp.sum(mlp_rows.astype(F32), axis=0)).astype(BF)

    incoming = inverse_of(new_slot)
    local_targets = lax.dynamic_slice_in_dim(incoming, group_index * slots_dev, slots_dev)
    sources = jnp.take(current_slot, local_targets)
    chosen = chosen[:, 0]
    pair = jnp.concatenate([chosen, across(chosen)], axis=0)
    held = [pair] + [turn(pair, by) for by in range(1, chips)]
    source_group = sources // slots_dev
    turns = (group_index // cores - source_group // cores) % chips
    other_core = (source_group % cores) != (group_index % cores)
    rows = sources % slots_dev + jnp.where(other_core, slots_dev, 0)
    new_states = pick_states(turns, rows, held, slots_dev)[:, None]
    return (hidden_out, new_states)


def solution(mesh):
    return jax.shard_map(
        local,
        mesh=mesh,
        in_specs=(
            P(),
            P(),
            P(),
            P(),
            P(),
            P(("req", "tok"), None),
            P(),
            P(),
            P(),
            P("req", "tok", None),
            P("req", "tok", None),
            P(None, "tok"),
            P(None, "tok"),
            P(None, "tok"),
            P(),
            P(None, "tok"),
            P("tok"),
            P("tok"),
            P("tok"),
            P("req", "tok", None, None),
            P("tok", None),
            P(),
            P(None, ("req", "tok")),
            P(None, ("req", "tok")),
            P(None, ("req", "tok")),
        ),
        out_specs=(P(("req", "tok"), None), P("req", "tok", None, None)),
        check_vma=False,
    )
```

```python
import functools

import jax
import jax.numpy as jnp
from jax import lax
from jax.experimental import pallas as pl
from jax.experimental.pallas import tpu as pltpu
from jax.sharding import PartitionSpec as P

BF = jnp.bfloat16
F32 = jnp.float32
NEG = -1e30
AUX = 128


def inverse_of(mapping):
    places = jnp.arange(mapping.shape[0], dtype=jnp.int32)
    matches = mapping[None, :] == places[:, None]
    return jnp.sum(jnp.where(matches, places[None, :], 0), axis=1)


def dot_nn(a, b, precision=None):
    return lax.dot_general(
        a, b, (((1,), (0,)), ((), ())), precision=precision, preferred_element_type=F32
    )


def dot_nt(a, b, precision=None):
    return lax.dot_general(
        a, b, (((1,), (1,)), ((), ())), precision=precision, preferred_element_type=F32
    )


def dot_tn(a, b, precision=None):
    return lax.dot_general(
        a, b, (((0,), (0,)), ((), ())), precision=precision, preferred_element_type=F32
    )


HI = lax.Precision.HIGHEST


def cost(flops, moved, special=0):
    return pl.CostEstimate(flops=flops, bytes_accessed=moved, transcendentals=special)


def whole(shapes):
    return [pl.BlockSpec(a.shape, lambda i, n=len(a.shape): (0,) * n) for a in shapes]


def near(count):
    return [pl.BlockSpec(memory_space=pltpu.VMEM)] * count


def streamed(count):
    return [pl.BlockSpec(memory_space=pltpu.HBM)] * count


def scalars(count):
    return [pl.BlockSpec(memory_space=pltpu.SMEM)] * count


PARAMS = pltpu.CompilerParams(vmem_limit_bytes=60 << 20)
SMALL = pltpu.CompilerParams(vmem_limit_bytes=8 << 20)


def fetch_kernel(
    turn, slots_row, ids_cols, table_far, payload, places, origin, most, table, sem, *, groups, members
):
    load = pltpu.make_async_copy(table_far, table, sem)
    load.start()
    drafts, requests = ids_cols.shape
    vocab = table.shape[0]
    count = requests * drafts // groups
    slots = requests // groups
    group = lax.axis_index("req")
    member = lax.axis_index("tok")
    me = group * members + member
    now = turn[0]
    sub = lax.broadcasted_iota(jnp.int32, (count, count), 0)
    lane = lax.broadcasted_iota(jnp.int32, (count, count), 1)
    sub_c = sub[:, :1]
    lane_r = lane[:1, :]
    ids = ids_cols[...]
    ids_hi = (ids // 256).astype(F32).astype(BF)
    ids_lo = (ids % 256).astype(F32).astype(BF)
    row_slot = lax.broadcasted_iota(jnp.int32, (count, requests), 0) // drafts
    token = lax.broadcasted_iota(jnp.int32, (count, drafts), 0) % drafts
    token_lane = lax.broadcasted_iota(jnp.int32, (count, drafts), 1)
    column = lax.broadcasted_iota(jnp.int32, (members, count), 0)
    local_iota = lax.broadcasted_iota(jnp.int32, (members, vocab), 1)
    own = count // members
    hots = []
    own_place = jnp.zeros((count, 1), jnp.int32)
    own_from = [jnp.zeros((1, count), jnp.int32)] * own
    peak = jnp.zeros((1, count), jnp.int32)
    for g in range(groups):
        pick = jnp.where(slots_row[...] == row_slot + g * slots, 1.0, 0.0).astype(BF)
        mixed_ids = dot_nt(pick, ids_hi) * 256.0 + dot_nt(pick, ids_lo)
        id_c = jnp.sum(
            jnp.where(token == token_lane, mixed_ids, 0.0), axis=1, keepdims=True
        ).astype(jnp.int32)
        id_r = jnp.sum(jnp.where(sub == lane, id_c, 0), axis=0, keepdims=True)
        same = id_c == id_r
        first_c = jnp.min(jnp.where(same, lane, count), axis=1, keepdims=True)
        first_r = jnp.min(jnp.where(same, sub, count), axis=0, keepdims=True)
        owner_c = id_c // vocab
        owner_r = id_r // vocab
        alike = owner_c == owner_r
        before_r = (first_c == sub_c) & alike & (sub < first_r)
        less_r = (first_c == sub_c) & (owner_c < owner_r)
        nth_r = jnp.sum(jnp.where(before_r, 1, 0), axis=0, keepdims=True)
        rank_r = nth_r + jnp.sum(jnp.where(less_r, 1, 0), axis=0, keepdims=True)
        peak = jnp.maximum(peak, nth_r // members + 1)
        before_c = (first_r == lane_r) & alike & (lane < first_c)
        less_c = (first_r == lane_r) & (owner_r < owner_c)
        nth_c = jnp.sum(jnp.where(before_c, 1, 0), axis=1, keepdims=True)
        rank_c = nth_c + jnp.sum(jnp.where(less_c, 1, 0), axis=1, keepdims=True)
        spot = (rank_c % members) * own + rank_c // members
        spot = jnp.where(nth_c // members == now, spot, -1)
        own_place = jnp.where(group == g, spot, own_place)
        sent_r = (first_r == lane_r) & (nth_r // members == now)
        asked = sent_r & (owner_r == me) & (rank_r % members == column)
        row = jnp.sum(jnp.where(asked, id_r % vocab + 1, 0), axis=1, keepdims=True) - 1
        hots.append(jnp.where(local_iota == row, 1.0, 0.0))
        for k in range(own):
            here = sent_r & (rank_r == k * members + member) & (group == g)
            own_from[k] = own_from[k] + jnp.where(here, owner_r + 1, 0)
    places[...] = jnp.broadcast_to(own_place, places.shape)
    for k in range(own):
        origin[k] = jnp.sum(own_from[k]) - 1
    most[0] = jnp.max(peak)
    hot = jnp.concatenate(hots, axis=0).astype(BF)
    load.wait()
    payload[...] = dot_nn(hot, table[...]).reshape(payload.shape).astype(BF)


def fetch(turn, slots_row, ids_cols, table, groups, members):
    count = ids_cols.size // groups
    outs = [
        jax.ShapeDtypeStruct((groups * members, table.shape[1] // AUX, AUX), BF),
        jax.ShapeDtypeStruct((count, AUX), jnp.int32),
        jax.ShapeDtypeStruct((count // members,), jnp.int32),
        jax.ShapeDtypeStruct((1,), jnp.int32),
    ]
    return pl.pallas_call(
        functools.partial(fetch_kernel, groups=groups, members=members),
        grid=(1,),
        in_specs=scalars(1) + whole([slots_row, ids_cols]) + streamed(1),
        out_specs=whole(outs[:2]) + scalars(2),
        out_shape=outs,
        scratch_shapes=[pltpu.VMEM(table.shape, table.dtype), pltpu.SemaphoreType.DMA],
        compiler_params=PARAMS,
        cost_estimate=cost(2 * groups * members * table.size, 2 * table.size),
        name="fetch",
    )(turn, slots_row, ids_cols, table)


def hand_kernel(origin, came, spread):
    peers, own, lines = spread.shape[0], origin.shape[0], came.shape[1]
    for k in range(own):
        source = origin[k]
        row = came[jnp.maximum(source, 0)]
        row = jnp.where(source >= 0, row.astype(F32), 0.0).astype(BF)
        for j in range(peers):
            spread[j, k * lines : (k + 1) * lines, :] = row


def hand(origin, came, members):
    own = origin.shape[0]
    out = jax.ShapeDtypeStruct((members, own * came.shape[1], AUX), BF)
    return pl.pallas_call(
        hand_kernel,
        in_specs=scalars(1) + near(1),
        out_specs=near(1)[0],
        out_shape=out,
        compiler_params=SMALL,
        name="hand",
    )(origin, came)


def rows_of(arrived, places):
    count = places.shape[0]
    width = arrived.size // count
    slot = lax.broadcasted_iota(jnp.int32, (count, count), 1)
    hot = jnp.where(slot == places[:, :1], 1.0, 0.0).astype(BF)
    lines = arrived[...].astype(F32).reshape(count, width // AUX, AUX)
    return dot_nn(hot, lines.reshape(count, width).astype(BF))


def place_kernel(arrived, places, before, out):
    out[...] = (before[...].astype(F32) + rows_of(arrived, places)).astype(BF)


def place(arrived, places, before):
    return pl.pallas_call(
        place_kernel,
        grid=(1,),
        in_specs=whole([arrived, places, before]),
        out_specs=whole([before])[0],
        out_shape=jax.ShapeDtypeStruct(before.shape, BF),
        compiler_params=PARAMS,
        name="place",
    )(arrived, places, before)


def attend_kernel(
    ints,
    arrived,
    places,
    extra,
    gain,
    query_weight,
    keyvalue_weight,
    keys,
    values,
    payload,
    embedded,
    normed,
    query_in,
    keyvalue_in,
    keys_in,
    values_in,
    sems,
):
    moves = []
    third = query_weight.shape[0] // 3
    for k in range(3):
        span = pl.ds(k * third, third)
        moves.append((query_weight.at[span, :], query_in.at[span, :]))
    moves += [(keyvalue_weight, keyvalue_in), (keys, keys_in), (values, values_in)]
    copies = [pltpu.make_async_copy(a, b, sems.at[n]) for n, (a, b) in enumerate(moves)]
    for copy in copies:
        copy.start()
    slots, cache, size = keys.shape
    tokens = extra.shape[0]
    drafts = tokens // slots
    heads = query_weight.shape[1] // size
    own = payload.shape[1]
    rows_in = (rows_of(arrived, places) + extra[...].astype(F32)).astype(BF)
    embedded[...] = rows_in
    wide = rows_in.astype(F32)
    factor = lax.rsqrt(jnp.mean(wide * wide, axis=-1, keepdims=True) + 1e-05)
    rows_norm = (wide * factor * gain[...]).astype(BF)
    normed[...] = rows_norm
    queries = None
    for k in range(3):
        copies[k].wait()
        span = slice(k * third, (k + 1) * third)
        part = dot_nn(rows_norm[:, span], query_in[span, :])
        queries = part if queries is None else queries + part
    queries = queries.astype(BF)
    copies[3].wait()
    keyvalue = dot_nn(rows_norm, keyvalue_in[...]).astype(BF)
    copies[4].wait()
    copies[5].wait()
    member = ints[8]
    scale = size ** (-0.5)
    rows = heads * drafts
    position = lax.broadcasted_iota(jnp.int32, (rows, cache), 1) + member * cache
    token = lax.broadcasted_iota(jnp.int32, (rows, drafts), 0) % drafts
    other = lax.broadcasted_iota(jnp.int32, (rows, drafts), 1)
    seen = other <= jnp.where(member == 0, token, -1)
    lane = lax.broadcasted_iota(jnp.int32, (drafts, AUX), 1)
    for slot in range(slots):
        span = slice(slot * drafts, (slot + 1) * drafts)
        length = ints[slot]
        query = jnp.concatenate(
            [queries[span, h * size : (h + 1) * size] for h in range(heads)], axis=0
        )
        scores = dot_nt(query, keys_in[slot]) * scale
        scores = jnp.where(position < length, scores, NEG)
        draft_scores = dot_nt(query, keyvalue[span, :size]) * scale
        draft_scores = jnp.where(seen, draft_scores, NEG)
        top = jnp.maximum(
            jnp.max(scores, axis=-1, keepdims=True),
            jnp.max(draft_scores, axis=-1, keepdims=True),
        )
        probs = jnp.where(position < length, jnp.exp(scores - top), 0.0)
        draft_probs = jnp.where(seen, jnp.exp(draft_scores - top), 0.0)
        total = jnp.sum(probs, axis=-1, keepdims=True) + jnp.sum(
            draft_probs, axis=-1, keepdims=True
        )
        summed = dot_nn(probs.astype(BF), values_in[slot]) + dot_nn(
            draft_probs.astype(BF), keyvalue[span, size:]
        )
        top_a = top.astype(BF).astype(F32)
        top_b = (top - top_a).astype(BF).astype(F32)
        top_c = top - top_a - top_b
        total_a = total.astype(BF).astype(F32)
        total_b = total - total_a
        aux = jnp.zeros((drafts, AUX), F32)
        for k, piece in enumerate((top_a, top_b, top_c, total_a, total_b)):
            for h in range(heads):
                part = piece[h * drafts : (h + 1) * drafts]
                aux = jnp.where(lane == k * heads + h, part, aux)
        flat = jnp.concatenate(
            [summed[h * drafts : (h + 1) * drafts] for h in range(heads)] + [aux], axis=1
        ).astype(BF)
        for q in range(drafts // own):
            payload[slot * (drafts // own) + q] = flat[q * own : (q + 1) * own]


def attend(ints, arrived, places, extra, gain, query_weight, keyvalue_weight, keys, values):
    tokens, width = extra.shape
    members = arrived.shape[0]
    wide = query_weight.shape[1] + AUX
    far = (query_weight, keyvalue_weight, keys, values)
    outs = [
        jax.ShapeDtypeStruct((members, tokens // members, wide), BF),
        jax.ShapeDtypeStruct((tokens, width), BF),
        jax.ShapeDtypeStruct((tokens, width), BF),
    ]
    return pl.pallas_call(
        attend_kernel,
        grid=(1,),
        in_specs=scalars(1) + near(1) + whole([places, extra, gain]) + streamed(4),
        out_specs=whole(outs),
        out_shape=outs,
        scratch_shapes=[pltpu.VMEM(a.shape, a.dtype) for a in far]
        + [pltpu.SemaphoreType.DMA((6,))],
        compiler_params=PARAMS,
        cost_estimate=cost(
            2 * tokens * query_weight.size * 2, 2 * (query_weight.size + keys.size * 2), keys.size
        ),
        name="attend",
    )(ints, arrived, places, extra, gain, query_weight, keyvalue_weight, keys, values)


def fold(block):
    half = block.shape[0] // 2
    rest = jnp.concatenate([block[:half, AUX:], block[half:, AUX:]], axis=1)
    return jnp.concatenate([block[:, :AUX], rest], axis=0)


def unfold(block, tokens):
    half = AUX // 2
    rest = jnp.concatenate([block[tokens:, :half], block[tokens:, half:]], axis=0)
    return jnp.concatenate([block[:tokens], rest], axis=1)


def mamba_kernel(
    ints,
    reals,
    normed,
    input_weight,
    gate_weight,
    state_proj,
    step_row,
    states,
    mamba_out,
    blocks,
    chosen,
    proj_in,
    input_in,
    gate_in,
    states_in,
    out_in,
    sems,
):
    moves = (
        (state_proj, proj_in),
        (input_weight, input_in),
        (gate_weight, gate_in),
        (states, states_in),
        (mamba_out, out_in),
    )
    copies = [pltpu.make_async_copy(a, b, sems.at[n]) for n, (a, b) in enumerate(moves)]
    for copy in copies:
        copy.start()
    slots = states.shape[0]
    tokens = normed.shape[0]
    drafts = tokens // slots
    rows = normed[...]
    step_in = (
        jnp.sum(rows.astype(F32) * step_row[...].astype(F32), axis=1, keepdims=True) + reals[0]
    )
    sizes = jnp.maximum(step_in, 0.0) + jnp.log1p(jnp.exp(-jnp.abs(step_in)))
    copies[0].wait()
    both = dot_nn(rows, proj_in[...])
    copies[1].wait()
    x_all = dot_nn(rows, input_in[...])
    copies[2].wait()
    z_all = dot_nn(rows, gate_in[...])
    copies[3].wait()
    state_size = both.shape[1] // 2
    row = lax.broadcasted_iota(jnp.int32, (drafts, drafts), 0)
    col = lax.broadcasted_iota(jnp.int32, (drafts, drafts), 1)
    rows_in = lax.broadcasted_iota(jnp.int32, (drafts, 1), 0)
    gated = []
    for slot in range(slots):
        span = slice(slot * drafts, (slot + 1) * drafts)
        accept = ints[4 + slot]
        size_t = sizes[span]
        size_row = jnp.sum(jnp.where(row == col, size_t, 0.0), axis=0, keepdims=True)
        log_decay = -reals[1] * jnp.sum(
            jnp.where(col <= row, size_row, 0.0), axis=1, keepdims=True
        )
        log_row = jnp.sum(jnp.where(row == col, log_decay, 0.0), axis=0, keepdims=True)
        between = jnp.exp(jnp.where(col <= row, log_decay - log_row, NEG))
        state_in = both[span, :state_size]
        state_read = both[span, state_size:]
        x = x_all[span]
        z = z_all[span]
        inputs = size_t * x
        start = states_in[slot, 0]
        weights = dot_nt(state_read, state_in, HI) * between
        readout = dot_nn(weights, inputs, HI) + jnp.exp(log_decay) * dot_nt(
            state_read, start, HI
        )
        readout = readout + reals[2] * x
        last = jnp.sum(jnp.where(rows_in == accept - 1, log_decay, 0.0), axis=0, keepdims=True)
        remain = jnp.exp(jnp.where(rows_in < accept, last - log_decay, NEG))
        chosen[slot, 0] = (
            jnp.exp(last) * start + dot_tn(remain * inputs, state_in, HI)
        ).astype(BF)
        gated.append((readout * (z / (1.0 + jnp.exp(-z)))).astype(BF))
    copies[4].wait()
    part = dot_nn(jnp.concatenate(gated, axis=0), out_in[...])
    share = part.shape[1] // blocks.shape[0]
    for j in range(blocks.shape[0]):
        blocks[j] = fold(part[:, j * share : (j + 1) * share]).astype(BF)


def mamba(ints, reals, normed, input_weight, gate_weight, state_proj, step_row, states, mamba_out, members):
    tokens = normed.shape[0]
    share = mamba_out.shape[1] // members
    outs = [
        jax.ShapeDtypeStruct((members, tokens * share // AUX, AUX), BF),
        jax.ShapeDtypeStruct(states.shape, BF),
    ]
    far = (state_proj, input_weight, gate_weight, states, mamba_out)
    return pl.pallas_call(
        mamba_kernel,
        grid=(1,),
        in_specs=scalars(2)
        + whole([normed])
        + streamed(3)
        + whole([step_row])
        + streamed(2),
        out_specs=whole(outs),
        out_shape=outs,
        scratch_shapes=[pltpu.VMEM(a.shape, a.dtype) for a in far]
        + [pltpu.SemaphoreType.DMA((5,))],
        compiler_params=PARAMS,
        cost_estimate=cost(2 * tokens * state_proj.size * 2, 4 * state_proj.size, tokens * 4096),
        name="mamba",
    )(ints, reals, normed, input_weight, gate_weight, state_proj, step_row, states, mamba_out)


def join_kernel(parts, blocks, payload, *, heads, size):
    peers, tokens, _ = blocks.shape
    own = parts.shape[1]
    aux = parts[:, :, heads * size : heads * size + AUX].astype(F32)
    payload[:, :tokens, :] = blocks[...]
    for h in range(heads):
        get = lambda k: aux[:, :, k * heads + h : k * heads + h + 1]
        top = get(0) + get(1) + get(2)
        total = get(3) + get(4)
        factor = jnp.exp(top - jnp.max(top, axis=0, keepdims=True))
        norm = jnp.sum(factor * total, axis=0)
        value = parts[:, :, h * size : (h + 1) * size].astype(F32)
        summed = jnp.sum(factor * value, axis=0)
        piece = (summed / norm).astype(BF)
        for j in range(peers):
            payload[j, tokens + h * own : tokens + (h + 1) * own, :size] = piece


def join(parts, blocks, heads, size):
    members, tokens, share = blocks.shape
    own = parts.shape[1]
    out = jax.ShapeDtypeStruct((members, tokens + heads * own, share), BF)
    return pl.pallas_call(
        functools.partial(join_kernel, heads=heads, size=size),
        grid=(1,),
        in_specs=near(1) + whole([blocks]),
        out_specs=whole([out])[0],
        out_shape=out,
        compiler_params=PARAMS,
        name="join",
    )(parts, blocks)


def project_kernel(parts, out_weight, spread, *, heads, size):
    peers, packed, _ = spread.shape
    own = (parts.shape[1] - packed) // heads
    tokens = own * peers
    acc = unfold(jnp.sum(parts[:, :packed, :].astype(F32), axis=0), tokens)
    for h in range(heads):
        attended = jnp.concatenate(
            [parts[j, packed + h * own : packed + (h + 1) * own, :size] for j in range(peers)],
            axis=0,
        )
        acc = acc + dot_nt(attended, out_weight[:, h * size : (h + 1) * size])
    out = fold(acc).astype(BF)
    for j in range(peers):
        spread[j] = out


def project(parts, out_weight, packed, heads, size):
    members = parts.shape[0]
    out = jax.ShapeDtypeStruct((members, packed, AUX), BF)
    return pl.pallas_call(
        functools.partial(project_kernel, heads=heads, size=size),
        grid=(1,),
        in_specs=near(1) + whole([out_weight]),
        out_specs=whole([out])[0],
        out_shape=out,
        compiler_params=PARAMS,
        name="project",
    )(parts, out_weight)


def feed_kernel(spread, embedded, gain, *refs, count):
    weights = refs[:count]
    out, mixed, gates, ups, downs, sems = refs[count:]
    peers, own, width = out.shape
    tokens = embedded.shape[0]
    total = gates.shape[0]
    pieces = []
    begin = 0
    units = min(w.shape[0] for w in weights) // 3
    for w in weights:
        for first in range(0, w.shape[0], 3 * units):
            pieces.append((w, first, begin))
            begin += units
    copies = []
    for n, (w, first, at) in enumerate(pieces):
        trio = []
        for k, to in enumerate((gates, ups, downs)):
            copy = pltpu.make_async_copy(
                w.at[pl.ds(first + k * units, units), :], to.at[pl.ds(at, units), :], sems.at[n, k]
            )
            copy.start()
            trio.append(copy)
        copies.append((at + units, trio))
    added = jnp.concatenate([unfold(spread[j].astype(F32), tokens) for j in range(peers)], axis=1)
    rows = (embedded[...].astype(F32) + added).astype(BF)
    mixed[...] = rows
    wide = rows.astype(F32)
    factor = lax.rsqrt(jnp.mean(wide * wide, axis=-1, keepdims=True) + 1e-05)
    second = (wide * factor * gain[...]).astype(BF)
    chunk = 256
    waited = 0
    ready = 0
    acc = None
    for c in range(total // chunk):
        while ready < (c + 1) * chunk:
            ready, trio = copies[waited]
            for copy in trio:
                copy.wait()
            waited += 1
        span = slice(c * chunk, (c + 1) * chunk)
        gate = dot_nt(second, gates[span, :])
        up = dot_nt(second, ups[span, :])
        hidden = (gate / (1.0 + jnp.exp(-gate)) * up).astype(BF)
        part = dot_nn(hidden, downs[span, :])
        acc = part if acc is None else acc + part
    for j in range(peers):
        out[j] = acc[j * own : (j + 1) * own, :].astype(BF)


def feed(spread, embedded, gain, weights):
    members = spread.shape[0]
    tokens, width = embedded.shape
    units = sum(w.shape[0] for w in weights) // 3
    count = 3 * units // min(w.shape[0] for w in weights)
    outs = [
        jax.ShapeDtypeStruct((members, tokens // members, width), BF),
        jax.ShapeDtypeStruct((tokens, width), BF),
    ]
    return pl.pallas_call(
        functools.partial(feed_kernel, count=len(weights)),
        grid=(1,),
        in_specs=near(1) + whole([embedded, gain]) + streamed(len(weights)),
        out_specs=whole(outs),
        out_shape=outs,
        scratch_shapes=[pltpu.VMEM((units, width), BF)] * 3
        + [pltpu.SemaphoreType.DMA((count, 3))],
        compiler_params=PARAMS,
        cost_estimate=cost(6 * tokens * units * width, 6 * units * width),
        name="feed",
    )(spread, embedded, gain, *weights)


def pack_kernel(gate, up, down, ready, low, high):
    half = low.shape[0] // 3
    for k, part in enumerate((gate, up, down)):
        low[k * half : (k + 1) * half] = part[:half]
        high[k * half : (k + 1) * half] = part[half:]


def pack(gate, up, down, ready):
    units, width = gate.shape
    out = jax.ShapeDtypeStruct((3 * units // 2, width), gate.dtype)
    return pl.pallas_call(
        pack_kernel,
        grid=(1,),
        in_specs=whole([gate, up, down]) + streamed(1),
        out_specs=whole([out, out]),
        out_shape=[out, out],
        compiler_params=PARAMS,
        cost_estimate=cost(0, 1024),
        name="pack",
    )(gate, up, down, ready)


def pick_kernel(turns, rows, *refs):
    held = refs[:-1]
    out = refs[-1]
    for i in range(out.shape[0]):
        for n, ref in enumerate(held):

            @pl.when(turns[i] == n)
            def _():
                out[i] = ref[rows[i]].astype(F32)


def pick_states(turns, rows, held, count):
    shape = (count,) + held[0].shape[1:]
    out = jax.ShapeDtypeStruct(shape, F32)
    return pl.pallas_call(
        pick_kernel,
        grid=(1,),
        in_specs=scalars(2) + whole(held),
        out_specs=whole([out])[0],
        out_shape=out,
        compiler_params=PARAMS,
        name="pick",
    )(turns, rows, *held)


def local(
    draft_ids,
    lengths,
    current_slot,
    new_slot,
    accepted,
    embed_table,
    mixer_gain,
    query_weight,
    keyvalue_weight,
    key_cache,
    value_cache,
    attention_out,
    mamba_input,
    mamba_gate,
    state_proj,
    mamba_step,
    step_bias,
    decay_log,
    skip_gain,
    states,
    mamba_out,
    mlp_gain,
    gate_weight,
    up_weight,
    down_weight,
):
    members = lax.axis_size("tok")
    groups = lax.axis_size("req")
    group_index = lax.axis_index("req")
    member = lax.axis_index("tok")
    slots_dev, cache_dev, head_size = key_cache.shape
    draft_len = draft_ids.shape[1]
    width = embed_table.shape[1]
    query_heads = query_weight.shape[1] // head_size
    own = slots_dev * draft_len // members

    cores = 2
    chips = groups // cores

    def turn(value, by):
        return lax.ppermute(
            value, "req", [(g, (g + by * cores) % groups) for g in range(groups)]
        )

    def across(value):
        return lax.ppermute(value, "req", [(g, g ^ 1) for g in range(groups)])

    def exchange(turn):
        sent, places, origin, most = fetch(
            turn, current_slot[None], draft_ids.T, embed_table, groups, members
        )
        came = lax.all_to_all(sent, ("req", "tok"), 0, 0, tiled=True)
        return came, places, origin, most

    def plane(rows):
        return lax.all_to_all(rows, "tok", 0, 0, tiled=True)

    came, places, origin, most = exchange(jnp.zeros((1,), jnp.int32))

    low, high = pack(gate_weight.T, up_weight.T, down_weight.T, places)
    low, high, came = lax.optimization_barrier((low, high, came))
    handed = hand(origin, came, members)
    arrived = plane(handed)
    near_a = [turn(low, 1), turn(high, -1)]

    def more(carry):
        return carry[0][0] < most[0]

    def round_of(carry):
        at, rows = carry
        later, spots, froms, _ = exchange(at)
        return at + 1, place(plane(hand(froms, later, members)), spots, rows)

    _, extra = lax.while_loop(
        more, round_of, (jnp.ones((1,), jnp.int32), jnp.zeros((members * own, width), BF))
    )

    slot_owner = inverse_of(current_slot)
    local_owner = lax.dynamic_slice_in_dim(slot_owner, group_index * slots_dev, slots_dev)
    ints = jnp.concatenate(
        [jnp.take(lengths, local_owner), jnp.take(accepted, local_owner), member[None]]
    )
    reals = jnp.concatenate([step_bias, jnp.exp(decay_log), skip_gain])
    payload, embedded, normed = attend(
        ints,
        arrived,
        places,
        extra,
        mixer_gain[None],
        query_weight,
        keyvalue_weight,
        key_cache,
        value_cache,
    )
    parts = lax.all_to_all(payload, "tok", 0, 0, tiled=True)
    blocks, chosen = mamba(
        ints,
        reals,
        normed,
        mamba_input,
        mamba_gate,
        state_proj,
        mamba_step.T,
        states,
        mamba_out,
        members,
    )
    *near_a, chosen, _ = lax.optimization_barrier((*near_a, chosen, parts))
    weights = [low, high] + near_a
    far = [turn(near_a[0], 1), turn(near_a[1], -1), turn(high, 1), turn(low, -1)]
    weights += [across(w) for w in weights]
    joined = lax.all_to_all(join(parts, blocks, query_heads, head_size), "tok", 0, 0, tiled=True)
    spread = project(joined, attention_out.T, blocks.shape[1], query_heads, head_size)
    *far, _ = lax.optimization_barrier((*far, spread))
    weights += far + [across(w) for w in far]
    added = lax.all_to_all(spread, "tok", 0, 0, tiled=True)
    mlp_part, mixed = feed(added, embedded, mlp_gain[None], weights)
    mlp_rows = lax.all_to_all(mlp_part, "tok", 0, 0, tiled=True)
    own_rows = lax.optimization_barrier(lax.dynamic_slice_in_dim(mixed, member * own, own))
    hidden_out = (own_rows.astype(F32) + jnp.sum(mlp_rows.astype(F32), axis=0)).astype(BF)

    incoming = inverse_of(new_slot)
    local_targets = lax.dynamic_slice_in_dim(incoming, group_index * slots_dev, slots_dev)
    sources = jnp.take(current_slot, local_targets)
    chosen = chosen[:, 0]
    pair = jnp.concatenate([chosen, across(chosen)], axis=0)
    held = [pair] + [turn(pair, by) for by in range(1, chips)]
    source_group = sources // slots_dev
    turns = (group_index // cores - source_group // cores) % chips
    other_core = (source_group % cores) != (group_index % cores)
    rows = sources % slots_dev + jnp.where(other_core, slots_dev, 0)
    new_states = pick_states(turns, rows, held, slots_dev)[:, None]
    return (hidden_out, new_states)


def solution(mesh):
    return jax.shard_map(
        local,
        mesh=mesh,
        in_specs=(
            P(),
            P(),
            P(),
            P(),
            P(),
            P(("req", "tok"), None),
            P(),
            P(),
            P(),
            P("req", "tok", None),
            P("req", "tok", None),
            P(None, "tok"),
            P(None, "tok"),
            P(None, "tok"),
            P(),
            P(None, "tok"),
            P("tok"),
            P("tok"),
            P("tok"),
            P("req", "tok", None, None),
            P("tok", None),
            P(),
            P(None, ("req", "tok")),
            P(None, ("req", "tok")),
            P(None, ("req", "tok")),
        ),
        out_specs=(P(("req", "tok"), None), P("req", "tok", None, None)),
        check_vma=False,
    )
```

```python
import functools

import jax
import jax.numpy as jnp
from jax import lax
from jax.experimental import pallas as pl
from jax.experimental.pallas import tpu as pltpu
from jax.sharding import PartitionSpec as P

BF = jnp.bfloat16
F32 = jnp.float32
NEG = -1e30
AUX = 128


def inverse_of(mapping):
    places = jnp.arange(mapping.shape[0], dtype=jnp.int32)
    matches = mapping[None, :] == places[:, None]
    return jnp.sum(jnp.where(matches, places[None, :], 0), axis=1)


def dot_nn(a, b, precision=None):
    return lax.dot_general(
        a, b, (((1,), (0,)), ((), ())), precision=precision, preferred_element_type=F32
    )


def dot_nt(a, b, precision=None):
    return lax.dot_general(
        a, b, (((1,), (1,)), ((), ())), precision=precision, preferred_element_type=F32
    )


def dot_tn(a, b, precision=None):
    return lax.dot_general(
        a, b, (((0,), (0,)), ((), ())), precision=precision, preferred_element_type=F32
    )


HI = lax.Precision.HIGHEST


def cost(flops, moved, special=0):
    return pl.CostEstimate(flops=flops, bytes_accessed=moved, transcendentals=special)


def lasting(microseconds):
    return cost(int(microseconds * 1e9), 1024)


def whole(shapes):
    return [pl.BlockSpec(a.shape, lambda i, n=len(a.shape): (0,) * n) for a in shapes]


def near(count):
    return [pl.BlockSpec(memory_space=pltpu.VMEM)] * count


def streamed(count):
    return [pl.BlockSpec(memory_space=pltpu.HBM)] * count


def scalars(count):
    return [pl.BlockSpec(memory_space=pltpu.SMEM)] * count


PARAMS = pltpu.CompilerParams(vmem_limit_bytes=60 << 20)
SMALL = pltpu.CompilerParams(vmem_limit_bytes=8 << 20)


def fetch_kernel(
    turn, slots_row, ids_cols, table_far, payload, places, origin, most, table, sem, *, groups, members
):
    load = pltpu.make_async_copy(table_far, table, sem)
    load.start()
    drafts, requests = ids_cols.shape
    vocab = table.shape[0]
    count = requests * drafts // groups
    slots = requests // groups
    group = lax.axis_index("req")
    member = lax.axis_index("tok")
    me = group * members + member
    now = turn[0]
    sub = lax.broadcasted_iota(jnp.int32, (count, count), 0)
    lane = lax.broadcasted_iota(jnp.int32, (count, count), 1)
    sub_c = sub[:, :1]
    lane_r = lane[:1, :]
    ids = ids_cols[...]
    ids_hi = (ids // 256).astype(F32).astype(BF)
    ids_lo = (ids % 256).astype(F32).astype(BF)
    row_slot = lax.broadcasted_iota(jnp.int32, (count, requests), 0) // drafts
    token = lax.broadcasted_iota(jnp.int32, (count, drafts), 0) % drafts
    token_lane = lax.broadcasted_iota(jnp.int32, (count, drafts), 1)
    column = lax.broadcasted_iota(jnp.int32, (members, count), 0)
    local_iota = lax.broadcasted_iota(jnp.int32, (members, vocab), 1)
    own = count // members
    hots = []
    own_place = jnp.zeros((count, 1), jnp.int32)
    own_from = [jnp.zeros((1, count), jnp.int32)] * own
    peak = jnp.zeros((1, count), jnp.int32)
    for g in range(groups):
        pick = jnp.where(slots_row[...] == row_slot + g * slots, 1.0, 0.0).astype(BF)
        mixed_ids = dot_nt(pick, ids_hi) * 256.0 + dot_nt(pick, ids_lo)
        id_c = jnp.sum(
            jnp.where(token == token_lane, mixed_ids, 0.0), axis=1, keepdims=True
        ).astype(jnp.int32)
        id_r = jnp.sum(jnp.where(sub == lane, id_c, 0), axis=0, keepdims=True)
        same = id_c == id_r
        first_c = jnp.min(jnp.where(same, lane, count), axis=1, keepdims=True)
        first_r = jnp.min(jnp.where(same, sub, count), axis=0, keepdims=True)
        owner_c = id_c // vocab
        owner_r = id_r // vocab
        alike = owner_c == owner_r
        before_r = (first_c == sub_c) & alike & (sub < first_r)
        less_r = (first_c == sub_c) & (owner_c < owner_r)
        nth_r = jnp.sum(jnp.where(before_r, 1, 0), axis=0, keepdims=True)
        rank_r = nth_r + jnp.sum(jnp.where(less_r, 1, 0), axis=0, keepdims=True)
        peak = jnp.maximum(peak, nth_r // members + 1)
        before_c = (first_r == lane_r) & alike & (lane < first_c)
        less_c = (first_r == lane_r) & (owner_r < owner_c)
        nth_c = jnp.sum(jnp.where(before_c, 1, 0), axis=1, keepdims=True)
        rank_c = nth_c + jnp.sum(jnp.where(less_c, 1, 0), axis=1, keepdims=True)
        spot = (rank_c % members) * own + rank_c // members
        spot = jnp.where(nth_c // members == now, spot, -1)
        own_place = jnp.where(group == g, spot, own_place)
        sent_r = (first_r == lane_r) & (nth_r // members == now)
        asked = sent_r & (owner_r == me) & (rank_r % members == column)
        row = jnp.sum(jnp.where(asked, id_r % vocab + 1, 0), axis=1, keepdims=True) - 1
        hots.append(jnp.where(local_iota == row, 1.0, 0.0))
        for k in range(own):
            here = sent_r & (rank_r == k * members + member) & (group == g)
            own_from[k] = own_from[k] + jnp.where(here, owner_r + 1, 0)
    places[...] = jnp.broadcast_to(own_place, places.shape)
    for k in range(own):
        origin[k] = jnp.sum(own_from[k]) - 1
    most[0] = jnp.max(peak)
    hot = jnp.concatenate(hots, axis=0).astype(BF)
    load.wait()
    payload[...] = dot_nn(hot, table[...]).reshape(payload.shape).astype(BF)


def fetch(turn, slots_row, ids_cols, table, groups, members):
    count = ids_cols.size // groups
    outs = [
        jax.ShapeDtypeStruct((groups * members, table.shape[1] // AUX, AUX), BF),
        jax.ShapeDtypeStruct((count, AUX), jnp.int32),
        jax.ShapeDtypeStruct((count // members,), jnp.int32),
        jax.ShapeDtypeStruct((1,), jnp.int32),
    ]
    return pl.pallas_call(
        functools.partial(fetch_kernel, groups=groups, members=members),
        grid=(1,),
        in_specs=scalars(1) + whole([slots_row, ids_cols]) + streamed(1),
        out_specs=whole(outs[:2]) + scalars(2),
        out_shape=outs,
        scratch_shapes=[pltpu.VMEM(table.shape, table.dtype), pltpu.SemaphoreType.DMA],
        compiler_params=PARAMS,
        cost_estimate=cost(2 * groups * members * table.size, 2 * table.size),
        name="fetch",
    )(turn, slots_row, ids_cols, table)


def hand_kernel(origin, came, spread):
    peers, own, lines = spread.shape[0], origin.shape[0], came.shape[1]
    for k in range(own):
        source = origin[k]
        row = came[jnp.maximum(source, 0)]
        row = jnp.where(source >= 0, row.astype(F32), 0.0).astype(BF)
        for j in range(peers):
            spread[j, k * lines : (k + 1) * lines, :] = row


def hand(origin, came, members):
    own = origin.shape[0]
    out = jax.ShapeDtypeStruct((members, own * came.shape[1], AUX), BF)
    return pl.pallas_call(
        hand_kernel,
        in_specs=scalars(1) + near(1),
        out_specs=near(1)[0],
        out_shape=out,
        compiler_params=SMALL,
        cost_estimate=lasting(10),
        name="hand",
    )(origin, came)


def rows_of(arrived, places):
    count = places.shape[0]
    width = arrived.size // count
    slot = lax.broadcasted_iota(jnp.int32, (count, count), 1)
    hot = jnp.where(slot == places[:, :1], 1.0, 0.0).astype(BF)
    lines = arrived[...].astype(F32).reshape(count, width // AUX, AUX)
    return dot_nn(hot, lines.reshape(count, width).astype(BF))


def place_kernel(arrived, places, before, out):
    out[...] = (before[...].astype(F32) + rows_of(arrived, places)).astype(BF)


def place(arrived, places, before):
    return pl.pallas_call(
        place_kernel,
        grid=(1,),
        in_specs=whole([arrived, places, before]),
        out_specs=whole([before])[0],
        out_shape=jax.ShapeDtypeStruct(before.shape, BF),
        compiler_params=PARAMS,
        name="place",
    )(arrived, places, before)


def attend_kernel(
    ints,
    arrived,
    places,
    extra,
    gain,
    query_weight,
    keyvalue_weight,
    keys,
    values,
    payload,
    embedded,
    normed,
    query_in,
    keyvalue_in,
    keys_in,
    values_in,
    sems,
):
    moves = []
    third = query_weight.shape[0] // 3
    for k in range(3):
        span = pl.ds(k * third, third)
        moves.append((query_weight.at[span, :], query_in.at[span, :]))
    moves += [(keyvalue_weight, keyvalue_in), (keys, keys_in), (values, values_in)]
    copies = [pltpu.make_async_copy(a, b, sems.at[n]) for n, (a, b) in enumerate(moves)]
    for copy in copies:
        copy.start()
    slots, cache, size = keys.shape
    tokens = extra.shape[0]
    drafts = tokens // slots
    heads = query_weight.shape[1] // size
    own = payload.shape[1]
    rows_in = (rows_of(arrived, places) + extra[...].astype(F32)).astype(BF)
    embedded[...] = rows_in
    wide = rows_in.astype(F32)
    factor = lax.rsqrt(jnp.mean(wide * wide, axis=-1, keepdims=True) + 1e-05)
    rows_norm = (wide * factor * gain[...]).astype(BF)
    normed[...] = rows_norm
    queries = None
    for k in range(3):
        copies[k].wait()
        span = slice(k * third, (k + 1) * third)
        part = dot_nn(rows_norm[:, span], query_in[span, :])
        queries = part if queries is None else queries + part
    queries = queries.astype(BF)
    copies[3].wait()
    keyvalue = dot_nn(rows_norm, keyvalue_in[...]).astype(BF)
    copies[4].wait()
    copies[5].wait()
    member = ints[8]
    scale = size ** (-0.5)
    rows = heads * drafts
    position = lax.broadcasted_iota(jnp.int32, (rows, cache), 1) + member * cache
    token = lax.broadcasted_iota(jnp.int32, (rows, drafts), 0) % drafts
    other = lax.broadcasted_iota(jnp.int32, (rows, drafts), 1)
    seen = other <= jnp.where(member == 0, token, -1)
    lane = lax.broadcasted_iota(jnp.int32, (drafts, AUX), 1)
    for slot in range(slots):
        span = slice(slot * drafts, (slot + 1) * drafts)
        length = ints[slot]
        query = jnp.concatenate(
            [queries[span, h * size : (h + 1) * size] for h in range(heads)], axis=0
        )
        scores = dot_nt(query, keys_in[slot]) * scale
        scores = jnp.where(position < length, scores, NEG)
        draft_scores = dot_nt(query, keyvalue[span, :size]) * scale
        draft_scores = jnp.where(seen, draft_scores, NEG)
        top = jnp.maximum(
            jnp.max(scores, axis=-1, keepdims=True),
            jnp.max(draft_scores, axis=-1, keepdims=True),
        )
        probs = jnp.where(position < length, jnp.exp(scores - top), 0.0)
        draft_probs = jnp.where(seen, jnp.exp(draft_scores - top), 0.0)
        total = jnp.sum(probs, axis=-1, keepdims=True) + jnp.sum(
            draft_probs, axis=-1, keepdims=True
        )
        summed = dot_nn(probs.astype(BF), values_in[slot]) + dot_nn(
            draft_probs.astype(BF), keyvalue[span, size:]
        )
        top_a = top.astype(BF).astype(F32)
        top_b = (top - top_a).astype(BF).astype(F32)
        top_c = top - top_a - top_b
        total_a = total.astype(BF).astype(F32)
        total_b = total - total_a
        aux = jnp.zeros((drafts, AUX), F32)
        for k, piece in enumerate((top_a, top_b, top_c, total_a, total_b)):
            for h in range(heads):
                part = piece[h * drafts : (h + 1) * drafts]
                aux = jnp.where(lane == k * heads + h, part, aux)
        flat = jnp.concatenate(
            [summed[h * drafts : (h + 1) * drafts] for h in range(heads)] + [aux], axis=1
        ).astype(BF)
        for q in range(drafts // own):
            payload[slot * (drafts // own) + q] = flat[q * own : (q + 1) * own]


def attend(ints, arrived, places, extra, gain, query_weight, keyvalue_weight, keys, values):
    tokens, width = extra.shape
    members = arrived.shape[0]
    wide = query_weight.shape[1] + AUX
    far = (query_weight, keyvalue_weight, keys, values)
    outs = [
        jax.ShapeDtypeStruct((members, tokens // members, wide), BF),
        jax.ShapeDtypeStruct((tokens, width), BF),
        jax.ShapeDtypeStruct((tokens, width), BF),
    ]
    return pl.pallas_call(
        attend_kernel,
        grid=(1,),
        in_specs=scalars(1) + near(1) + whole([places, extra, gain]) + streamed(4),
        out_specs=whole(outs),
        out_shape=outs,
        scratch_shapes=[pltpu.VMEM(a.shape, a.dtype) for a in far]
        + [pltpu.SemaphoreType.DMA((6,))],
        compiler_params=PARAMS,
        cost_estimate=lasting(20),
        name="attend",
    )(ints, arrived, places, extra, gain, query_weight, keyvalue_weight, keys, values)


def fold(block):
    half = block.shape[0] // 2
    rest = jnp.concatenate([block[:half, AUX:], block[half:, AUX:]], axis=1)
    return jnp.concatenate([block[:, :AUX], rest], axis=0)


def unfold(block, tokens):
    half = AUX // 2
    rest = jnp.concatenate([block[tokens:, :half], block[tokens:, half:]], axis=0)
    return jnp.concatenate([block[:tokens], rest], axis=1)


def mamba_kernel(
    ints,
    reals,
    normed,
    input_weight,
    gate_weight,
    state_proj,
    step_row,
    states,
    mamba_out,
    blocks,
    chosen,
    proj_in,
    input_in,
    gate_in,
    states_in,
    out_in,
    sems,
):
    moves = (
        (state_proj, proj_in),
        (input_weight, input_in),
        (gate_weight, gate_in),
        (states, states_in),
        (mamba_out, out_in),
    )
    copies = [pltpu.make_async_copy(a, b, sems.at[n]) for n, (a, b) in enumerate(moves)]
    for copy in copies:
        copy.start()
    slots = states.shape[0]
    tokens = normed.shape[0]
    drafts = tokens // slots
    rows = normed[...]
    step_in = (
        jnp.sum(rows.astype(F32) * step_row[...].astype(F32), axis=1, keepdims=True) + reals[0]
    )
    sizes = jnp.maximum(step_in, 0.0) + jnp.log1p(jnp.exp(-jnp.abs(step_in)))
    copies[0].wait()
    both = dot_nn(rows, proj_in[...])
    copies[1].wait()
    x_all = dot_nn(rows, input_in[...])
    copies[2].wait()
    z_all = dot_nn(rows, gate_in[...])
    copies[3].wait()
    state_size = both.shape[1] // 2
    row = lax.broadcasted_iota(jnp.int32, (drafts, drafts), 0)
    col = lax.broadcasted_iota(jnp.int32, (drafts, drafts), 1)
    rows_in = lax.broadcasted_iota(jnp.int32, (drafts, 1), 0)
    gated = []
    for slot in range(slots):
        span = slice(slot * drafts, (slot + 1) * drafts)
        accept = ints[4 + slot]
        size_t = sizes[span]
        size_row = jnp.sum(jnp.where(row == col, size_t, 0.0), axis=0, keepdims=True)
        log_decay = -reals[1] * jnp.sum(
            jnp.where(col <= row, size_row, 0.0), axis=1, keepdims=True
        )
        log_row = jnp.sum(jnp.where(row == col, log_decay, 0.0), axis=0, keepdims=True)
        between = jnp.exp(jnp.where(col <= row, log_decay - log_row, NEG))
        state_in = both[span, :state_size]
        state_read = both[span, state_size:]
        x = x_all[span]
        z = z_all[span]
        inputs = size_t * x
        start = states_in[slot, 0]
        weights = dot_nt(state_read, state_in, HI) * between
        readout = dot_nn(weights, inputs, HI) + jnp.exp(log_decay) * dot_nt(
            state_read, start, HI
        )
        readout = readout + reals[2] * x
        last = jnp.sum(jnp.where(rows_in == accept - 1, log_decay, 0.0), axis=0, keepdims=True)
        remain = jnp.exp(jnp.where(rows_in < accept, last - log_decay, NEG))
        chosen[slot, 0] = (
            jnp.exp(last) * start + dot_tn(remain * inputs, state_in, HI)
        ).astype(BF)
        gated.append((readout * (z / (1.0 + jnp.exp(-z)))).astype(BF))
    copies[4].wait()
    part = dot_nn(jnp.concatenate(gated, axis=0), out_in[...])
    share = part.shape[1] // blocks.shape[0]
    for j in range(blocks.shape[0]):
        block = fold(part[:, j * share : (j + 1) * share]).astype(BF)
        blocks[j, : block.shape[0]] = block
        blocks[j, block.shape[0] :] = jnp.zeros_like(blocks[j, block.shape[0] :])


def mamba(
    ints,
    reals,
    normed,
    input_weight,
    gate_weight,
    state_proj,
    step_row,
    states,
    mamba_out,
    members,
    room,
):
    tokens = normed.shape[0]
    share = mamba_out.shape[1] // members
    outs = [
        jax.ShapeDtypeStruct((members, tokens * share // AUX + room, AUX), BF),
        jax.ShapeDtypeStruct(states.shape, BF),
    ]
    far = (state_proj, input_weight, gate_weight, states, mamba_out)
    return pl.pallas_call(
        mamba_kernel,
        grid=(1,),
        in_specs=scalars(2)
        + whole([normed])
        + streamed(3)
        + whole([step_row])
        + streamed(2),
        out_specs=whole(outs),
        out_shape=outs,
        scratch_shapes=[pltpu.VMEM(a.shape, a.dtype) for a in far]
        + [pltpu.SemaphoreType.DMA((5,))],
        compiler_params=PARAMS,
        cost_estimate=lasting(8),
        name="mamba",
    )(ints, reals, normed, input_weight, gate_weight, state_proj, step_row, states, mamba_out)


def join_kernel(parts, blocks, payload, piece, sem, *, heads, size):
    peers, own, _ = parts.shape
    rows = heads * own
    aux = parts[:, :, heads * size : heads * size + AUX].astype(F32)
    for h in range(heads):
        get = lambda k: aux[:, :, k * heads + h : k * heads + h + 1]
        top = get(0) + get(1) + get(2)
        total = get(3) + get(4)
        factor = jnp.exp(top - jnp.max(top, axis=0, keepdims=True))
        norm = jnp.sum(factor * total, axis=0)
        value = parts[:, :, h * size : (h + 1) * size].astype(F32)
        summed = jnp.sum(factor * value, axis=0)
        piece[h * own : (h + 1) * own, :] = (summed / norm).astype(BF)
    first = payload.shape[1] - rows
    copies = [
        pltpu.make_async_copy(piece, payload.at[j, pl.ds(first, rows), :], sem.at[j])
        for j in range(peers)
    ]
    for copy in copies:
        copy.start()
    for copy in copies:
        copy.wait()


def join(parts, blocks, heads, size):
    peers, own, _ = parts.shape
    return pl.pallas_call(
        functools.partial(join_kernel, heads=heads, size=size),
        grid=(1,),
        in_specs=near(1) + streamed(1),
        out_specs=streamed(1)[0],
        out_shape=jax.ShapeDtypeStruct(blocks.shape, BF),
        input_output_aliases={1: 0},
        scratch_shapes=[
            pltpu.VMEM((heads * own, size), BF),
            pltpu.SemaphoreType.DMA((peers,)),
        ],
        compiler_params=PARAMS,
        cost_estimate=lasting(20),
        name="join",
    )(parts, blocks)


def project_kernel(parts, out_weight, spread, *, heads, size):
    peers, packed, _ = spread.shape
    own = (parts.shape[1] - packed) // heads
    tokens = own * peers
    acc = unfold(jnp.sum(parts[:, :packed, :].astype(F32), axis=0), tokens)
    for h in range(heads):
        attended = jnp.concatenate(
            [parts[j, packed + h * own : packed + (h + 1) * own, :size] for j in range(peers)],
            axis=0,
        )
        acc = acc + dot_nt(attended, out_weight[:, h * size : (h + 1) * size])
    out = fold(acc).astype(BF)
    for j in range(peers):
        spread[j] = out


def project(parts, out_weight, packed, heads, size):
    members = parts.shape[0]
    out = jax.ShapeDtypeStruct((members, packed, AUX), BF)
    return pl.pallas_call(
        functools.partial(project_kernel, heads=heads, size=size),
        grid=(1,),
        in_specs=near(1) + whole([out_weight]),
        out_specs=whole([out])[0],
        out_shape=out,
        compiler_params=PARAMS,
        cost_estimate=lasting(20),
        name="project",
    )(parts, out_weight)


def load_units(weights, gates, ups, downs, sems, units):
    copies = []
    begin = 0
    for w in weights:
        for first in range(0, w.shape[0], 3 * units):
            trio = []
            for k, to in enumerate((gates, ups, downs)):
                copy = pltpu.make_async_copy(
                    w.at[pl.ds(first + k * units, units), :],
                    to.at[pl.ds(begin, units), :],
                    sems.at[len(copies), k],
                )
                copy.start()
                trio.append(copy)
            begin += units
            copies.append((begin, trio))
    return copies


def use_units(second, copies, gates, ups, downs, acc, chunk=192):
    ready = 0
    waiting = list(copies)
    for first in range(0, gates.shape[0], chunk):
        while ready < first + chunk:
            ready, trio = waiting.pop(0)
            for copy in trio:
                copy.wait()
        span = slice(first, first + chunk)
        gate = dot_nt(second, gates[span, :])
        up = dot_nt(second, ups[span, :])
        hidden = (gate / (1.0 + jnp.exp(-gate)) * up).astype(BF)
        part = dot_nn(hidden, downs[span, :])
        acc = part if acc is None else acc + part
    return acc


def feed_kernel(spread, embedded, gain, *refs, count, units):
    weights = refs[:count]
    acc, second, mixed, gates, ups, downs, sems = refs[count:]
    copies = load_units(weights, gates, ups, downs, sems, units)
    tokens = embedded.shape[0]
    peers = spread.shape[0]
    added = jnp.concatenate([unfold(spread[j].astype(F32), tokens) for j in range(peers)], axis=1)
    rows = (embedded[...].astype(F32) + added).astype(BF)
    mixed[...] = rows
    wide = rows.astype(F32)
    factor = lax.rsqrt(jnp.mean(wide * wide, axis=-1, keepdims=True) + 1e-05)
    rows_norm = (wide * factor * gain[...]).astype(BF)
    second[...] = rows_norm
    acc[...] = use_units(rows_norm, copies, gates, ups, downs, None)


def rest_kernel(so_far, second, *refs, count, units):
    weights = refs[:count]
    out, gates, ups, downs, sems = refs[count:]
    copies = load_units(weights, gates, ups, downs, sems, units)
    peers, own, _ = out.shape
    acc = use_units(second[...], copies, gates, ups, downs, so_far[...])
    for j in range(peers):
        out[j] = acc[j * own : (j + 1) * own, :].astype(BF)


def unit_scratch(weights, units):
    width = weights[0].shape[1]
    rows = sum(w.shape[0] for w in weights)
    count = rows // (3 * units)
    return [pltpu.VMEM((rows // 3, width), BF)] * 3 + [pltpu.SemaphoreType.DMA((count, 3))]


def feed(spread, embedded, gain, weights, units):
    outs = [
        jax.ShapeDtypeStruct(embedded.shape, F32),
        jax.ShapeDtypeStruct(embedded.shape, BF),
        jax.ShapeDtypeStruct(embedded.shape, BF),
    ]
    return pl.pallas_call(
        functools.partial(feed_kernel, count=len(weights), units=units),
        grid=(1,),
        in_specs=near(1) + whole([embedded, gain]) + streamed(len(weights)),
        out_specs=whole(outs),
        out_shape=outs,
        scratch_shapes=unit_scratch(weights, units),
        compiler_params=PARAMS,
        cost_estimate=lasting(20),
        name="feed",
    )(spread, embedded, gain, *weights)


def feed_rest(acc, second, weights, units, members):
    tokens, width = acc.shape
    out = jax.ShapeDtypeStruct((members, tokens // members, width), BF)
    return pl.pallas_call(
        functools.partial(rest_kernel, count=len(weights), units=units),
        grid=(1,),
        in_specs=whole([acc, second]) + streamed(len(weights)),
        out_specs=whole([out])[0],
        out_shape=out,
        scratch_shapes=unit_scratch(weights, units),
        compiler_params=PARAMS,
        cost_estimate=lasting(4),
        name="feed_rest",
    )(acc, second, *weights)


def pack_kernel(gate, up, down, ready, out):
    half = gate.shape[0] // 2
    for h in range(2):
        for k, part in enumerate((gate, up, down)):
            at = (3 * h + k) * half
            out[at : at + half] = part[h * half : (h + 1) * half]


def pack(gate, up, down, ready):
    units, width = gate.shape
    out = jax.ShapeDtypeStruct((3 * units, width), gate.dtype)
    return pl.pallas_call(
        pack_kernel,
        grid=(1,),
        in_specs=whole([gate, up, down]) + streamed(1),
        out_specs=whole([out])[0],
        out_shape=out,
        compiler_params=PARAMS,
        cost_estimate=cost(0, 1024),
        name="pack",
    )(gate, up, down, ready)


def split_kernel(below, above, beside, ready, low, high):
    low[...] = below[...]
    high[...] = above[...]


def split(below, above, beside, ready):
    rows, width = below.shape
    out = jax.ShapeDtypeStruct((rows // 2, width), below.dtype)
    block = lambda n: pl.BlockSpec(out.shape, lambda i: (n, 0))
    return pl.pallas_call(
        split_kernel,
        grid=(1,),
        in_specs=[block(0), block(1)] + streamed(2),
        out_specs=[block(0), block(0)],
        out_shape=[out, out],
        compiler_params=PARAMS,
        cost_estimate=cost(0, 1024),
        name="split",
    )(below, above, beside, ready)


def pick_kernel(turns, rows, *refs):
    held = refs[:-1]
    out = refs[-1]
    for i in range(out.shape[0]):
        for n, ref in enumerate(held):

            @pl.when(turns[i] == n)
            def _():
                out[i] = ref[rows[i]].astype(F32)


def pick_states(turns, rows, held, count):
    shape = (count,) + held[0].shape[1:]
    out = jax.ShapeDtypeStruct(shape, F32)
    return pl.pallas_call(
        pick_kernel,
        grid=(1,),
        in_specs=scalars(2) + whole(held),
        out_specs=whole([out])[0],
        out_shape=out,
        compiler_params=PARAMS,
        name="pick",
    )(turns, rows, *held)


def local(
    draft_ids,
    lengths,
    current_slot,
    new_slot,
    accepted,
    embed_table,
    mixer_gain,
    query_weight,
    keyvalue_weight,
    key_cache,
    value_cache,
    attention_out,
    mamba_input,
    mamba_gate,
    state_proj,
    mamba_step,
    step_bias,
    decay_log,
    skip_gain,
    states,
    mamba_out,
    mlp_gain,
    gate_weight,
    up_weight,
    down_weight,
):
    members = lax.axis_size("tok")
    groups = lax.axis_size("req")
    group_index = lax.axis_index("req")
    member = lax.axis_index("tok")
    slots_dev, cache_dev, head_size = key_cache.shape
    draft_len = draft_ids.shape[1]
    width = embed_table.shape[1]
    query_heads = query_weight.shape[1] // head_size
    own = slots_dev * draft_len // members

    cores = 2
    chips = groups // cores

    def turn(value, by):
        return lax.ppermute(
            value, "req", [(g, (g + by * cores) % groups) for g in range(groups)]
        )

    def across(value):
        return lax.ppermute(value, "req", [(g, g ^ 1) for g in range(groups)])

    def exchange(turn):
        sent, places, origin, most = fetch(
            turn, current_slot[None], draft_ids.T, embed_table, groups, members
        )
        came = lax.all_to_all(sent, ("req", "tok"), 0, 0, tiled=True)
        return came, places, origin, most

    def plane(rows):
        return lax.all_to_all(rows, "tok", 0, 0, tiled=True)

    came, places, origin, most = exchange(jnp.zeros((1,), jnp.int32))

    block = pack(gate_weight.T, up_weight.T, down_weight.T, places)
    below, above = turn(block, 1), turn(block, -1)
    arrived = plane(hand(origin, came, members))

    def more(carry):
        return carry[0][0] < most[0]

    def round_of(carry):
        at, rows = carry
        later, spots, froms, _ = exchange(at)
        return at + 1, place(plane(hand(froms, later, members)), spots, rows)

    _, extra = lax.while_loop(
        more, round_of, (jnp.ones((1,), jnp.int32), jnp.zeros((members * own, width), BF))
    )

    slot_owner = inverse_of(current_slot)
    local_owner = lax.dynamic_slice_in_dim(slot_owner, group_index * slots_dev, slots_dev)
    ints = jnp.concatenate(
        [jnp.take(lengths, local_owner), jnp.take(accepted, local_owner), member[None]]
    )
    reals = jnp.concatenate([step_bias, jnp.exp(decay_log), skip_gain])
    payload, embedded, normed = attend(
        ints,
        arrived,
        places,
        extra,
        mixer_gain[None],
        query_weight,
        keyvalue_weight,
        key_cache,
        value_cache,
    )
    parts = lax.all_to_all(payload, "tok", 0, 0, tiled=True)
    beside = across(block)
    low, high = split(below, above, beside, payload)
    far = [turn(low, 1), turn(high, -1)]
    weights = [block, beside, below, above]
    blocks, chosen = mamba(
        ints,
        reals,
        normed,
        mamba_input,
        mamba_gate,
        state_proj,
        mamba_step.T,
        states,
        mamba_out,
        members,
        query_heads * own,
    )
    blocks, *_ = lax.optimization_barrier((blocks, low, high))
    joint = join(parts, blocks, query_heads, head_size)
    joined = lax.all_to_all(joint, "tok", 0, 0, tiled=True)
    below, above, chosen, _ = lax.optimization_barrier((below, above, chosen, joint))
    weights += [across(below), across(above)]
    folded = members * own * (width // members) // AUX
    spread = project(joined, attention_out.T, folded, query_heads, head_size)
    *far, _ = lax.optimization_barrier((*far, spread))
    half = gate_weight.shape[1] // 2
    last = far + [across(w) for w in far]
    added = lax.all_to_all(spread, "tok", 0, 0, tiled=True)
    acc, second, mixed = feed(added, embedded, mlp_gain[None], weights, half)
    mlp_part = feed_rest(acc, second, last, half, members)
    mlp_rows = lax.all_to_all(mlp_part, "tok", 0, 0, tiled=True)
    own_rows = lax.optimization_barrier(lax.dynamic_slice_in_dim(mixed, member * own, own))
    hidden_out = (own_rows.astype(F32) + jnp.sum(mlp_rows.astype(F32), axis=0)).astype(BF)

    incoming = inverse_of(new_slot)
    local_targets = lax.dynamic_slice_in_dim(incoming, group_index * slots_dev, slots_dev)
    sources = jnp.take(current_slot, local_targets)
    chosen = chosen[:, 0]
    pair = jnp.concatenate([chosen, across(chosen)], axis=0)
    held = [pair] + [turn(pair, by) for by in range(1, chips)]
    source_group = sources // slots_dev
    turns = (group_index // cores - source_group // cores) % chips
    other_core = (source_group % cores) != (group_index % cores)
    rows = sources % slots_dev + jnp.where(other_core, slots_dev, 0)
    new_states = pick_states(turns, rows, held, slots_dev)[:, None]
    return (hidden_out, new_states)


def solution(mesh):
    return jax.shard_map(
        local,
        mesh=mesh,
        in_specs=(
            P(),
            P(),
            P(),
            P(),
            P(),
            P(("req", "tok"), None),
            P(),
            P(),
            P(),
            P("req", "tok", None),
            P("req", "tok", None),
            P(None, "tok"),
            P(None, "tok"),
            P(None, "tok"),
            P(),
            P(None, "tok"),
            P("tok"),
            P("tok"),
            P("tok"),
            P("req", "tok", None, None),
            P("tok", None),
            P(),
            P(None, ("req", "tok")),
            P(None, ("req", "tok")),
            P(None, ("req", "tok")),
        ),
        out_specs=(P(("req", "tok"), None), P("req", "tok", None, None)),
        check_vma=False,
    )
```

```python
import functools

import jax
import jax.numpy as jnp
from jax import lax
from jax.experimental import pallas as pl
from jax.experimental.pallas import tpu as pltpu
from jax.sharding import PartitionSpec as P

BF = jnp.bfloat16
F32 = jnp.float32
NEG = -1e30
AUX = 128


def inverse_of(mapping):
    places = jnp.arange(mapping.shape[0], dtype=jnp.int32)
    matches = mapping[None, :] == places[:, None]
    return jnp.sum(jnp.where(matches, places[None, :], 0), axis=1)


def dot_nn(a, b, precision=None):
    return lax.dot_general(
        a, b, (((1,), (0,)), ((), ())), precision=precision, preferred_element_type=F32
    )


def dot_nt(a, b, precision=None):
    return lax.dot_general(
        a, b, (((1,), (1,)), ((), ())), precision=precision, preferred_element_type=F32
    )


def dot_tn(a, b, precision=None):
    return lax.dot_general(
        a, b, (((0,), (0,)), ((), ())), precision=precision, preferred_element_type=F32
    )


HI = lax.Precision.HIGHEST


def cost(flops, moved, special=0):
    return pl.CostEstimate(flops=flops, bytes_accessed=moved, transcendentals=special)


def lasting(microseconds):
    return cost(int(microseconds * 1e9), 1024)


def whole(shapes):
    return [pl.BlockSpec(a.shape, lambda i, n=len(a.shape): (0,) * n) for a in shapes]


def near(count):
    return [pl.BlockSpec(memory_space=pltpu.VMEM)] * count


def streamed(count):
    return [pl.BlockSpec(memory_space=pltpu.HBM)] * count


def scalars(count):
    return [pl.BlockSpec(memory_space=pltpu.SMEM)] * count


PARAMS = pltpu.CompilerParams(vmem_limit_bytes=60 << 20)
SMALL = pltpu.CompilerParams(vmem_limit_bytes=8 << 20)


def fetch_kernel(
    turn, slots_row, ids_cols, table_far, payload, places, origin, most, table, sem, *, groups, members
):
    load = pltpu.make_async_copy(table_far, table, sem)
    load.start()
    drafts, requests = ids_cols.shape
    vocab = table.shape[0]
    count = requests * drafts // groups
    slots = requests // groups
    group = lax.axis_index("req")
    member = lax.axis_index("tok")
    me = group * members + member
    now = turn[0]
    sub = lax.broadcasted_iota(jnp.int32, (count, count), 0)
    lane = lax.broadcasted_iota(jnp.int32, (count, count), 1)
    sub_c = sub[:, :1]
    lane_r = lane[:1, :]
    ids = ids_cols[...]
    ids_hi = (ids // 256).astype(F32).astype(BF)
    ids_lo = (ids % 256).astype(F32).astype(BF)
    row_slot = lax.broadcasted_iota(jnp.int32, (count, requests), 0) // drafts
    token = lax.broadcasted_iota(jnp.int32, (count, drafts), 0) % drafts
    token_lane = lax.broadcasted_iota(jnp.int32, (count, drafts), 1)
    column = lax.broadcasted_iota(jnp.int32, (members, count), 0)
    local_iota = lax.broadcasted_iota(jnp.int32, (members, vocab), 1)
    own = count // members
    hots = []
    own_place = jnp.zeros((count, 1), jnp.int32)
    own_from = [jnp.zeros((1, count), jnp.int32)] * own
    peak = jnp.zeros((1, count), jnp.int32)
    for g in range(groups):
        pick = jnp.where(slots_row[...] == row_slot + g * slots, 1.0, 0.0).astype(BF)
        mixed_ids = dot_nt(pick, ids_hi) * 256.0 + dot_nt(pick, ids_lo)
        id_c = jnp.sum(
            jnp.where(token == token_lane, mixed_ids, 0.0), axis=1, keepdims=True
        ).astype(jnp.int32)
        id_r = jnp.sum(jnp.where(sub == lane, id_c, 0), axis=0, keepdims=True)
        same = id_c == id_r
        first_c = jnp.min(jnp.where(same, lane, count), axis=1, keepdims=True)
        first_r = jnp.min(jnp.where(same, sub, count), axis=0, keepdims=True)
        owner_c = id_c // vocab
        owner_r = id_r // vocab
        alike = owner_c == owner_r
        before_r = (first_c == sub_c) & alike & (sub < first_r)
        less_r = (first_c == sub_c) & (owner_c < owner_r)
        nth_r = jnp.sum(jnp.where(before_r, 1, 0), axis=0, keepdims=True)
        rank_r = nth_r + jnp.sum(jnp.where(less_r, 1, 0), axis=0, keepdims=True)
        peak = jnp.maximum(peak, nth_r // members + 1)
        before_c = (first_r == lane_r) & alike & (lane < first_c)
        less_c = (first_r == lane_r) & (owner_r < owner_c)
        nth_c = jnp.sum(jnp.where(before_c, 1, 0), axis=1, keepdims=True)
        rank_c = nth_c + jnp.sum(jnp.where(less_c, 1, 0), axis=1, keepdims=True)
        spot = (rank_c % members) * own + rank_c // members
        spot = jnp.where(nth_c // members == now, spot, -1)
        own_place = jnp.where(group == g, spot, own_place)
        sent_r = (first_r == lane_r) & (nth_r // members == now)
        asked = sent_r & (owner_r == me) & (rank_r % members == column)
        row = jnp.sum(jnp.where(asked, id_r % vocab + 1, 0), axis=1, keepdims=True) - 1
        hots.append(jnp.where(local_iota == row, 1.0, 0.0))
        for k in range(own):
            here = sent_r & (rank_r == k * members + member) & (group == g)
            own_from[k] = own_from[k] + jnp.where(here, owner_r + 1, 0)
    places[...] = jnp.broadcast_to(own_place, places.shape)
    for k in range(own):
        origin[k] = jnp.sum(own_from[k]) - 1
    most[0] = jnp.max(peak)
    hot = jnp.concatenate(hots, axis=0).astype(BF)
    load.wait()
    payload[...] = dot_nn(hot, table[...]).reshape(payload.shape).astype(BF)


def fetch(turn, slots_row, ids_cols, table, groups, members):
    count = ids_cols.size // groups
    outs = [
        jax.ShapeDtypeStruct((groups * members, table.shape[1] // AUX, AUX), BF),
        jax.ShapeDtypeStruct((count, AUX), jnp.int32),
        jax.ShapeDtypeStruct((count // members,), jnp.int32),
        jax.ShapeDtypeStruct((1,), jnp.int32),
    ]
    return pl.pallas_call(
        functools.partial(fetch_kernel, groups=groups, members=members),
        grid=(1,),
        in_specs=scalars(1) + whole([slots_row, ids_cols]) + streamed(1),
        out_specs=whole(outs[:2]) + scalars(2),
        out_shape=outs,
        scratch_shapes=[pltpu.VMEM(table.shape, table.dtype), pltpu.SemaphoreType.DMA],
        compiler_params=PARAMS,
        cost_estimate=cost(2 * groups * members * table.size, 2 * table.size),
        name="fetch",
    )(turn, slots_row, ids_cols, table)


def hand_kernel(origin, came, spread):
    peers, own, lines = spread.shape[0], origin.shape[0], came.shape[1]
    for k in range(own):
        source = origin[k]
        row = came[jnp.maximum(source, 0)]
        row = jnp.where(source >= 0, row.astype(F32), 0.0).astype(BF)
        for j in range(peers):
            spread[j, k * lines : (k + 1) * lines, :] = row


def hand(origin, came, members):
    own = origin.shape[0]
    out = jax.ShapeDtypeStruct((members, own * came.shape[1], AUX), BF)
    return pl.pallas_call(
        hand_kernel,
        in_specs=scalars(1) + near(1),
        out_specs=near(1)[0],
        out_shape=out,
        compiler_params=SMALL,
        cost_estimate=lasting(10),
        name="hand",
    )(origin, came)


def rows_of(arrived, places):
    count = places.shape[0]
    width = arrived.size // count
    slot = lax.broadcasted_iota(jnp.int32, (count, count), 1)
    hot = jnp.where(slot == places[:, :1], 1.0, 0.0).astype(BF)
    lines = arrived[...].astype(F32).reshape(count, width // AUX, AUX)
    return dot_nn(hot, lines.reshape(count, width).astype(BF))


def place_kernel(arrived, places, before, out):
    out[...] = (before[...].astype(F32) + rows_of(arrived, places)).astype(BF)


def place(arrived, places, before):
    return pl.pallas_call(
        place_kernel,
        grid=(1,),
        in_specs=whole([arrived, places, before]),
        out_specs=whole([before])[0],
        out_shape=jax.ShapeDtypeStruct(before.shape, BF),
        compiler_params=PARAMS,
        name="place",
    )(arrived, places, before)


def attend_kernel(
    ints,
    arrived,
    places,
    extra,
    gain,
    query_weight,
    keyvalue_weight,
    keys,
    values,
    payload,
    embedded,
    normed,
    query_in,
    keyvalue_in,
    keys_in,
    values_in,
    sems,
):
    moves = []
    third = query_weight.shape[0] // 3
    for k in range(3):
        span = pl.ds(k * third, third)
        moves.append((query_weight.at[span, :], query_in.at[span, :]))
    moves += [(keyvalue_weight, keyvalue_in), (keys, keys_in), (values, values_in)]
    copies = [pltpu.make_async_copy(a, b, sems.at[n]) for n, (a, b) in enumerate(moves)]
    for copy in copies:
        copy.start()
    slots, cache, size = keys.shape
    tokens = extra.shape[0]
    drafts = tokens // slots
    heads = query_weight.shape[1] // size
    own = payload.shape[1]
    rows_in = (rows_of(arrived, places) + extra[...].astype(F32)).astype(BF)
    embedded[...] = rows_in
    wide = rows_in.astype(F32)
    factor = lax.rsqrt(jnp.mean(wide * wide, axis=-1, keepdims=True) + 1e-05)
    rows_norm = (wide * factor * gain[...]).astype(BF)
    normed[...] = rows_norm
    queries = None
    for k in range(3):
        copies[k].wait()
        span = slice(k * third, (k + 1) * third)
        part = dot_nn(rows_norm[:, span], query_in[span, :])
        queries = part if queries is None else queries + part
    queries = queries.astype(BF)
    copies[3].wait()
    keyvalue = dot_nn(rows_norm, keyvalue_in[...]).astype(BF)
    copies[4].wait()
    copies[5].wait()
    member = ints[8]
    scale = size ** (-0.5)
    rows = heads * drafts
    position = lax.broadcasted_iota(jnp.int32, (rows, cache), 1) + member * cache
    token = lax.broadcasted_iota(jnp.int32, (rows, drafts), 0) % drafts
    other = lax.broadcasted_iota(jnp.int32, (rows, drafts), 1)
    seen = other <= jnp.where(member == 0, token, -1)
    lane = lax.broadcasted_iota(jnp.int32, (drafts, AUX), 1)
    for slot in range(slots):
        span = slice(slot * drafts, (slot + 1) * drafts)
        length = ints[slot]
        query = jnp.concatenate(
            [queries[span, h * size : (h + 1) * size] for h in range(heads)], axis=0
        )
        scores = dot_nt(query, keys_in[slot]) * scale
        scores = jnp.where(position < length, scores, NEG)
        draft_scores = dot_nt(query, keyvalue[span, :size]) * scale
        draft_scores = jnp.where(seen, draft_scores, NEG)
        top = jnp.maximum(
            jnp.max(scores, axis=-1, keepdims=True),
            jnp.max(draft_scores, axis=-1, keepdims=True),
        )
        probs = jnp.where(position < length, jnp.exp(scores - top), 0.0)
        draft_probs = jnp.where(seen, jnp.exp(draft_scores - top), 0.0)
        total = jnp.sum(probs, axis=-1, keepdims=True) + jnp.sum(
            draft_probs, axis=-1, keepdims=True
        )
        summed = dot_nn(probs.astype(BF), values_in[slot]) + dot_nn(
            draft_probs.astype(BF), keyvalue[span, size:]
        )
        top_a = top.astype(BF).astype(F32)
        top_b = (top - top_a).astype(BF).astype(F32)
        top_c = top - top_a - top_b
        total_a = total.astype(BF).astype(F32)
        total_b = total - total_a
        aux = jnp.zeros((drafts, AUX), F32)
        for k, piece in enumerate((top_a, top_b, top_c, total_a, total_b)):
            for h in range(heads):
                part = piece[h * drafts : (h + 1) * drafts]
                aux = jnp.where(lane == k * heads + h, part, aux)
        flat = jnp.concatenate(
            [summed[h * drafts : (h + 1) * drafts] for h in range(heads)] + [aux], axis=1
        ).astype(BF)
        for q in range(drafts // own):
            payload[slot * (drafts // own) + q] = flat[q * own : (q + 1) * own]


def attend(ints, arrived, places, extra, gain, query_weight, keyvalue_weight, keys, values):
    tokens, width = extra.shape
    members = arrived.shape[0]
    wide = query_weight.shape[1] + AUX
    far = (query_weight, keyvalue_weight, keys, values)
    outs = [
        jax.ShapeDtypeStruct((members, tokens // members, wide), BF),
        jax.ShapeDtypeStruct((tokens, width), BF),
        jax.ShapeDtypeStruct((tokens, width), BF),
    ]
    return pl.pallas_call(
        attend_kernel,
        grid=(1,),
        in_specs=scalars(1) + near(1) + whole([places, extra, gain]) + streamed(4),
        out_specs=whole(outs),
        out_shape=outs,
        scratch_shapes=[pltpu.VMEM(a.shape, a.dtype) for a in far]
        + [pltpu.SemaphoreType.DMA((6,))],
        compiler_params=PARAMS,
        cost_estimate=lasting(20),
        name="attend",
    )(ints, arrived, places, extra, gain, query_weight, keyvalue_weight, keys, values)


def fold(block):
    half = block.shape[0] // 2
    rest = jnp.concatenate([block[:half, AUX:], block[half:, AUX:]], axis=1)
    return jnp.concatenate([block[:, :AUX], rest], axis=0)


def unfold(block, tokens):
    half = AUX // 2
    rest = jnp.concatenate([block[tokens:, :half], block[tokens:, half:]], axis=0)
    return jnp.concatenate([block[:tokens], rest], axis=1)


def mamba_kernel(
    ints,
    reals,
    normed,
    input_weight,
    gate_weight,
    state_proj,
    step_row,
    states,
    mamba_out,
    blocks,
    chosen,
    proj_in,
    input_in,
    gate_in,
    states_in,
    out_in,
    sems,
):
    moves = (
        (state_proj, proj_in),
        (input_weight, input_in),
        (gate_weight, gate_in),
        (states, states_in),
        (mamba_out, out_in),
    )
    copies = [pltpu.make_async_copy(a, b, sems.at[n]) for n, (a, b) in enumerate(moves)]
    for copy in copies:
        copy.start()
    slots = states.shape[0]
    tokens = normed.shape[0]
    drafts = tokens // slots
    rows = normed[...]
    step_in = (
        jnp.sum(rows.astype(F32) * step_row[...].astype(F32), axis=1, keepdims=True) + reals[0]
    )
    sizes = jnp.maximum(step_in, 0.0) + jnp.log1p(jnp.exp(-jnp.abs(step_in)))
    copies[0].wait()
    both = dot_nn(rows, proj_in[...])
    copies[1].wait()
    x_all = dot_nn(rows, input_in[...])
    copies[2].wait()
    z_all = dot_nn(rows, gate_in[...])
    copies[3].wait()
    state_size = both.shape[1] // 2
    row = lax.broadcasted_iota(jnp.int32, (drafts, drafts), 0)
    col = lax.broadcasted_iota(jnp.int32, (drafts, drafts), 1)
    rows_in = lax.broadcasted_iota(jnp.int32, (drafts, 1), 0)
    gated = []
    for slot in range(slots):
        span = slice(slot * drafts, (slot + 1) * drafts)
        accept = ints[4 + slot]
        size_t = sizes[span]
        size_row = jnp.sum(jnp.where(row == col, size_t, 0.0), axis=0, keepdims=True)
        log_decay = -reals[1] * jnp.sum(
            jnp.where(col <= row, size_row, 0.0), axis=1, keepdims=True
        )
        log_row = jnp.sum(jnp.where(row == col, log_decay, 0.0), axis=0, keepdims=True)
        between = jnp.exp(jnp.where(col <= row, log_decay - log_row, NEG))
        state_in = both[span, :state_size]
        state_read = both[span, state_size:]
        x = x_all[span]
        z = z_all[span]
        inputs = size_t * x
        start = states_in[slot, 0]
        weights = dot_nt(state_read, state_in, HI) * between
        readout = dot_nn(weights, inputs, HI) + jnp.exp(log_decay) * dot_nt(
            state_read, start, HI
        )
        readout = readout + reals[2] * x
        last = jnp.sum(jnp.where(rows_in == accept - 1, log_decay, 0.0), axis=0, keepdims=True)
        remain = jnp.exp(jnp.where(rows_in < accept, last - log_decay, NEG))
        chosen[slot, 0] = (
            jnp.exp(last) * start + dot_tn(remain * inputs, state_in, HI)
        ).astype(BF)
        gated.append((readout * (z / (1.0 + jnp.exp(-z)))).astype(BF))
    copies[4].wait()
    part = dot_nn(jnp.concatenate(gated, axis=0), out_in[...])
    share = part.shape[1] // blocks.shape[0]
    for j in range(blocks.shape[0]):
        block = fold(part[:, j * share : (j + 1) * share]).astype(BF)
        blocks[j, : block.shape[0]] = block
        blocks[j, block.shape[0] :] = jnp.zeros_like(blocks[j, block.shape[0] :])


def mamba(
    ints,
    reals,
    normed,
    input_weight,
    gate_weight,
    state_proj,
    step_row,
    states,
    mamba_out,
    members,
    room,
):
    tokens = normed.shape[0]
    share = mamba_out.shape[1] // members
    outs = [
        jax.ShapeDtypeStruct((members, tokens * share // AUX + room, AUX), BF),
        jax.ShapeDtypeStruct(states.shape, BF),
    ]
    far = (state_proj, input_weight, gate_weight, states, mamba_out)
    return pl.pallas_call(
        mamba_kernel,
        grid=(1,),
        in_specs=scalars(2)
        + whole([normed])
        + streamed(3)
        + whole([step_row])
        + streamed(2),
        out_specs=whole(outs),
        out_shape=outs,
        scratch_shapes=[pltpu.VMEM(a.shape, a.dtype) for a in far]
        + [pltpu.SemaphoreType.DMA((5,))],
        compiler_params=PARAMS,
        cost_estimate=lasting(8),
        name="mamba",
    )(ints, reals, normed, input_weight, gate_weight, state_proj, step_row, states, mamba_out)


def join_kernel(parts, blocks, payload, piece, sem, *, heads, size):
    peers, own, _ = parts.shape
    rows = heads * own
    aux = parts[:, :, heads * size : heads * size + AUX].astype(F32)
    for h in range(heads):
        get = lambda k: aux[:, :, k * heads + h : k * heads + h + 1]
        top = get(0) + get(1) + get(2)
        total = get(3) + get(4)
        factor = jnp.exp(top - jnp.max(top, axis=0, keepdims=True))
        norm = jnp.sum(factor * total, axis=0)
        value = parts[:, :, h * size : (h + 1) * size].astype(F32)
        summed = jnp.sum(factor * value, axis=0)
        piece[h * own : (h + 1) * own, :] = (summed / norm).astype(BF)
    first = payload.shape[1] - rows
    copies = [
        pltpu.make_async_copy(piece, payload.at[j, pl.ds(first, rows), :], sem.at[j])
        for j in range(peers)
    ]
    for copy in copies:
        copy.start()
    for copy in copies:
        copy.wait()


def join(parts, blocks, heads, size):
    peers, own, _ = parts.shape
    return pl.pallas_call(
        functools.partial(join_kernel, heads=heads, size=size),
        grid=(1,),
        in_specs=near(1) + streamed(1),
        out_specs=streamed(1)[0],
        out_shape=jax.ShapeDtypeStruct(blocks.shape, BF),
        input_output_aliases={1: 0},
        scratch_shapes=[
            pltpu.VMEM((heads * own, size), BF),
            pltpu.SemaphoreType.DMA((peers,)),
        ],
        compiler_params=PARAMS,
        cost_estimate=lasting(20),
        name="join",
    )(parts, blocks)


def project_kernel(parts, out_weight, spread, *, heads, size):
    peers, packed, _ = spread.shape
    own = (parts.shape[1] - packed) // heads
    tokens = own * peers
    acc = unfold(jnp.sum(parts[:, :packed, :].astype(F32), axis=0), tokens)
    for h in range(heads):
        attended = jnp.concatenate(
            [parts[j, packed + h * own : packed + (h + 1) * own, :size] for j in range(peers)],
            axis=0,
        )
        acc = acc + dot_nt(attended, out_weight[:, h * size : (h + 1) * size])
    out = fold(acc).astype(BF)
    for j in range(peers):
        spread[j] = out


def project(parts, out_weight, packed, heads, size):
    members = parts.shape[0]
    out = jax.ShapeDtypeStruct((members, packed, AUX), BF)
    return pl.pallas_call(
        functools.partial(project_kernel, heads=heads, size=size),
        grid=(1,),
        in_specs=near(1) + whole([out_weight]),
        out_specs=whole([out])[0],
        out_shape=out,
        compiler_params=PARAMS,
        cost_estimate=lasting(20),
        name="project",
    )(parts, out_weight)


def load_units(weights, gates, ups, downs, sems, units):
    copies = []
    begin = 0
    for w in weights:
        for first in range(0, w.shape[0], 3 * units):
            trio = []
            for k, to in enumerate((gates, ups, downs)):
                copy = pltpu.make_async_copy(
                    w.at[pl.ds(first + k * units, units), :],
                    to.at[pl.ds(begin, units), :],
                    sems.at[len(copies), k],
                )
                copy.start()
                trio.append(copy)
            begin += units
            copies.append((begin, trio))
    return copies


def use_units(second, copies, gates, ups, downs, chunk=256):
    acc = None
    ready = 0
    waiting = list(copies)
    for first in range(0, gates.shape[0], chunk):
        while ready < first + chunk:
            ready, trio = waiting.pop(0)
            for copy in trio:
                copy.wait()
        span = slice(first, first + chunk)
        gate = dot_nt(second, gates[span, :])
        up = dot_nt(second, ups[span, :])
        hidden = (gate / (1.0 + jnp.exp(-gate)) * up).astype(BF)
        part = dot_nn(hidden, downs[span, :])
        acc = part if acc is None else acc + part
    return acc


def feed_kernel(spread, embedded, gain, *refs, count, units):
    weights = refs[:count]
    out, mixed, gates, ups, downs, sems = refs[count:]
    copies = load_units(weights, gates, ups, downs, sems, units)
    tokens = embedded.shape[0]
    peers, own, _ = out.shape
    added = jnp.concatenate([unfold(spread[j].astype(F32), tokens) for j in range(peers)], axis=1)
    rows = (embedded[...].astype(F32) + added).astype(BF)
    mixed[...] = rows
    wide = rows.astype(F32)
    factor = lax.rsqrt(jnp.mean(wide * wide, axis=-1, keepdims=True) + 1e-05)
    rows_norm = (wide * factor * gain[...]).astype(BF)
    acc = use_units(rows_norm, copies, gates, ups, downs)
    for j in range(peers):
        out[j] = acc[j * own : (j + 1) * own, :].astype(BF)


def unit_scratch(weights, units):
    width = weights[0].shape[1]
    rows = sum(w.shape[0] for w in weights)
    count = rows // (3 * units)
    return [pltpu.VMEM((rows // 3, width), BF)] * 3 + [pltpu.SemaphoreType.DMA((count, 3))]


def feed(spread, embedded, gain, weights, units):
    members = spread.shape[0]
    tokens, width = embedded.shape
    outs = [
        jax.ShapeDtypeStruct((members, tokens // members, width), BF),
        jax.ShapeDtypeStruct(embedded.shape, BF),
    ]
    return pl.pallas_call(
        functools.partial(feed_kernel, count=len(weights), units=units),
        grid=(1,),
        in_specs=near(1) + whole([embedded, gain]) + streamed(len(weights)),
        out_specs=whole(outs),
        out_shape=outs,
        scratch_shapes=unit_scratch(weights, units),
        compiler_params=PARAMS,
        cost_estimate=lasting(20),
        name="feed",
    )(spread, embedded, gain, *weights)


def pack_kernel(gate, up, down, ready, low, high):
    half = low.shape[0] // 3
    for k, part in enumerate((gate, up, down)):
        low[k * half : (k + 1) * half] = part[:half]
        high[k * half : (k + 1) * half] = part[half:]


def pack(gate, up, down, ready):
    units, width = gate.shape
    out = jax.ShapeDtypeStruct((3 * units // 2, width), gate.dtype)
    return pl.pallas_call(
        pack_kernel,
        grid=(1,),
        in_specs=whole([gate, up, down]) + streamed(1),
        out_specs=whole([out, out]),
        out_shape=[out, out],
        compiler_params=PARAMS,
        cost_estimate=cost(0, 1024),
        name="pack",
    )(gate, up, down, ready)


def pick_kernel(turns, rows, *refs):
    held = refs[:-1]
    out = refs[-1]
    for i in range(out.shape[0]):
        for n, ref in enumerate(held):

            @pl.when(turns[i] == n)
            def _():
                out[i] = ref[rows[i]].astype(F32)


def pick_states(turns, rows, held, count):
    shape = (count,) + held[0].shape[1:]
    out = jax.ShapeDtypeStruct(shape, F32)
    return pl.pallas_call(
        pick_kernel,
        grid=(1,),
        in_specs=scalars(2) + whole(held),
        out_specs=whole([out])[0],
        out_shape=out,
        compiler_params=PARAMS,
        name="pick",
    )(turns, rows, *held)


def local(
    draft_ids,
    lengths,
    current_slot,
    new_slot,
    accepted,
    embed_table,
    mixer_gain,
    query_weight,
    keyvalue_weight,
    key_cache,
    value_cache,
    attention_out,
    mamba_input,
    mamba_gate,
    state_proj,
    mamba_step,
    step_bias,
    decay_log,
    skip_gain,
    states,
    mamba_out,
    mlp_gain,
    gate_weight,
    up_weight,
    down_weight,
):
    members = lax.axis_size("tok")
    groups = lax.axis_size("req")
    group_index = lax.axis_index("req")
    member = lax.axis_index("tok")
    slots_dev, cache_dev, head_size = key_cache.shape
    draft_len = draft_ids.shape[1]
    width = embed_table.shape[1]
    query_heads = query_weight.shape[1] // head_size
    own = slots_dev * draft_len // members

    cores = 2
    chips = groups // cores

    def turn(value, by):
        return lax.ppermute(
            value, "req", [(g, (g + by * cores) % groups) for g in range(groups)]
        )

    def across(value):
        return lax.ppermute(value, "req", [(g, g ^ 1) for g in range(groups)])

    def exchange(turn):
        sent, places, origin, most = fetch(
            turn, current_slot[None], draft_ids.T, embed_table, groups, members
        )
        came = lax.all_to_all(sent, ("req", "tok"), 0, 0, tiled=True)
        return came, places, origin, most

    def plane(rows):
        return lax.all_to_all(rows, "tok", 0, 0, tiled=True)

    came, places, origin, most = exchange(jnp.zeros((1,), jnp.int32))

    low, high = pack(gate_weight.T, up_weight.T, down_weight.T, places)
    near_z = [turn(low, 1), turn(high, -1), turn(high, 1), turn(low, -1)]
    handed = hand(origin, came, members)
    weights = [low, high] + near_z
    arrived = plane(handed)

    def more(carry):
        return carry[0][0] < most[0]

    def round_of(carry):
        at, rows = carry
        later, spots, froms, _ = exchange(at)
        return at + 1, place(plane(hand(froms, later, members)), spots, rows)

    _, extra = lax.while_loop(
        more, round_of, (jnp.ones((1,), jnp.int32), jnp.zeros((members * own, width), BF))
    )

    slot_owner = inverse_of(current_slot)
    local_owner = lax.dynamic_slice_in_dim(slot_owner, group_index * slots_dev, slots_dev)
    ints = jnp.concatenate(
        [jnp.take(lengths, local_owner), jnp.take(accepted, local_owner), member[None]]
    )
    reals = jnp.concatenate([step_bias, jnp.exp(decay_log), skip_gain])
    payload, embedded, normed = attend(
        ints,
        arrived,
        places,
        extra,
        mixer_gain[None],
        query_weight,
        keyvalue_weight,
        key_cache,
        value_cache,
    )
    parts = lax.all_to_all(payload, "tok", 0, 0, tiled=True)
    later = lax.optimization_barrier((near_z[0], near_z[1], payload))
    far = [turn(later[0], 1), turn(later[1], -1)]
    blocks, chosen = mamba(
        ints,
        reals,
        normed,
        mamba_input,
        mamba_gate,
        state_proj,
        mamba_step.T,
        states,
        mamba_out,
        members,
        query_heads * own,
    )
    joint = join(parts, blocks, query_heads, head_size)
    joined = lax.all_to_all(joint, "tok", 0, 0, tiled=True)
    *later, chosen, _ = lax.optimization_barrier((*weights, chosen, joint))
    weights += [across(w) for w in later]
    chosen = chosen[:, 0]
    pair = jnp.concatenate([chosen, across(chosen)], axis=0)
    joined, *_ = lax.optimization_barrier((joined, *far))
    folded = members * own * (width // members) // AUX
    spread = project(joined, attention_out.T, folded, query_heads, head_size)
    first, second, spread, pair, *_ = lax.optimization_barrier((*far, spread, pair, *weights[-6:]))
    far = [first, second]
    weights += far + [across(w) for w in far]
    added = lax.all_to_all(spread, "tok", 0, 0, tiled=True)
    half = gate_weight.shape[1] // 2
    mlp_part, mixed = feed(added, embedded, mlp_gain[None], weights, half)
    mlp_rows = lax.all_to_all(mlp_part, "tok", 0, 0, tiled=True)
    own_rows = lax.optimization_barrier(lax.dynamic_slice_in_dim(mixed, member * own, own))
    hidden_out = (own_rows.astype(F32) + jnp.sum(mlp_rows.astype(F32), axis=0)).astype(BF)

    incoming = inverse_of(new_slot)
    local_targets = lax.dynamic_slice_in_dim(incoming, group_index * slots_dev, slots_dev)
    sources = jnp.take(current_slot, local_targets)
    held = [pair] + [turn(pair, by) for by in range(1, chips)]
    source_group = sources // slots_dev
    turns = (group_index // cores - source_group // cores) % chips
    other_core = (source_group % cores) != (group_index % cores)
    rows = sources % slots_dev + jnp.where(other_core, slots_dev, 0)
    new_states = pick_states(turns, rows, held, slots_dev)[:, None]
    return (hidden_out, new_states)


def solution(mesh):
    return jax.shard_map(
        local,
        mesh=mesh,
        in_specs=(
            P(),
            P(),
            P(),
            P(),
            P(),
            P(("req", "tok"), None),
            P(),
            P(),
            P(),
            P("req", "tok", None),
            P("req", "tok", None),
            P(None, "tok"),
            P(None, "tok"),
            P(None, "tok"),
            P(),
            P(None, "tok"),
            P("tok"),
            P("tok"),
            P("tok"),
            P("req", "tok", None, None),
            P("tok", None),
            P(),
            P(None, ("req", "tok")),
            P(None, ("req", "tok")),
            P(None, ("req", "tok")),
        ),
        out_specs=(P(("req", "tok"), None), P("req", "tok", None, None)),
        check_vma=False,
    )
```

```python
import functools

import jax
import jax.numpy as jnp
from jax import lax
from jax.experimental import pallas as pl
from jax.experimental.pallas import tpu as pltpu
from jax.sharding import PartitionSpec as P

BF = jnp.bfloat16
F32 = jnp.float32
NEG = -1e30
AUX = 128
VMEM = 63 << 10


def inverse_of(mapping):
    places = jnp.arange(mapping.shape[0], dtype=jnp.int32)
    matches = mapping[None, :] == places[:, None]
    return jnp.sum(jnp.where(matches, places[None, :], 0), axis=1)


def dot_nn(a, b, precision=None):
    return lax.dot_general(
        a, b, (((1,), (0,)), ((), ())), precision=precision, preferred_element_type=F32
    )


def dot_nt(a, b, precision=None):
    return lax.dot_general(
        a, b, (((1,), (1,)), ((), ())), precision=precision, preferred_element_type=F32
    )


def dot_tn(a, b, precision=None):
    return lax.dot_general(
        a, b, (((0,), (0,)), ((), ())), precision=precision, preferred_element_type=F32
    )


HI = lax.Precision.HIGHEST


def cost(flops, moved, special=0):
    return pl.CostEstimate(flops=flops, bytes_accessed=moved, transcendentals=special)


def lasting(microseconds):
    return cost(int(microseconds * 1e9), 1024)


def whole(shapes):
    return [pl.BlockSpec(a.shape, lambda i, n=len(a.shape): (0,) * n) for a in shapes]


def near(count):
    return [pl.BlockSpec(memory_space=pltpu.VMEM)] * count


def streamed(count):
    return [pl.BlockSpec(memory_space=pltpu.HBM)] * count


def scalars(count):
    return [pl.BlockSpec(memory_space=pltpu.SMEM)] * count


PARAMS = pltpu.CompilerParams(vmem_limit_bytes=VMEM << 10)
SMALL = pltpu.CompilerParams(vmem_limit_bytes=8 << 20)


def fetch_kernel(
    turn, slots_row, ids_cols, table_far, payload, places, origin, most, table, sem, *, groups, members
):
    load = pltpu.make_async_copy(table_far, table, sem)
    load.start()
    drafts, requests = ids_cols.shape
    vocab = table.shape[0]
    count = requests * drafts // groups
    slots = requests // groups
    group = lax.axis_index("req")
    member = lax.axis_index("tok")
    me = group * members + member
    now = turn[0]
    sub = lax.broadcasted_iota(jnp.int32, (count, count), 0)
    lane = lax.broadcasted_iota(jnp.int32, (count, count), 1)
    sub_c = sub[:, :1]
    lane_r = lane[:1, :]
    ids = ids_cols[...]
    ids_hi = (ids // 256).astype(F32).astype(BF)
    ids_lo = (ids % 256).astype(F32).astype(BF)
    row_slot = lax.broadcasted_iota(jnp.int32, (count, requests), 0) // drafts
    token = lax.broadcasted_iota(jnp.int32, (count, drafts), 0) % drafts
    token_lane = lax.broadcasted_iota(jnp.int32, (count, drafts), 1)
    column = lax.broadcasted_iota(jnp.int32, (members, count), 0)
    local_iota = lax.broadcasted_iota(jnp.int32, (members, vocab), 1)
    own = count // members
    hots = []
    own_place = jnp.zeros((count, 1), jnp.int32)
    own_from = [jnp.zeros((1, count), jnp.int32)] * own
    peak = jnp.zeros((1, count), jnp.int32)
    for g in range(groups):
        pick = jnp.where(slots_row[...] == row_slot + g * slots, 1.0, 0.0).astype(BF)
        mixed_ids = dot_nt(pick, ids_hi) * 256.0 + dot_nt(pick, ids_lo)
        id_c = jnp.sum(
            jnp.where(token == token_lane, mixed_ids, 0.0), axis=1, keepdims=True
        ).astype(jnp.int32)
        id_r = jnp.sum(jnp.where(sub == lane, id_c, 0), axis=0, keepdims=True)
        same = id_c == id_r
        first_c = jnp.min(jnp.where(same, lane, count), axis=1, keepdims=True)
        first_r = jnp.min(jnp.where(same, sub, count), axis=0, keepdims=True)
        owner_c = id_c // vocab
        owner_r = id_r // vocab
        alike = owner_c == owner_r
        before_r = (first_c == sub_c) & alike & (sub < first_r)
        less_r = (first_c == sub_c) & (owner_c < owner_r)
        nth_r = jnp.sum(jnp.where(before_r, 1, 0), axis=0, keepdims=True)
        rank_r = nth_r + jnp.sum(jnp.where(less_r, 1, 0), axis=0, keepdims=True)
        peak = jnp.maximum(peak, nth_r // members + 1)
        before_c = (first_r == lane_r) & alike & (lane < first_c)
        less_c = (first_r == lane_r) & (owner_r < owner_c)
        nth_c = jnp.sum(jnp.where(before_c, 1, 0), axis=1, keepdims=True)
        rank_c = nth_c + jnp.sum(jnp.where(less_c, 1, 0), axis=1, keepdims=True)
        spot = (rank_c % members) * own + rank_c // members
        spot = jnp.where(nth_c // members == now, spot, -1)
        own_place = jnp.where(group == g, spot, own_place)
        sent_r = (first_r == lane_r) & (nth_r // members == now)
        asked = sent_r & (owner_r == me) & (rank_r % members == column)
        row = jnp.sum(jnp.where(asked, id_r % vocab + 1, 0), axis=1, keepdims=True) - 1
        hots.append(jnp.where(local_iota == row, 1.0, 0.0))
        for k in range(own):
            here = sent_r & (rank_r == k * members + member) & (group == g)
            own_from[k] = own_from[k] + jnp.where(here, owner_r + 1, 0)
    places[...] = jnp.broadcast_to(own_place, places.shape)
    for k in range(own):
        origin[k] = jnp.sum(own_from[k]) - 1
    most[0] = jnp.max(peak)
    hot = jnp.concatenate(hots, axis=0).astype(BF)
    load.wait()
    payload[...] = dot_nn(hot, table[...]).reshape(payload.shape).astype(BF)


def fetch(turn, slots_row, ids_cols, table, groups, members):
    count = ids_cols.size // groups
    outs = [
        jax.ShapeDtypeStruct((groups * members, table.shape[1] // AUX, AUX), BF),
        jax.ShapeDtypeStruct((count, AUX), jnp.int32),
        jax.ShapeDtypeStruct((count // members,), jnp.int32),
        jax.ShapeDtypeStruct((1,), jnp.int32),
    ]
    return pl.pallas_call(
        functools.partial(fetch_kernel, groups=groups, members=members),
        grid=(1,),
        in_specs=scalars(1) + whole([slots_row, ids_cols]) + streamed(1),
        out_specs=whole(outs[:2]) + scalars(2),
        out_shape=outs,
        scratch_shapes=[pltpu.VMEM(table.shape, table.dtype), pltpu.SemaphoreType.DMA],
        compiler_params=PARAMS,
        cost_estimate=cost(2 * groups * members * table.size, 2 * table.size),
        name="fetch",
    )(turn, slots_row, ids_cols, table)


def hand_kernel(origin, came, spread):
    peers, own, lines = spread.shape[0], origin.shape[0], came.shape[1]
    for k in range(own):
        source = origin[k]
        row = came[jnp.maximum(source, 0)]
        row = jnp.where(source >= 0, row.astype(F32), 0.0).astype(BF)
        for j in range(peers):
            spread[j, k * lines : (k + 1) * lines, :] = row


def hand(origin, came, members):
    own = origin.shape[0]
    out = jax.ShapeDtypeStruct((members, own * came.shape[1], AUX), BF)
    return pl.pallas_call(
        hand_kernel,
        in_specs=scalars(1) + near(1),
        out_specs=near(1)[0],
        out_shape=out,
        compiler_params=SMALL,
        cost_estimate=lasting(10),
        name="hand",
    )(origin, came)


def rows_of(arrived, places):
    count = places.shape[0]
    width = arrived.size // count
    slot = lax.broadcasted_iota(jnp.int32, (count, count), 1)
    hot = jnp.where(slot == places[:, :1], 1.0, 0.0).astype(BF)
    lines = arrived[...].astype(F32).reshape(count, width // AUX, AUX)
    return dot_nn(hot, lines.reshape(count, width).astype(BF))


def place_kernel(arrived, places, before, out):
    out[...] = (before[...].astype(F32) + rows_of(arrived, places)).astype(BF)


def place(arrived, places, before):
    return pl.pallas_call(
        place_kernel,
        grid=(1,),
        in_specs=whole([arrived, places, before]),
        out_specs=whole([before])[0],
        out_shape=jax.ShapeDtypeStruct(before.shape, BF),
        compiler_params=PARAMS,
        name="place",
    )(arrived, places, before)


def attend_kernel(
    ints,
    arrived,
    places,
    extra,
    gain,
    query_weight,
    keyvalue_weight,
    keys,
    values,
    payload,
    embedded,
    normed,
    query_in,
    keyvalue_in,
    keys_in,
    values_in,
    sems,
):
    moves = []
    third = query_weight.shape[0] // 3
    for k in range(3):
        span = pl.ds(k * third, third)
        moves.append((query_weight.at[span, :], query_in.at[span, :]))
    moves += [(keyvalue_weight, keyvalue_in), (keys, keys_in), (values, values_in)]
    copies = [pltpu.make_async_copy(a, b, sems.at[n]) for n, (a, b) in enumerate(moves)]
    for copy in copies:
        copy.start()
    slots, cache, size = keys.shape
    tokens = extra.shape[0]
    drafts = tokens // slots
    heads = query_weight.shape[1] // size
    own = payload.shape[1]
    rows_in = (rows_of(arrived, places) + extra[...].astype(F32)).astype(BF)
    embedded[...] = rows_in
    wide = rows_in.astype(F32)
    factor = lax.rsqrt(jnp.mean(wide * wide, axis=-1, keepdims=True) + 1e-05)
    rows_norm = (wide * factor * gain[...]).astype(BF)
    normed[...] = rows_norm
    queries = None
    for k in range(3):
        copies[k].wait()
        span = slice(k * third, (k + 1) * third)
        part = dot_nn(rows_norm[:, span], query_in[span, :])
        queries = part if queries is None else queries + part
    queries = queries.astype(BF)
    copies[3].wait()
    keyvalue = dot_nn(rows_norm, keyvalue_in[...]).astype(BF)
    copies[4].wait()
    copies[5].wait()
    member = ints[8]
    scale = size ** (-0.5)
    rows = heads * drafts
    position = lax.broadcasted_iota(jnp.int32, (rows, cache), 1) + member * cache
    token = lax.broadcasted_iota(jnp.int32, (rows, drafts), 0) % drafts
    other = lax.broadcasted_iota(jnp.int32, (rows, drafts), 1)
    seen = other <= jnp.where(member == 0, token, -1)
    lane = lax.broadcasted_iota(jnp.int32, (drafts, AUX), 1)
    for slot in range(slots):
        span = slice(slot * drafts, (slot + 1) * drafts)
        length = ints[slot]
        query = jnp.concatenate(
            [queries[span, h * size : (h + 1) * size] for h in range(heads)], axis=0
        )
        scores = dot_nt(query, keys_in[slot]) * scale
        scores = jnp.where(position < length, scores, NEG)
        draft_scores = dot_nt(query, keyvalue[span, :size]) * scale
        draft_scores = jnp.where(seen, draft_scores, NEG)
        top = jnp.maximum(
            jnp.max(scores, axis=-1, keepdims=True),
            jnp.max(draft_scores, axis=-1, keepdims=True),
        )
        probs = jnp.where(position < length, jnp.exp(scores - top), 0.0)
        draft_probs = jnp.where(seen, jnp.exp(draft_scores - top), 0.0)
        total = jnp.sum(probs, axis=-1, keepdims=True) + jnp.sum(
            draft_probs, axis=-1, keepdims=True
        )
        summed = dot_nn(probs.astype(BF), values_in[slot]) + dot_nn(
            draft_probs.astype(BF), keyvalue[span, size:]
        )
        top_a = top.astype(BF).astype(F32)
        top_b = (top - top_a).astype(BF).astype(F32)
        top_c = top - top_a - top_b
        total_a = total.astype(BF).astype(F32)
        total_b = total - total_a
        aux = jnp.zeros((drafts, AUX), F32)
        for k, piece in enumerate((top_a, top_b, top_c, total_a, total_b)):
            for h in range(heads):
                part = piece[h * drafts : (h + 1) * drafts]
                aux = jnp.where(lane == k * heads + h, part, aux)
        flat = jnp.concatenate(
            [summed[h * drafts : (h + 1) * drafts] for h in range(heads)] + [aux], axis=1
        ).astype(BF)
        for q in range(drafts // own):
            payload[slot * (drafts // own) + q] = flat[q * own : (q + 1) * own]


def attend(ints, arrived, places, extra, gain, query_weight, keyvalue_weight, keys, values):
    tokens, width = extra.shape
    members = arrived.shape[0]
    wide = query_weight.shape[1] + AUX
    far = (query_weight, keyvalue_weight, keys, values)
    outs = [
        jax.ShapeDtypeStruct((members, tokens // members, wide), BF),
        jax.ShapeDtypeStruct((tokens, width), BF),
        jax.ShapeDtypeStruct((tokens, width), BF),
    ]
    return pl.pallas_call(
        attend_kernel,
        grid=(1,),
        in_specs=scalars(1) + whole([arrived, places, extra, gain]) + streamed(4),
        out_specs=whole(outs),
        out_shape=outs,
        scratch_shapes=[pltpu.VMEM(a.shape, a.dtype) for a in far]
        + [pltpu.SemaphoreType.DMA((6,))],
        compiler_params=PARAMS,
        cost_estimate=lasting(20),
        name="attend",
    )(ints, arrived, places, extra, gain, query_weight, keyvalue_weight, keys, values)


def fold(block):
    half = block.shape[0] // 2
    rest = jnp.concatenate([block[:half, AUX:], block[half:, AUX:]], axis=1)
    return jnp.concatenate([block[:, :AUX], rest], axis=0)


def unfold(block, tokens):
    half = AUX // 2
    rest = jnp.concatenate([block[tokens:, :half], block[tokens:, half:]], axis=0)
    return jnp.concatenate([block[:tokens], rest], axis=1)


def mamba_kernel(
    ints,
    reals,
    normed,
    input_weight,
    gate_weight,
    state_proj,
    step_row,
    states,
    mamba_out,
    blocks,
    chosen,
    proj_in,
    input_in,
    gate_in,
    states_in,
    out_in,
    sems,
):
    moves = (
        (state_proj, proj_in),
        (input_weight, input_in),
        (gate_weight, gate_in),
        (states, states_in),
        (mamba_out, out_in),
    )
    copies = [pltpu.make_async_copy(a, b, sems.at[n]) for n, (a, b) in enumerate(moves)]
    for copy in copies:
        copy.start()
    slots = states.shape[0]
    tokens = normed.shape[0]
    drafts = tokens // slots
    rows = normed[...]
    step_in = (
        jnp.sum(rows.astype(F32) * step_row[...].astype(F32), axis=1, keepdims=True) + reals[0]
    )
    sizes = jnp.maximum(step_in, 0.0) + jnp.log1p(jnp.exp(-jnp.abs(step_in)))
    copies[0].wait()
    both = dot_nn(rows, proj_in[...])
    copies[1].wait()
    x_all = dot_nn(rows, input_in[...])
    copies[2].wait()
    z_all = dot_nn(rows, gate_in[...])
    copies[3].wait()
    state_size = both.shape[1] // 2
    row = lax.broadcasted_iota(jnp.int32, (drafts, drafts), 0)
    col = lax.broadcasted_iota(jnp.int32, (drafts, drafts), 1)
    rows_in = lax.broadcasted_iota(jnp.int32, (drafts, 1), 0)
    gated = []
    for slot in range(slots):
        span = slice(slot * drafts, (slot + 1) * drafts)
        accept = ints[4 + slot]
        size_t = sizes[span]
        size_row = jnp.sum(jnp.where(row == col, size_t, 0.0), axis=0, keepdims=True)
        log_decay = -reals[1] * jnp.sum(
            jnp.where(col <= row, size_row, 0.0), axis=1, keepdims=True
        )
        log_row = jnp.sum(jnp.where(row == col, log_decay, 0.0), axis=0, keepdims=True)
        between = jnp.exp(jnp.where(col <= row, log_decay - log_row, NEG))
        state_in = both[span, :state_size]
        state_read = both[span, state_size:]
        x = x_all[span]
        z = z_all[span]
        inputs = size_t * x
        start = states_in[slot, 0]
        weights = dot_nt(state_read, state_in, HI) * between
        readout = dot_nn(weights, inputs, HI) + jnp.exp(log_decay) * dot_nt(
            state_read, start, HI
        )
        readout = readout + reals[2] * x
        last = jnp.sum(jnp.where(rows_in == accept - 1, log_decay, 0.0), axis=0, keepdims=True)
        remain = jnp.exp(jnp.where(rows_in < accept, last - log_decay, NEG))
        chosen[slot, 0] = (
            jnp.exp(last) * start + dot_tn(remain * inputs, state_in, HI)
        ).astype(BF)
        gated.append((readout * (z / (1.0 + jnp.exp(-z)))).astype(BF))
    copies[4].wait()
    part = dot_nn(jnp.concatenate(gated, axis=0), out_in[...])
    share = part.shape[1] // blocks.shape[0]
    for j in range(blocks.shape[0]):
        block = fold(part[:, j * share : (j + 1) * share]).astype(BF)
        blocks[j, : block.shape[0]] = block
        blocks[j, block.shape[0] :] = jnp.zeros_like(blocks[j, block.shape[0] :])


def mamba(
    ints,
    reals,
    normed,
    input_weight,
    gate_weight,
    state_proj,
    step_row,
    states,
    mamba_out,
    members,
    room,
):
    tokens = normed.shape[0]
    share = mamba_out.shape[1] // members
    outs = [
        jax.ShapeDtypeStruct((members, tokens * share // AUX + room, AUX), BF),
        jax.ShapeDtypeStruct(states.shape, BF),
    ]
    far = (state_proj, input_weight, gate_weight, states, mamba_out)
    return pl.pallas_call(
        mamba_kernel,
        grid=(1,),
        in_specs=scalars(2)
        + whole([normed])
        + streamed(3)
        + whole([step_row])
        + streamed(2),
        out_specs=whole(outs),
        out_shape=outs,
        scratch_shapes=[pltpu.VMEM(a.shape, a.dtype) for a in far]
        + [pltpu.SemaphoreType.DMA((5,))],
        compiler_params=PARAMS,
        cost_estimate=lasting(8),
        name="mamba",
    )(ints, reals, normed, input_weight, gate_weight, state_proj, step_row, states, mamba_out)


def join_kernel(parts, blocks, payload, piece, sem, *, heads, size):
    peers, own, _ = parts.shape
    rows = heads * own
    aux = parts[:, :, heads * size : heads * size + AUX].astype(F32)
    get = lambda k: aux[:, :, k * heads : (k + 1) * heads]
    top = get(0) + get(1) + get(2)
    total = get(3) + get(4)
    factors = jnp.exp(top - jnp.max(top, axis=0, keepdims=True))
    factors = factors / jnp.sum(factors * total, axis=0, keepdims=True)
    for h in range(heads):
        value = parts[:, :, h * size : (h + 1) * size].astype(F32)
        summed = jnp.sum(factors[:, :, h : h + 1] * value, axis=0)
        piece[h * own : (h + 1) * own, :] = summed.astype(BF)
    first = payload.shape[1] - rows
    copies = [
        pltpu.make_async_copy(piece, payload.at[j, pl.ds(first, rows), :], sem.at[j])
        for j in range(peers)
    ]
    for copy in copies:
        copy.start()
    for copy in copies:
        copy.wait()


def join(parts, blocks, heads, size):
    peers, own, _ = parts.shape
    return pl.pallas_call(
        functools.partial(join_kernel, heads=heads, size=size),
        grid=(1,),
        in_specs=whole([parts]) + streamed(1),
        out_specs=streamed(1)[0],
        out_shape=jax.ShapeDtypeStruct(blocks.shape, BF),
        input_output_aliases={1: 0},
        scratch_shapes=[
            pltpu.VMEM((heads * own, size), BF),
            pltpu.SemaphoreType.DMA((peers,)),
        ],
        compiler_params=PARAMS,
        cost_estimate=lasting(20),
        name="join",
    )(parts, blocks)


def project_kernel(parts, out_weight, spread, *, heads, size):
    peers, packed, _ = spread.shape
    own = (parts.shape[1] - packed) // heads
    tokens = own * peers
    acc = unfold(jnp.sum(parts[:, :packed, :].astype(F32), axis=0), tokens)
    for h in range(heads):
        attended = jnp.concatenate(
            [parts[j, packed + h * own : packed + (h + 1) * own, :size] for j in range(peers)],
            axis=0,
        )
        acc = acc + dot_nt(attended, out_weight[:, h * size : (h + 1) * size])
    out = fold(acc).astype(BF)
    for j in range(peers):
        spread[j] = out


def project(parts, out_weight, packed, heads, size):
    members = parts.shape[0]
    out = jax.ShapeDtypeStruct((members, packed, AUX), BF)
    return pl.pallas_call(
        functools.partial(project_kernel, heads=heads, size=size),
        grid=(1,),
        in_specs=whole([parts, out_weight]),
        out_specs=whole([out])[0],
        out_shape=out,
        compiler_params=PARAMS,
        cost_estimate=lasting(20),
        name="project",
    )(parts, out_weight)


def load_units(weights, gates, ups, downs, sems, units):
    copies = []
    begin = 0
    for w in weights:
        for first in range(0, w.shape[0], 3 * units):
            trio = []
            for k, to in enumerate((gates, ups, downs)):
                copy = pltpu.make_async_copy(
                    w.at[pl.ds(first + k * units, units), :],
                    to.at[pl.ds(begin, units), :],
                    sems.at[len(copies), k],
                )
                copy.start()
                trio.append(copy)
            begin += units
            copies.append((begin, trio))
    return copies


def use_units(second, copies, gates, ups, downs, chunk=256):
    acc = None
    ready = 0
    waiting = list(copies)
    for first in range(0, gates.shape[0], chunk):
        while ready < first + chunk:
            ready, trio = waiting.pop(0)
            for copy in trio:
                copy.wait()
        span = slice(first, first + chunk)
        gate = dot_nt(second, gates[span, :])
        up = dot_nt(second, ups[span, :])
        hidden = (gate / (1.0 + jnp.exp(-gate)) * up).astype(BF)
        part = dot_nn(hidden, downs[span, :])
        acc = part if acc is None else acc + part
    return acc


def feed_kernel(spread, embedded, gain, *refs, count, units):
    weights = refs[:count]
    out, mixed, gates, ups, downs, sems = refs[count:]
    copies = load_units(weights, gates, ups, downs, sems, units)
    tokens = embedded.shape[0]
    peers, own, _ = out.shape
    added = jnp.concatenate([unfold(spread[j].astype(F32), tokens) for j in range(peers)], axis=1)
    rows = (embedded[...].astype(F32) + added).astype(BF)
    mixed[...] = rows
    wide = rows.astype(F32)
    factor = lax.rsqrt(jnp.mean(wide * wide, axis=-1, keepdims=True) + 1e-05)
    rows_norm = (wide * factor * gain[...]).astype(BF)
    acc = use_units(rows_norm, copies, gates, ups, downs)
    for j in range(peers):
        out[j] = acc[j * own : (j + 1) * own, :].astype(BF)


def unit_scratch(weights, units):
    width = weights[0].shape[1]
    rows = sum(w.shape[0] for w in weights)
    count = rows // (3 * units)
    return [pltpu.VMEM((rows // 3, width), BF)] * 3 + [pltpu.SemaphoreType.DMA((count, 3))]


def feed(spread, embedded, gain, weights, units):
    members = spread.shape[0]
    tokens, width = embedded.shape
    outs = [
        jax.ShapeDtypeStruct((members, tokens // members, width), BF),
        jax.ShapeDtypeStruct(embedded.shape, BF),
    ]
    return pl.pallas_call(
        functools.partial(feed_kernel, count=len(weights), units=units),
        grid=(1,),
        in_specs=whole([spread, embedded, gain]) + streamed(len(weights)),
        out_specs=whole(outs),
        out_shape=outs,
        scratch_shapes=unit_scratch(weights, units),
        compiler_params=PARAMS,
        cost_estimate=lasting(20),
        name="feed",
    )(spread, embedded, gain, *weights)


def pack_kernel(gate, up, down, ready, low, high):
    half = low.shape[0] // 3
    for k, part in enumerate((gate, up, down)):
        low[k * half : (k + 1) * half] = part[:half]
        high[k * half : (k + 1) * half] = part[half:]


def pack(gate, up, down, ready):
    units, width = gate.shape
    out = jax.ShapeDtypeStruct((3 * units // 2, width), gate.dtype)
    return pl.pallas_call(
        pack_kernel,
        grid=(1,),
        in_specs=whole([gate, up, down]) + streamed(1),
        out_specs=whole([out, out]),
        out_shape=[out, out],
        compiler_params=PARAMS,
        cost_estimate=cost(0, 1024),
        name="pack",
    )(gate, up, down, ready)


def pick_kernel(turns, rows, *refs):
    held = refs[:-1]
    out = refs[-1]
    for i in range(out.shape[0]):
        for n, ref in enumerate(held):

            @pl.when(turns[i] == n)
            def _():
                out[i] = ref[rows[i]].astype(F32)


def pick_states(turns, rows, held, count):
    shape = (count,) + held[0].shape[1:]
    out = jax.ShapeDtypeStruct(shape, F32)
    return pl.pallas_call(
        pick_kernel,
        grid=(1,),
        in_specs=scalars(2) + whole(held),
        out_specs=whole([out])[0],
        out_shape=out,
        compiler_params=PARAMS,
        name="pick",
    )(turns, rows, *held)


def local(
    draft_ids,
    lengths,
    current_slot,
    new_slot,
    accepted,
    embed_table,
    mixer_gain,
    query_weight,
    keyvalue_weight,
    key_cache,
    value_cache,
    attention_out,
    mamba_input,
    mamba_gate,
    state_proj,
    mamba_step,
    step_bias,
    decay_log,
    skip_gain,
    states,
    mamba_out,
    mlp_gain,
    gate_weight,
    up_weight,
    down_weight,
):
    members = lax.axis_size("tok")
    groups = lax.axis_size("req")
    group_index = lax.axis_index("req")
    member = lax.axis_index("tok")
    slots_dev, cache_dev, head_size = key_cache.shape
    draft_len = draft_ids.shape[1]
    width = embed_table.shape[1]
    query_heads = query_weight.shape[1] // head_size
    own = slots_dev * draft_len // members

    cores = 2
    chips = groups // cores

    def turn(value, by):
        return lax.ppermute(
            value, "req", [(g, (g + by * cores) % groups) for g in range(groups)]
        )

    def across(value):
        return lax.ppermute(value, "req", [(g, g ^ 1) for g in range(groups)])

    def exchange(turn):
        sent, places, origin, most = fetch(
            turn, current_slot[None], draft_ids.T, embed_table, groups, members
        )
        came = lax.all_to_all(sent, ("req", "tok"), 0, 0, tiled=True)
        return came, places, origin, most

    def plane(rows):
        return lax.all_to_all(rows, "tok", 0, 0, tiled=True)

    came, places, origin, most = exchange(jnp.zeros((1,), jnp.int32))

    low, high = pack(gate_weight.T, up_weight.T, down_weight.T, places)
    near_z = [turn(low, 1), turn(high, -1), turn(high, 1), turn(low, -1)]
    handed = hand(origin, came, members)
    weights = [low, high] + near_z
    arrived = plane(handed)

    def more(carry):
        return carry[0][0] < most[0]

    def round_of(carry):
        at, rows = carry
        later, spots, froms, _ = exchange(at)
        return at + 1, place(plane(hand(froms, later, members)), spots, rows)

    _, extra = lax.while_loop(
        more, round_of, (jnp.ones((1,), jnp.int32), jnp.zeros((members * own, width), BF))
    )

    slot_owner = inverse_of(current_slot)
    local_owner = lax.dynamic_slice_in_dim(slot_owner, group_index * slots_dev, slots_dev)
    ints = jnp.concatenate(
        [jnp.take(lengths, local_owner), jnp.take(accepted, local_owner), member[None]]
    )
    reals = jnp.concatenate([step_bias, jnp.exp(decay_log), skip_gain])
    payload, embedded, normed = attend(
        ints,
        arrived,
        places,
        extra,
        mixer_gain[None],
        query_weight,
        keyvalue_weight,
        key_cache,
        value_cache,
    )
    parts = lax.all_to_all(payload, "tok", 0, 0, tiled=True)
    blocks, chosen = mamba(
        ints,
        reals,
        normed,
        mamba_input,
        mamba_gate,
        state_proj,
        mamba_step.T,
        states,
        mamba_out,
        members,
        query_heads * own,
    )
    later = lax.optimization_barrier((near_z[0], near_z[1], blocks))
    far = [turn(later[0], 1), turn(later[1], -1)]
    joint = join(parts, blocks, query_heads, head_size)
    joined = lax.all_to_all(joint, "tok", 0, 0, tiled=True)
    *later, chosen, _ = lax.optimization_barrier((*weights, chosen, joint))
    weights += [across(w) for w in later]
    chosen = chosen[:, 0]
    pair = jnp.concatenate([chosen, across(chosen)], axis=0)
    joined, *_ = lax.optimization_barrier((joined, *far))
    folded = members * own * (width // members) // AUX
    spread = project(joined, attention_out.T, folded, query_heads, head_size)
    first, second, spread, pair, *_ = lax.optimization_barrier((*far, spread, pair, *weights[-6:]))
    far = [first, second]
    weights += far + [across(w) for w in far]
    added = lax.all_to_all(spread, "tok", 0, 0, tiled=True)
    half = gate_weight.shape[1] // 2
    mlp_part, mixed = feed(added, embedded, mlp_gain[None], weights, half)
    mlp_rows = lax.all_to_all(mlp_part, "tok", 0, 0, tiled=True)
    own_rows = lax.optimization_barrier(lax.dynamic_slice_in_dim(mixed, member * own, own))
    hidden_out = (own_rows.astype(F32) + jnp.sum(mlp_rows.astype(F32), axis=0)).astype(BF)

    incoming = inverse_of(new_slot)
    local_targets = lax.dynamic_slice_in_dim(incoming, group_index * slots_dev, slots_dev)
    sources = jnp.take(current_slot, local_targets)
    held = [pair] + [turn(pair, by) for by in range(1, chips)]
    source_group = sources // slots_dev
    turns = (group_index // cores - source_group // cores) % chips
    other_core = (source_group % cores) != (group_index % cores)
    rows = sources % slots_dev + jnp.where(other_core, slots_dev, 0)
    new_states = pick_states(turns, rows, held, slots_dev)[:, None]
    return (hidden_out, new_states)


def solution(mesh):
    return jax.shard_map(
        local,
        mesh=mesh,
        in_specs=(
            P(),
            P(),
            P(),
            P(),
            P(),
            P(("req", "tok"), None),
            P(),
            P(),
            P(),
            P("req", "tok", None),
            P("req", "tok", None),
            P(None, "tok"),
            P(None, "tok"),
            P(None, "tok"),
            P(),
            P(None, "tok"),
            P("tok"),
            P("tok"),
            P("tok"),
            P("req", "tok", None, None),
            P("tok", None),
            P(),
            P(None, ("req", "tok")),
            P(None, ("req", "tok")),
            P(None, ("req", "tok")),
        ),
        out_specs=(P(("req", "tok"), None), P("req", "tok", None, None)),
        check_vma=False,
    )
```

```python
import functools

import jax
import jax.numpy as jnp
from jax import lax
from jax.experimental import pallas as pl
from jax.experimental.pallas import tpu as pltpu
from jax.sharding import Mesh
from jax.sharding import PartitionSpec as P

BF = jnp.bfloat16
F32 = jnp.float32
NEG = -1e30
AUX = 128
VMEM = 63 << 10


def inverse_of(mapping):
    places = jnp.arange(mapping.shape[0], dtype=jnp.int32)
    matches = mapping[None, :] == places[:, None]
    return jnp.sum(jnp.where(matches, places[None, :], 0), axis=1)


def dot_nn(a, b, precision=None):
    return lax.dot_general(
        a, b, (((1,), (0,)), ((), ())), precision=precision, preferred_element_type=F32
    )


def dot_nt(a, b, precision=None):
    return lax.dot_general(
        a, b, (((1,), (1,)), ((), ())), precision=precision, preferred_element_type=F32
    )


def dot_tn(a, b, precision=None):
    return lax.dot_general(
        a, b, (((0,), (0,)), ((), ())), precision=precision, preferred_element_type=F32
    )


HI = lax.Precision.HIGHEST
REQ = ("z", "core")
CORES = 2


def cost(flops, moved, special=0):
    return pl.CostEstimate(flops=flops, bytes_accessed=moved, transcendentals=special)


def lasting(microseconds):
    return cost(int(microseconds * 1e9), 1024)


def whole(shapes):
    return [pl.BlockSpec(a.shape, lambda i, n=len(a.shape): (0,) * n) for a in shapes]


def near(count):
    return [pl.BlockSpec(memory_space=pltpu.VMEM)] * count


def streamed(count):
    return [pl.BlockSpec(memory_space=pltpu.HBM)] * count


def scalars(count):
    return [pl.BlockSpec(memory_space=pltpu.SMEM)] * count


PARAMS = pltpu.CompilerParams(vmem_limit_bytes=VMEM << 10)
SMALL = pltpu.CompilerParams(vmem_limit_bytes=8 << 20)


def fetch_kernel(
    turn, slots_row, ids_cols, table_far, keep, give, places, origin, most, table, sem, *, groups, members
):
    load = pltpu.make_async_copy(table_far, table, sem)
    load.start()
    drafts, requests = ids_cols.shape
    vocab = table.shape[0]
    count = requests * drafts // groups
    slots = requests // groups
    core = lax.axis_index("core")
    group = lax.axis_index("z") * CORES + core
    member = lax.axis_index("tok")
    me = group * members + member
    now = turn[0]
    sub = lax.broadcasted_iota(jnp.int32, (count, count), 0)
    lane = lax.broadcasted_iota(jnp.int32, (count, count), 1)
    sub_c = sub[:, :1]
    lane_r = lane[:1, :]
    ids = ids_cols[...]
    ids_hi = (ids // 256).astype(F32).astype(BF)
    ids_lo = (ids % 256).astype(F32).astype(BF)
    row_slot = lax.broadcasted_iota(jnp.int32, (count, requests), 0) // drafts
    token = lax.broadcasted_iota(jnp.int32, (count, drafts), 0) % drafts
    token_lane = lax.broadcasted_iota(jnp.int32, (count, drafts), 1)
    column = lax.broadcasted_iota(jnp.int32, (members, count), 0)
    local_iota = lax.broadcasted_iota(jnp.int32, (members, vocab), 1)
    own = count // members
    hots = []
    own_place = jnp.zeros((count, 1), jnp.int32)
    own_from = [jnp.zeros((1, count), jnp.int32)] * own
    peak = jnp.zeros((1, count), jnp.int32)
    for n in range(groups):
        chips = groups // CORES
        g = (n % chips) * CORES + (core if n < chips else 1 - core)
        pick = jnp.where(slots_row[...] == row_slot + g * slots, 1.0, 0.0).astype(BF)
        mixed_ids = dot_nt(pick, ids_hi) * 256.0 + dot_nt(pick, ids_lo)
        id_c = jnp.sum(
            jnp.where(token == token_lane, mixed_ids, 0.0), axis=1, keepdims=True
        ).astype(jnp.int32)
        id_r = jnp.sum(jnp.where(sub == lane, id_c, 0), axis=0, keepdims=True)
        same = id_c == id_r
        first_c = jnp.min(jnp.where(same, lane, count), axis=1, keepdims=True)
        first_r = jnp.min(jnp.where(same, sub, count), axis=0, keepdims=True)
        owner_c = id_c // vocab
        owner_r = id_r // vocab
        chip_c = (owner_c // (CORES * members)) * members + owner_c % members
        chip_r = (owner_r // (CORES * members)) * members + owner_r % members
        alike = chip_c == chip_r
        before_r = (first_c == sub_c) & alike & (sub < first_r)
        less_r = (first_c == sub_c) & (chip_c < chip_r)
        nth_r = jnp.sum(jnp.where(before_r, 1, 0), axis=0, keepdims=True)
        rank_r = nth_r + jnp.sum(jnp.where(less_r, 1, 0), axis=0, keepdims=True)
        peak = jnp.maximum(peak, nth_r // members + 1)
        before_c = (first_r == lane_r) & alike & (lane < first_c)
        less_c = (first_r == lane_r) & (chip_r < chip_c)
        nth_c = jnp.sum(jnp.where(before_c, 1, 0), axis=1, keepdims=True)
        rank_c = nth_c + jnp.sum(jnp.where(less_c, 1, 0), axis=1, keepdims=True)
        spot = (rank_c % members) * own + rank_c // members
        spot = jnp.where(nth_c // members == now, spot, -1)
        own_place = jnp.where(group == g, spot, own_place)
        sent_r = (first_r == lane_r) & (nth_r // members == now)
        asked = sent_r & (owner_r == me) & (rank_r % members == column)
        row = jnp.sum(jnp.where(asked, id_r % vocab + 1, 0), axis=1, keepdims=True) - 1
        hots.append(jnp.where(local_iota == row, 1.0, 0.0))
        for k in range(own):
            here = sent_r & (rank_r == k * members + member) & (group == g)
            own_from[k] = own_from[k] + jnp.where(here, chip_r + 1, 0)
    places[...] = jnp.broadcast_to(own_place, places.shape)
    for k in range(own):
        origin[k] = jnp.sum(own_from[k]) - 1
    most[0] = jnp.max(peak)
    hot = jnp.concatenate(hots, axis=0).astype(BF)
    load.wait()
    peers = keep.shape[0]
    keep[...] = dot_nn(hot[:peers], table[...]).reshape(keep.shape).astype(BF)
    give[...] = dot_nn(hot[peers:], table[...]).reshape(give.shape).astype(BF)


def fetch(turn, slots_row, ids_cols, table, groups, members):
    count = ids_cols.size // groups
    rows = jax.ShapeDtypeStruct((groups // CORES * members, table.shape[1] // AUX, AUX), BF)
    outs = [
        rows,
        rows,
        jax.ShapeDtypeStruct((count, AUX), jnp.int32),
        jax.ShapeDtypeStruct((count // members,), jnp.int32),
        jax.ShapeDtypeStruct((1,), jnp.int32),
    ]
    return pl.pallas_call(
        functools.partial(fetch_kernel, groups=groups, members=members),
        grid=(1,),
        in_specs=scalars(1) + whole([slots_row, ids_cols]) + streamed(1),
        out_specs=whole(outs[:3]) + scalars(2),
        out_shape=outs,
        scratch_shapes=[pltpu.VMEM(table.shape, table.dtype), pltpu.SemaphoreType.DMA],
        compiler_params=PARAMS,
        cost_estimate=cost(2 * groups * members * table.size, 2 * table.size),
        name="fetch",
    )(turn, slots_row, ids_cols, table)


def hand_kernel(origin, came, spread):
    peers, own, lines = spread.shape[0], origin.shape[0], came.shape[1]
    for k in range(own):
        source = origin[k]
        row = came[jnp.maximum(source, 0)]
        row = jnp.where(source >= 0, row.astype(F32), 0.0).astype(BF)
        for j in range(peers):
            spread[j, k * lines : (k + 1) * lines, :] = row


def hand(origin, came, members):
    own = origin.shape[0]
    out = jax.ShapeDtypeStruct((members, own * came.shape[1], AUX), BF)
    return pl.pallas_call(
        hand_kernel,
        in_specs=scalars(1) + near(1),
        out_specs=near(1)[0],
        out_shape=out,
        compiler_params=SMALL,
        cost_estimate=lasting(10),
        name="hand",
    )(origin, came)


def rows_of(arrived, places):
    count = places.shape[0]
    width = arrived.size // count
    slot = lax.broadcasted_iota(jnp.int32, (count, count), 1)
    hot = jnp.where(slot == places[:, :1], 1.0, 0.0).astype(BF)
    lines = arrived[...].astype(F32).reshape(count, width // AUX, AUX)
    return dot_nn(hot, lines.reshape(count, width).astype(BF))


def place_kernel(arrived, places, before, out):
    out[...] = (before[...].astype(F32) + rows_of(arrived, places)).astype(BF)


def place(arrived, places, before):
    return pl.pallas_call(
        place_kernel,
        grid=(1,),
        in_specs=whole([arrived, places, before]),
        out_specs=whole([before])[0],
        out_shape=jax.ShapeDtypeStruct(before.shape, BF),
        compiler_params=PARAMS,
        name="place",
    )(arrived, places, before)


def attend_kernel(
    ints,
    arrived,
    places,
    extra,
    gain,
    query_weight,
    keyvalue_weight,
    keys,
    values,
    payload,
    embedded,
    normed,
    query_in,
    keyvalue_in,
    keys_in,
    values_in,
    sems,
):
    moves = []
    third = query_weight.shape[0] // 3
    for k in range(3):
        span = pl.ds(k * third, third)
        moves.append((query_weight.at[span, :], query_in.at[span, :]))
    moves += [(keyvalue_weight, keyvalue_in), (keys, keys_in), (values, values_in)]
    copies = [pltpu.make_async_copy(a, b, sems.at[n]) for n, (a, b) in enumerate(moves)]
    for copy in copies:
        copy.start()
    slots, cache, size = keys.shape
    tokens = extra.shape[0]
    drafts = tokens // slots
    heads = query_weight.shape[1] // size
    own = payload.shape[1]
    rows_in = (rows_of(arrived, places) + extra[...].astype(F32)).astype(BF)
    embedded[...] = rows_in
    wide = rows_in.astype(F32)
    factor = lax.rsqrt(jnp.mean(wide * wide, axis=-1, keepdims=True) + 1e-05)
    rows_norm = (wide * factor * gain[...]).astype(BF)
    normed[...] = rows_norm
    queries = None
    for k in range(3):
        copies[k].wait()
        span = slice(k * third, (k + 1) * third)
        part = dot_nn(rows_norm[:, span], query_in[span, :])
        queries = part if queries is None else queries + part
    queries = queries.astype(BF)
    copies[3].wait()
    keyvalue = dot_nn(rows_norm, keyvalue_in[...]).astype(BF)
    copies[4].wait()
    copies[5].wait()
    member = ints[8]
    scale = size ** (-0.5)
    rows = heads * drafts
    position = lax.broadcasted_iota(jnp.int32, (rows, cache), 1) + member * cache
    token = lax.broadcasted_iota(jnp.int32, (rows, drafts), 0) % drafts
    other = lax.broadcasted_iota(jnp.int32, (rows, drafts), 1)
    seen = other <= jnp.where(member == 0, token, -1)
    lane = lax.broadcasted_iota(jnp.int32, (drafts, AUX), 1)
    for slot in range(slots):
        span = slice(slot * drafts, (slot + 1) * drafts)
        length = ints[slot]
        query = jnp.concatenate(
            [queries[span, h * size : (h + 1) * size] for h in range(heads)], axis=0
        )
        scores = dot_nt(query, keys_in[slot]) * scale
        scores = jnp.where(position < length, scores, NEG)
        draft_scores = dot_nt(query, keyvalue[span, :size]) * scale
        draft_scores = jnp.where(seen, draft_scores, NEG)
        top = jnp.maximum(
            jnp.max(scores, axis=-1, keepdims=True),
            jnp.max(draft_scores, axis=-1, keepdims=True),
        )
        probs = jnp.where(position < length, jnp.exp(scores - top), 0.0)
        draft_probs = jnp.where(seen, jnp.exp(draft_scores - top), 0.0)
        total = jnp.sum(probs, axis=-1, keepdims=True) + jnp.sum(
            draft_probs, axis=-1, keepdims=True
        )
        summed = dot_nn(probs.astype(BF), values_in[slot]) + dot_nn(
            draft_probs.astype(BF), keyvalue[span, size:]
        )
        top_a = top.astype(BF).astype(F32)
        top_b = (top - top_a).astype(BF).astype(F32)
        top_c = top - top_a - top_b
        total_a = total.astype(BF).astype(F32)
        total_b = total - total_a
        aux = jnp.zeros((drafts, AUX), F32)
        for k, piece in enumerate((top_a, top_b, top_c, total_a, total_b)):
            for h in range(heads):
                part = piece[h * drafts : (h + 1) * drafts]
                aux = jnp.where(lane == k * heads + h, part, aux)
        flat = jnp.concatenate(
            [summed[h * drafts : (h + 1) * drafts] for h in range(heads)] + [aux], axis=1
        ).astype(BF)
        for q in range(drafts // own):
            payload[slot * (drafts // own) + q] = flat[q * own : (q + 1) * own]


def attend(ints, arrived, places, extra, gain, query_weight, keyvalue_weight, keys, values):
    tokens, width = extra.shape
    members = arrived.shape[0]
    wide = query_weight.shape[1] + AUX
    far = (query_weight, keyvalue_weight, keys, values)
    outs = [
        jax.ShapeDtypeStruct((members, tokens // members, wide), BF),
        jax.ShapeDtypeStruct((tokens, width), BF),
        jax.ShapeDtypeStruct((tokens, width), BF),
    ]
    return pl.pallas_call(
        attend_kernel,
        grid=(1,),
        in_specs=scalars(1) + whole([arrived, places, extra, gain]) + streamed(4),
        out_specs=whole(outs),
        out_shape=outs,
        scratch_shapes=[pltpu.VMEM(a.shape, a.dtype) for a in far]
        + [pltpu.SemaphoreType.DMA((6,))],
        compiler_params=PARAMS,
        cost_estimate=lasting(20),
        name="attend",
    )(ints, arrived, places, extra, gain, query_weight, keyvalue_weight, keys, values)


def fold(block):
    half = block.shape[0] // 2
    rest = jnp.concatenate([block[:half, AUX:], block[half:, AUX:]], axis=1)
    return jnp.concatenate([block[:, :AUX], rest], axis=0)


def unfold(block, tokens):
    half = AUX // 2
    rest = jnp.concatenate([block[tokens:, :half], block[tokens:, half:]], axis=0)
    return jnp.concatenate([block[:tokens], rest], axis=1)


def mamba_kernel(
    ints,
    reals,
    normed,
    input_weight,
    gate_weight,
    state_proj,
    step_row,
    states,
    mamba_out,
    blocks,
    chosen,
    proj_in,
    input_in,
    gate_in,
    states_in,
    out_in,
    sems,
):
    moves = (
        (state_proj, proj_in),
        (input_weight, input_in),
        (gate_weight, gate_in),
        (states, states_in),
        (mamba_out, out_in),
    )
    copies = [pltpu.make_async_copy(a, b, sems.at[n]) for n, (a, b) in enumerate(moves)]
    for copy in copies:
        copy.start()
    slots = states.shape[0]
    tokens = normed.shape[0]
    drafts = tokens // slots
    rows = normed[...]
    step_in = (
        jnp.sum(rows.astype(F32) * step_row[...].astype(F32), axis=1, keepdims=True) + reals[0]
    )
    sizes = jnp.maximum(step_in, 0.0) + jnp.log1p(jnp.exp(-jnp.abs(step_in)))
    copies[0].wait()
    both = dot_nn(rows, proj_in[...])
    copies[1].wait()
    x_all = dot_nn(rows, input_in[...])
    copies[2].wait()
    z_all = dot_nn(rows, gate_in[...])
    copies[3].wait()
    state_size = both.shape[1] // 2
    row = lax.broadcasted_iota(jnp.int32, (drafts, drafts), 0)
    col = lax.broadcasted_iota(jnp.int32, (drafts, drafts), 1)
    rows_in = lax.broadcasted_iota(jnp.int32, (drafts, 1), 0)
    gated = []
    for slot in range(slots):
        span = slice(slot * drafts, (slot + 1) * drafts)
        accept = ints[4 + slot]
        size_t = sizes[span]
        size_row = jnp.sum(jnp.where(row == col, size_t, 0.0), axis=0, keepdims=True)
        log_decay = -reals[1] * jnp.sum(
            jnp.where(col <= row, size_row, 0.0), axis=1, keepdims=True
        )
        log_row = jnp.sum(jnp.where(row == col, log_decay, 0.0), axis=0, keepdims=True)
        between = jnp.exp(jnp.where(col <= row, log_decay - log_row, NEG))
        state_in = both[span, :state_size]
        state_read = both[span, state_size:]
        x = x_all[span]
        z = z_all[span]
        inputs = size_t * x
        start = states_in[slot, 0]
        weights = dot_nt(state_read, state_in, HI) * between
        readout = dot_nn(weights, inputs, HI) + jnp.exp(log_decay) * dot_nt(
            state_read, start, HI
        )
        readout = readout + reals[2] * x
        last = jnp.sum(jnp.where(rows_in == accept - 1, log_decay, 0.0), axis=0, keepdims=True)
        remain = jnp.exp(jnp.where(rows_in < accept, last - log_decay, NEG))
        chosen[slot, 0] = (
            jnp.exp(last) * start + dot_tn(remain * inputs, state_in, HI)
        ).astype(BF)
        gated.append((readout * (z / (1.0 + jnp.exp(-z)))).astype(BF))
    copies[4].wait()
    part = dot_nn(jnp.concatenate(gated, axis=0), out_in[...])
    share = part.shape[1] // blocks.shape[0]
    for j in range(blocks.shape[0]):
        block = fold(part[:, j * share : (j + 1) * share]).astype(BF)
        blocks[j, : block.shape[0]] = block
        blocks[j, block.shape[0] :] = jnp.zeros_like(blocks[j, block.shape[0] :])


def mamba(
    ints,
    reals,
    normed,
    input_weight,
    gate_weight,
    state_proj,
    step_row,
    states,
    mamba_out,
    members,
    room,
):
    tokens = normed.shape[0]
    share = mamba_out.shape[1] // members
    outs = [
        jax.ShapeDtypeStruct((members, tokens * share // AUX + room, AUX), BF),
        jax.ShapeDtypeStruct(states.shape, BF),
    ]
    far = (state_proj, input_weight, gate_weight, states, mamba_out)
    return pl.pallas_call(
        mamba_kernel,
        grid=(1,),
        in_specs=scalars(2)
        + whole([normed])
        + streamed(3)
        + whole([step_row])
        + streamed(2),
        out_specs=whole(outs),
        out_shape=outs,
        scratch_shapes=[pltpu.VMEM(a.shape, a.dtype) for a in far]
        + [pltpu.SemaphoreType.DMA((5,))],
        compiler_params=PARAMS,
        cost_estimate=lasting(8),
        name="mamba",
    )(ints, reals, normed, input_weight, gate_weight, state_proj, step_row, states, mamba_out)


def join_kernel(parts, blocks, payload, piece, sem, *, heads, size):
    peers, own, _ = parts.shape
    rows = heads * own
    aux = parts[:, :, heads * size : heads * size + AUX].astype(F32)
    get = lambda k: aux[:, :, k * heads : (k + 1) * heads]
    top = get(0) + get(1) + get(2)
    total = get(3) + get(4)
    factors = jnp.exp(top - jnp.max(top, axis=0, keepdims=True))
    factors = factors / jnp.sum(factors * total, axis=0, keepdims=True)
    for h in range(heads):
        value = parts[:, :, h * size : (h + 1) * size].astype(F32)
        summed = jnp.sum(factors[:, :, h : h + 1] * value, axis=0)
        piece[h * own : (h + 1) * own, :] = summed.astype(BF)
    first = payload.shape[1] - rows
    copies = [
        pltpu.make_async_copy(piece, payload.at[j, pl.ds(first, rows), :], sem.at[j])
        for j in range(peers)
    ]
    for copy in copies:
        copy.start()
    for copy in copies:
        copy.wait()


def join(parts, blocks, heads, size):
    peers, own, _ = parts.shape
    return pl.pallas_call(
        functools.partial(join_kernel, heads=heads, size=size),
        grid=(1,),
        in_specs=whole([parts]) + streamed(1),
        out_specs=streamed(1)[0],
        out_shape=jax.ShapeDtypeStruct(blocks.shape, BF),
        input_output_aliases={1: 0},
        scratch_shapes=[
            pltpu.VMEM((heads * own, size), BF),
            pltpu.SemaphoreType.DMA((peers,)),
        ],
        compiler_params=PARAMS,
        cost_estimate=lasting(20),
        name="join",
    )(parts, blocks)


def project_kernel(parts, out_weight, spread, *, heads, size):
    peers, packed, _ = spread.shape
    own = (parts.shape[1] - packed) // heads
    tokens = own * peers
    acc = unfold(jnp.sum(parts[:, :packed, :].astype(F32), axis=0), tokens)
    for h in range(heads):
        attended = jnp.concatenate(
            [parts[j, packed + h * own : packed + (h + 1) * own, :size] for j in range(peers)],
            axis=0,
        )
        acc = acc + dot_nt(attended, out_weight[:, h * size : (h + 1) * size])
    out = fold(acc).astype(BF)
    for j in range(peers):
        spread[j] = out


def project(parts, out_weight, packed, heads, size):
    members = parts.shape[0]
    out = jax.ShapeDtypeStruct((members, packed, AUX), BF)
    return pl.pallas_call(
        functools.partial(project_kernel, heads=heads, size=size),
        grid=(1,),
        in_specs=whole([parts, out_weight]),
        out_specs=whole([out])[0],
        out_shape=out,
        compiler_params=PARAMS,
        cost_estimate=lasting(20),
        name="project",
    )(parts, out_weight)


def load_units(weights, gates, ups, downs, sems, units):
    copies = []
    begin = 0
    for w in weights:
        for first in range(0, w.shape[0], 3 * units):
            trio = []
            for k, to in enumerate((gates, ups, downs)):
                copy = pltpu.make_async_copy(
                    w.at[pl.ds(first + k * units, units), :],
                    to.at[pl.ds(begin, units), :],
                    sems.at[len(copies), k],
                )
                copy.start()
                trio.append(copy)
            begin += units
            copies.append((begin, trio))
    return copies


def use_units(second, copies, gates, ups, downs, chunk=256):
    acc = None
    ready = 0
    waiting = list(copies)
    for first in range(0, gates.shape[0], chunk):
        while ready < first + chunk:
            ready, trio = waiting.pop(0)
            for copy in trio:
                copy.wait()
        span = slice(first, first + chunk)
        gate = dot_nt(second, gates[span, :])
        up = dot_nt(second, ups[span, :])
        hidden = (gate / (1.0 + jnp.exp(-gate)) * up).astype(BF)
        part = dot_nn(hidden, downs[span, :])
        acc = part if acc is None else acc + part
    return acc


def feed_kernel(spread, embedded, gain, *refs, count, units):
    weights = refs[:count]
    out, mixed, gates, ups, downs, sems = refs[count:]
    copies = load_units(weights, gates, ups, downs, sems, units)
    tokens = embedded.shape[0]
    peers, own, _ = out.shape
    added = jnp.concatenate([unfold(spread[j].astype(F32), tokens) for j in range(peers)], axis=1)
    rows = (embedded[...].astype(F32) + added).astype(BF)
    mixed[...] = rows
    wide = rows.astype(F32)
    factor = lax.rsqrt(jnp.mean(wide * wide, axis=-1, keepdims=True) + 1e-05)
    rows_norm = (wide * factor * gain[...]).astype(BF)
    acc = use_units(rows_norm, copies, gates, ups, downs)
    for j in range(peers):
        out[j] = acc[j * own : (j + 1) * own, :].astype(BF)


def unit_scratch(weights, units):
    width = weights[0].shape[1]
    rows = sum(w.shape[0] for w in weights)
    count = rows // (3 * units)
    return [pltpu.VMEM((rows // 3, width), BF)] * 3 + [pltpu.SemaphoreType.DMA((count, 3))]


def feed(spread, embedded, gain, weights, units):
    members = spread.shape[0]
    tokens, width = embedded.shape
    outs = [
        jax.ShapeDtypeStruct((members, tokens // members, width), BF),
        jax.ShapeDtypeStruct(embedded.shape, BF),
    ]
    return pl.pallas_call(
        functools.partial(feed_kernel, count=len(weights), units=units),
        grid=(1,),
        in_specs=whole([spread, embedded, gain]) + streamed(len(weights)),
        out_specs=whole(outs),
        out_shape=outs,
        scratch_shapes=unit_scratch(weights, units),
        compiler_params=PARAMS,
        cost_estimate=lasting(20),
        name="feed",
    )(spread, embedded, gain, *weights)


def pack_kernel(gate, up, down, ready, low, high):
    half = low.shape[0] // 3
    for k, part in enumerate((gate, up, down)):
        low[k * half : (k + 1) * half] = part[:half]
        high[k * half : (k + 1) * half] = part[half:]


def pack(gate, up, down, ready):
    units, width = gate.shape
    out = jax.ShapeDtypeStruct((3 * units // 2, width), gate.dtype)
    return pl.pallas_call(
        pack_kernel,
        grid=(1,),
        in_specs=whole([gate, up, down]) + streamed(1),
        out_specs=whole([out, out]),
        out_shape=[out, out],
        compiler_params=PARAMS,
        cost_estimate=cost(0, 1024),
        name="pack",
    )(gate, up, down, ready)


def pick_kernel(turns, rows, *refs):
    held = refs[:-1]
    out = refs[-1]
    for i in range(out.shape[0]):
        for n, ref in enumerate(held):

            @pl.when(turns[i] == n)
            def _():
                out[i] = ref[rows[i]].astype(F32)


def pick_states(turns, rows, held, count):
    shape = (count,) + held[0].shape[1:]
    out = jax.ShapeDtypeStruct(shape, F32)
    return pl.pallas_call(
        pick_kernel,
        grid=(1,),
        in_specs=scalars(2) + whole(held),
        out_specs=whole([out])[0],
        out_shape=out,
        compiler_params=PARAMS,
        name="pick",
    )(turns, rows, *held)


def local(
    draft_ids,
    lengths,
    current_slot,
    new_slot,
    accepted,
    embed_table,
    mixer_gain,
    query_weight,
    keyvalue_weight,
    key_cache,
    value_cache,
    attention_out,
    mamba_input,
    mamba_gate,
    state_proj,
    mamba_step,
    step_bias,
    decay_log,
    skip_gain,
    states,
    mamba_out,
    mlp_gain,
    gate_weight,
    up_weight,
    down_weight,
):
    members = lax.axis_size("tok")
    groups = lax.axis_size(REQ)
    group_index = lax.axis_index(REQ)
    member = lax.axis_index("tok")
    slots_dev, cache_dev, head_size = key_cache.shape
    draft_len = draft_ids.shape[1]
    width = embed_table.shape[1]
    query_heads = query_weight.shape[1] // head_size
    own = slots_dev * draft_len // members

    cores = CORES
    chips = groups // cores

    def turn(value, by):
        return lax.ppermute(
            value, REQ, [(g, (g + by * cores) % groups) for g in range(groups)]
        )

    def across(value):
        return lax.ppermute(value, REQ, [(g, g ^ 1) for g in range(groups)])

    def exchange(turn):
        keep, give, places, origin, most = fetch(
            turn, current_slot[None], draft_ids.T, embed_table, groups, members
        )
        came = lax.all_to_all(keep + across(give), ("z", "tok"), 0, 0, tiled=True)
        return came, places, origin, most

    def plane(rows):
        return lax.all_to_all(rows, "tok", 0, 0, tiled=True)

    came, places, origin, most = exchange(jnp.zeros((1,), jnp.int32))

    low, high = pack(gate_weight.T, up_weight.T, down_weight.T, places)
    near_z = [turn(low, 1), turn(high, -1), turn(high, 1), turn(low, -1)]
    handed = hand(origin, came, members)
    weights = [low, high] + near_z
    arrived = plane(handed)

    def more(carry):
        return carry[0][0] < most[0]

    def round_of(carry):
        at, rows = carry
        later, spots, froms, _ = exchange(at)
        return at + 1, place(plane(hand(froms, later, members)), spots, rows)

    _, extra = lax.while_loop(
        more, round_of, (jnp.ones((1,), jnp.int32), jnp.zeros((members * own, width), BF))
    )

    slot_owner = inverse_of(current_slot)
    local_owner = lax.dynamic_slice_in_dim(slot_owner, group_index * slots_dev, slots_dev)
    ints = jnp.concatenate(
        [jnp.take(lengths, local_owner), jnp.take(accepted, local_owner), member[None]]
    )
    reals = jnp.concatenate([step_bias, jnp.exp(decay_log), skip_gain])
    payload, embedded, normed = attend(
        ints,
        arrived,
        places,
        extra,
        mixer_gain[None],
        query_weight,
        keyvalue_weight,
        key_cache,
        value_cache,
    )
    parts = lax.all_to_all(payload, "tok", 0, 0, tiled=True)
    blocks, chosen = mamba(
        ints,
        reals,
        normed,
        mamba_input,
        mamba_gate,
        state_proj,
        mamba_step.T,
        states,
        mamba_out,
        members,
        query_heads * own,
    )
    later = lax.optimization_barrier((near_z[0], near_z[1], blocks))
    far = [turn(later[0], 1), turn(later[1], -1)]
    joint = join(parts, blocks, query_heads, head_size)
    joined = lax.all_to_all(joint, "tok", 0, 0, tiled=True)
    *later, chosen, _ = lax.optimization_barrier((*weights, chosen, joint))
    weights += [across(w) for w in later]
    chosen = chosen[:, 0]
    pair = jnp.concatenate([chosen, across(chosen)], axis=0)
    joined, *_ = lax.optimization_barrier((joined, *far))
    folded = members * own * (width // members) // AUX
    spread = project(joined, attention_out.T, folded, query_heads, head_size)
    first, second, spread, pair, *_ = lax.optimization_barrier((*far, spread, pair, *weights[-6:]))
    far = [first, second]
    weights += far + [across(w) for w in far]
    added = lax.all_to_all(spread, "tok", 0, 0, tiled=True)
    half = gate_weight.shape[1] // 2
    mlp_part, mixed = feed(added, embedded, mlp_gain[None], weights, half)
    mlp_rows = lax.all_to_all(mlp_part, "tok", 0, 0, tiled=True)
    own_rows = lax.optimization_barrier(lax.dynamic_slice_in_dim(mixed, member * own, own))
    hidden_out = (own_rows.astype(F32) + jnp.sum(mlp_rows.astype(F32), axis=0)).astype(BF)

    incoming = inverse_of(new_slot)
    local_targets = lax.dynamic_slice_in_dim(incoming, group_index * slots_dev, slots_dev)
    sources = jnp.take(current_slot, local_targets)
    held = [pair] + [turn(pair, by) for by in range(1, chips)]
    source_group = sources // slots_dev
    turns = (group_index // cores - source_group // cores) % chips
    other_core = (source_group % cores) != (group_index % cores)
    rows = sources % slots_dev + jnp.where(other_core, slots_dev, 0)
    new_states = pick_states(turns, rows, held, slots_dev)[:, None]
    return (hidden_out, new_states)


def solution(mesh):
    groups, members = mesh.devices.shape
    devices = mesh.devices.reshape(groups // CORES, CORES, members)
    mesh = Mesh(devices, ("z", "core", "tok"))
    return jax.shard_map(
        local,
        mesh=mesh,
        in_specs=(
            P(),
            P(),
            P(),
            P(),
            P(),
            P(("z", "core", "tok"), None),
            P(),
            P(),
            P(),
            P(REQ, "tok", None),
            P(REQ, "tok", None),
            P(None, "tok"),
            P(None, "tok"),
            P(None, "tok"),
            P(),
            P(None, "tok"),
            P("tok"),
            P("tok"),
            P("tok"),
            P(REQ, "tok", None, None),
            P("tok", None),
            P(),
            P(None, ("z", "core", "tok")),
            P(None, ("z", "core", "tok")),
            P(None, ("z", "core", "tok")),
        ),
        out_specs=(P(("z", "core", "tok"), None), P(REQ, "tok", None, None)),
        check_vma=False,
    )
```

```python
import functools

import jax
import jax.numpy as jnp
from jax import lax
from jax.experimental import pallas as pl
from jax.experimental.pallas import tpu as pltpu
from jax.sharding import Mesh
from jax.sharding import PartitionSpec as P

BF = jnp.bfloat16
F32 = jnp.float32
NEG = -1e30
AUX = 128
VMEM = 63 << 10


def inverse_of(mapping):
    places = jnp.arange(mapping.shape[0], dtype=jnp.int32)
    matches = mapping[None, :] == places[:, None]
    return jnp.sum(jnp.where(matches, places[None, :], 0), axis=1)


def dot_nn(a, b, precision=None):
    return lax.dot_general(
        a, b, (((1,), (0,)), ((), ())), precision=precision, preferred_element_type=F32
    )


def dot_nt(a, b, precision=None):
    return lax.dot_general(
        a, b, (((1,), (1,)), ((), ())), precision=precision, preferred_element_type=F32
    )


def dot_tn(a, b, precision=None):
    return lax.dot_general(
        a, b, (((0,), (0,)), ((), ())), precision=precision, preferred_element_type=F32
    )


HI = lax.Precision.HIGHEST
REQ = ("z", "core")
CORES = 2


def cost(flops, moved, special=0):
    return pl.CostEstimate(flops=flops, bytes_accessed=moved, transcendentals=special)


def lasting(microseconds):
    return cost(int(microseconds * 1e9), 1024)


def whole(shapes):
    return [pl.BlockSpec(a.shape, lambda i, n=len(a.shape): (0,) * n) for a in shapes]


def near(count):
    return [pl.BlockSpec(memory_space=pltpu.VMEM)] * count


def streamed(count):
    return [pl.BlockSpec(memory_space=pltpu.HBM)] * count


def scalars(count):
    return [pl.BlockSpec(memory_space=pltpu.SMEM)] * count


PARAMS = pltpu.CompilerParams(vmem_limit_bytes=VMEM << 10)
SMALL = pltpu.CompilerParams(vmem_limit_bytes=8 << 20)


def fetch_kernel(
    turn, slots_row, ids_cols, table_far, keep, give, places, origin, most, table, sem, *, groups, members
):
    load = pltpu.make_async_copy(table_far, table, sem)
    load.start()
    drafts, requests = ids_cols.shape
    vocab = table.shape[0]
    count = requests * drafts // groups
    slots = requests // groups
    core = lax.axis_index("core")
    group = lax.axis_index("z") * CORES + core
    member = lax.axis_index("tok")
    me = group * members + member
    now = turn[0]
    sub = lax.broadcasted_iota(jnp.int32, (count, count), 0)
    lane = lax.broadcasted_iota(jnp.int32, (count, count), 1)
    sub_c = sub[:, :1]
    lane_r = lane[:1, :]
    ids = ids_cols[...]
    ids_hi = (ids // 256).astype(F32).astype(BF)
    ids_lo = (ids % 256).astype(F32).astype(BF)
    row_slot = lax.broadcasted_iota(jnp.int32, (count, requests), 0) // drafts
    token = lax.broadcasted_iota(jnp.int32, (count, drafts), 0) % drafts
    token_lane = lax.broadcasted_iota(jnp.int32, (count, drafts), 1)
    column = lax.broadcasted_iota(jnp.int32, (members, count), 0)
    local_iota = lax.broadcasted_iota(jnp.int32, (members, vocab), 1)
    own = count // members
    hots = []
    own_place = jnp.zeros((count, 1), jnp.int32)
    own_from = [jnp.zeros((1, count), jnp.int32)] * own
    peak = jnp.zeros((1, count), jnp.int32)
    for n in range(groups):
        chips = groups // CORES
        g = (n % chips) * CORES + (core if n < chips else 1 - core)
        pick = jnp.where(slots_row[...] == row_slot + g * slots, 1.0, 0.0).astype(BF)
        mixed_ids = dot_nt(pick, ids_hi) * 256.0 + dot_nt(pick, ids_lo)
        id_c = jnp.sum(
            jnp.where(token == token_lane, mixed_ids, 0.0), axis=1, keepdims=True
        ).astype(jnp.int32)
        id_r = jnp.sum(jnp.where(sub == lane, id_c, 0), axis=0, keepdims=True)
        same = id_c == id_r
        first_c = jnp.min(jnp.where(same, lane, count), axis=1, keepdims=True)
        first_r = jnp.min(jnp.where(same, sub, count), axis=0, keepdims=True)
        owner_c = id_c // vocab
        owner_r = id_r // vocab
        chip_c = (owner_c // (CORES * members)) * members + owner_c % members
        chip_r = (owner_r // (CORES * members)) * members + owner_r % members
        alike = chip_c == chip_r
        before_r = (first_c == sub_c) & alike & (sub < first_r)
        less_r = (first_c == sub_c) & (chip_c < chip_r)
        nth_r = jnp.sum(jnp.where(before_r, 1, 0), axis=0, keepdims=True)
        rank_r = nth_r + jnp.sum(jnp.where(less_r, 1, 0), axis=0, keepdims=True)
        peak = jnp.maximum(peak, nth_r // members + 1)
        before_c = (first_r == lane_r) & alike & (lane < first_c)
        less_c = (first_r == lane_r) & (chip_r < chip_c)
        nth_c = jnp.sum(jnp.where(before_c, 1, 0), axis=1, keepdims=True)
        rank_c = nth_c + jnp.sum(jnp.where(less_c, 1, 0), axis=1, keepdims=True)
        spot = (rank_c % members) * own + rank_c // members
        spot = jnp.where(nth_c // members == now, spot, -1)
        own_place = jnp.where(group == g, spot, own_place)
        sent_r = (first_r == lane_r) & (nth_r // members == now)
        asked = sent_r & (owner_r == me) & (rank_r % members == column)
        row = jnp.sum(jnp.where(asked, id_r % vocab + 1, 0), axis=1, keepdims=True) - 1
        hots.append(jnp.where(local_iota == row, 1.0, 0.0))
        for k in range(own):
            here = sent_r & (rank_r == k * members + member) & (group == g)
            own_from[k] = own_from[k] + jnp.where(here, chip_r + 1, 0)
    places[...] = jnp.broadcast_to(own_place, places.shape)
    for k in range(own):
        origin[k] = jnp.sum(own_from[k]) - 1
    most[0] = jnp.max(peak)
    hot = jnp.concatenate(hots, axis=0).astype(BF)
    load.wait()
    peers = keep.shape[0]
    keep[...] = dot_nn(hot[:peers], table[...]).reshape(keep.shape).astype(BF)
    give[...] = dot_nn(hot[peers:], table[...]).reshape(give.shape).astype(BF)


def fetch(turn, slots_row, ids_cols, table, groups, members):
    count = ids_cols.size // groups
    rows = jax.ShapeDtypeStruct((groups // CORES * members, table.shape[1] // AUX, AUX), BF)
    outs = [
        rows,
        rows,
        jax.ShapeDtypeStruct((count, AUX), jnp.int32),
        jax.ShapeDtypeStruct((count // members,), jnp.int32),
        jax.ShapeDtypeStruct((1,), jnp.int32),
    ]
    return pl.pallas_call(
        functools.partial(fetch_kernel, groups=groups, members=members),
        grid=(1,),
        in_specs=scalars(1) + whole([slots_row, ids_cols]) + streamed(1),
        out_specs=whole(outs[:3]) + scalars(2),
        out_shape=outs,
        scratch_shapes=[pltpu.VMEM(table.shape, table.dtype), pltpu.SemaphoreType.DMA],
        compiler_params=PARAMS,
        cost_estimate=cost(2 * groups * members * table.size, 2 * table.size),
        name="fetch",
    )(turn, slots_row, ids_cols, table)


def hand_kernel(origin, came, spread):
    peers, own, lines = spread.shape[0], origin.shape[0], came.shape[1]
    for k in range(own):
        source = origin[k]
        row = came[jnp.maximum(source, 0)]
        row = jnp.where(source >= 0, row.astype(F32), 0.0).astype(BF)
        for j in range(peers):
            spread[j, k * lines : (k + 1) * lines, :] = row


def hand(origin, came, members):
    own = origin.shape[0]
    out = jax.ShapeDtypeStruct((members, own * came.shape[1], AUX), BF)
    return pl.pallas_call(
        hand_kernel,
        in_specs=scalars(1) + near(1),
        out_specs=near(1)[0],
        out_shape=out,
        compiler_params=SMALL,
        cost_estimate=lasting(10),
        name="hand",
    )(origin, came)


def rows_of(arrived, places):
    count = places.shape[0]
    width = arrived.size // count
    slot = lax.broadcasted_iota(jnp.int32, (count, count), 1)
    hot = jnp.where(slot == places[:, :1], 1.0, 0.0).astype(BF)
    lines = arrived[...].astype(F32).reshape(count, width // AUX, AUX)
    return dot_nn(hot, lines.reshape(count, width).astype(BF))


def place_kernel(arrived, places, before, out):
    out[...] = (before[...].astype(F32) + rows_of(arrived, places)).astype(BF)


def place(arrived, places, before):
    return pl.pallas_call(
        place_kernel,
        grid=(1,),
        in_specs=whole([arrived, places, before]),
        out_specs=whole([before])[0],
        out_shape=jax.ShapeDtypeStruct(before.shape, BF),
        compiler_params=PARAMS,
        name="place",
    )(arrived, places, before)


def attend_kernel(
    ints,
    arrived,
    places,
    extra,
    gain,
    query_weight,
    keyvalue_weight,
    keys,
    values,
    payload,
    embedded,
    normed,
    query_in,
    keyvalue_in,
    keys_in,
    values_in,
    sems,
):
    moves = []
    third = query_weight.shape[0] // 3
    for k in range(3):
        span = pl.ds(k * third, third)
        moves.append((query_weight.at[span, :], query_in.at[span, :]))
    moves += [(keyvalue_weight, keyvalue_in), (keys, keys_in), (values, values_in)]
    copies = [pltpu.make_async_copy(a, b, sems.at[n]) for n, (a, b) in enumerate(moves)]
    for copy in copies:
        copy.start()
    slots, cache, size = keys.shape
    tokens = extra.shape[0]
    drafts = tokens // slots
    heads = query_weight.shape[1] // size
    own = payload.shape[1]
    rows_in = (rows_of(arrived, places) + extra[...].astype(F32)).astype(BF)
    embedded[...] = rows_in
    wide = rows_in.astype(F32)
    factor = lax.rsqrt(jnp.mean(wide * wide, axis=-1, keepdims=True) + 1e-05)
    rows_norm = (wide * factor * gain[...]).astype(BF)
    normed[...] = rows_norm
    queries = None
    for k in range(3):
        copies[k].wait()
        span = slice(k * third, (k + 1) * third)
        part = dot_nn(rows_norm[:, span], query_in[span, :])
        queries = part if queries is None else queries + part
    queries = queries.astype(BF)
    copies[3].wait()
    keyvalue = dot_nn(rows_norm, keyvalue_in[...]).astype(BF)
    copies[4].wait()
    copies[5].wait()
    member = ints[8]
    scale = size ** (-0.5)
    rows = heads * drafts
    position = lax.broadcasted_iota(jnp.int32, (rows, cache), 1) + member * cache
    token = lax.broadcasted_iota(jnp.int32, (rows, drafts), 0) % drafts
    other = lax.broadcasted_iota(jnp.int32, (rows, drafts), 1)
    seen = other <= jnp.where(member == 0, token, -1)
    lane = lax.broadcasted_iota(jnp.int32, (drafts, AUX), 1)
    for slot in range(slots):
        span = slice(slot * drafts, (slot + 1) * drafts)
        length = ints[slot]
        query = jnp.concatenate(
            [queries[span, h * size : (h + 1) * size] for h in range(heads)], axis=0
        )
        scores = dot_nt(query, keys_in[slot]) * scale
        scores = jnp.where(position < length, scores, NEG)
        draft_scores = dot_nt(query, keyvalue[span, :size]) * scale
        draft_scores = jnp.where(seen, draft_scores, NEG)
        top = jnp.maximum(
            jnp.max(scores, axis=-1, keepdims=True),
            jnp.max(draft_scores, axis=-1, keepdims=True),
        )
        probs = jnp.where(position < length, jnp.exp(scores - top), 0.0)
        draft_probs = jnp.where(seen, jnp.exp(draft_scores - top), 0.0)
        total = jnp.sum(probs, axis=-1, keepdims=True) + jnp.sum(
            draft_probs, axis=-1, keepdims=True
        )
        summed = dot_nn(probs.astype(BF), values_in[slot]) + dot_nn(
            draft_probs.astype(BF), keyvalue[span, size:]
        )
        top_a = top.astype(BF).astype(F32)
        top_b = (top - top_a).astype(BF).astype(F32)
        top_c = top - top_a - top_b
        total_a = total.astype(BF).astype(F32)
        total_b = total - total_a
        aux = jnp.zeros((drafts, AUX), F32)
        for k, piece in enumerate((top_a, top_b, top_c, total_a, total_b)):
            for h in range(heads):
                part = piece[h * drafts : (h + 1) * drafts]
                aux = jnp.where(lane == k * heads + h, part, aux)
        flat = jnp.concatenate(
            [summed[h * drafts : (h + 1) * drafts] for h in range(heads)] + [aux], axis=1
        ).astype(BF)
        for q in range(drafts // own):
            payload[slot * (drafts // own) + q] = flat[q * own : (q + 1) * own]


def attend(ints, arrived, places, extra, gain, query_weight, keyvalue_weight, keys, values):
    tokens, width = extra.shape
    members = arrived.shape[0]
    wide = query_weight.shape[1] + AUX
    far = (query_weight, keyvalue_weight, keys, values)
    outs = [
        jax.ShapeDtypeStruct((members, tokens // members, wide), BF),
        jax.ShapeDtypeStruct((tokens, width), BF),
        jax.ShapeDtypeStruct((tokens, width), BF),
    ]
    return pl.pallas_call(
        attend_kernel,
        grid=(1,),
        in_specs=scalars(1) + whole([arrived, places, extra, gain]) + streamed(4),
        out_specs=whole(outs),
        out_shape=outs,
        scratch_shapes=[pltpu.VMEM(a.shape, a.dtype) for a in far]
        + [pltpu.SemaphoreType.DMA((6,))],
        compiler_params=PARAMS,
        cost_estimate=lasting(20),
        name="attend",
    )(ints, arrived, places, extra, gain, query_weight, keyvalue_weight, keys, values)


def fold(block):
    half = block.shape[0] // 2
    rest = jnp.concatenate([block[:half, AUX:], block[half:, AUX:]], axis=1)
    return jnp.concatenate([block[:, :AUX], rest], axis=0)


def unfold(block, tokens):
    half = AUX // 2
    rest = jnp.concatenate([block[tokens:, :half], block[tokens:, half:]], axis=0)
    return jnp.concatenate([block[:tokens], rest], axis=1)


def mamba_kernel(
    ints,
    reals,
    normed,
    input_weight,
    gate_weight,
    state_proj,
    step_row,
    states,
    mamba_out,
    blocks,
    chosen,
    proj_in,
    input_in,
    gate_in,
    states_in,
    out_in,
    sems,
):
    moves = (
        (state_proj, proj_in),
        (input_weight, input_in),
        (gate_weight, gate_in),
        (states, states_in),
        (mamba_out, out_in),
    )
    copies = [pltpu.make_async_copy(a, b, sems.at[n]) for n, (a, b) in enumerate(moves)]
    for copy in copies:
        copy.start()
    slots = states.shape[0]
    tokens = normed.shape[0]
    drafts = tokens // slots
    rows = normed[...]
    step_in = (
        jnp.sum(rows.astype(F32) * step_row[...].astype(F32), axis=1, keepdims=True) + reals[0]
    )
    sizes = jnp.maximum(step_in, 0.0) + jnp.log1p(jnp.exp(-jnp.abs(step_in)))
    copies[0].wait()
    both = dot_nn(rows, proj_in[...])
    copies[1].wait()
    x_all = dot_nn(rows, input_in[...])
    copies[2].wait()
    z_all = dot_nn(rows, gate_in[...])
    copies[3].wait()
    state_size = both.shape[1] // 2
    row = lax.broadcasted_iota(jnp.int32, (drafts, drafts), 0)
    col = lax.broadcasted_iota(jnp.int32, (drafts, drafts), 1)
    rows_in = lax.broadcasted_iota(jnp.int32, (drafts, 1), 0)
    gated = []
    for slot in range(slots):
        span = slice(slot * drafts, (slot + 1) * drafts)
        accept = ints[4 + slot]
        size_t = sizes[span]
        size_row = jnp.sum(jnp.where(row == col, size_t, 0.0), axis=0, keepdims=True)
        log_decay = -reals[1] * jnp.sum(
            jnp.where(col <= row, size_row, 0.0), axis=1, keepdims=True
        )
        log_row = jnp.sum(jnp.where(row == col, log_decay, 0.0), axis=0, keepdims=True)
        between = jnp.exp(jnp.where(col <= row, log_decay - log_row, NEG))
        state_in = both[span, :state_size]
        state_read = both[span, state_size:]
        x = x_all[span]
        z = z_all[span]
        inputs = size_t * x
        start = states_in[slot, 0]
        weights = dot_nt(state_read, state_in, HI) * between
        readout = dot_nn(weights, inputs, HI) + jnp.exp(log_decay) * dot_nt(
            state_read, start, HI
        )
        readout = readout + reals[2] * x
        last = jnp.sum(jnp.where(rows_in == accept - 1, log_decay, 0.0), axis=0, keepdims=True)
        remain = jnp.exp(jnp.where(rows_in < accept, last - log_decay, NEG))
        chosen[slot, 0] = (
            jnp.exp(last) * start + dot_tn(remain * inputs, state_in, HI)
        ).astype(BF)
        gated.append((readout * (z / (1.0 + jnp.exp(-z)))).astype(BF))
    copies[4].wait()
    part = dot_nn(jnp.concatenate(gated, axis=0), out_in[...])
    share = part.shape[1] // blocks.shape[0]
    for j in range(blocks.shape[0]):
        block = fold(part[:, j * share : (j + 1) * share]).astype(BF)
        blocks[j, : block.shape[0]] = block
        blocks[j, block.shape[0] :] = jnp.zeros_like(blocks[j, block.shape[0] :])


def mamba(
    ints,
    reals,
    normed,
    input_weight,
    gate_weight,
    state_proj,
    step_row,
    states,
    mamba_out,
    members,
    room,
):
    tokens = normed.shape[0]
    share = mamba_out.shape[1] // members
    outs = [
        jax.ShapeDtypeStruct((members, tokens * share // AUX + room, AUX), BF),
        jax.ShapeDtypeStruct(states.shape, BF),
    ]
    far = (state_proj, input_weight, gate_weight, states, mamba_out)
    return pl.pallas_call(
        mamba_kernel,
        grid=(1,),
        in_specs=scalars(2)
        + whole([normed])
        + streamed(3)
        + whole([step_row])
        + streamed(2),
        out_specs=whole(outs),
        out_shape=outs,
        scratch_shapes=[pltpu.VMEM(a.shape, a.dtype) for a in far]
        + [pltpu.SemaphoreType.DMA((5,))],
        compiler_params=PARAMS,
        cost_estimate=lasting(8),
        name="mamba",
    )(ints, reals, normed, input_weight, gate_weight, state_proj, step_row, states, mamba_out)


def join_kernel(parts, blocks, payload, piece, sem, *, heads, size):
    peers, own, _ = parts.shape
    rows = heads * own
    aux = parts[:, :, heads * size : heads * size + AUX].astype(F32)
    get = lambda k: aux[:, :, k * heads : (k + 1) * heads]
    top = get(0) + get(1) + get(2)
    total = get(3) + get(4)
    factors = jnp.exp(top - jnp.max(top, axis=0, keepdims=True))
    factors = factors / jnp.sum(factors * total, axis=0, keepdims=True)
    for h in range(heads):
        value = parts[:, :, h * size : (h + 1) * size].astype(F32)
        summed = jnp.sum(factors[:, :, h : h + 1] * value, axis=0)
        piece[h * own : (h + 1) * own, :] = summed.astype(BF)
    first = payload.shape[1] - rows
    copies = [
        pltpu.make_async_copy(piece, payload.at[j, pl.ds(first, rows), :], sem.at[j])
        for j in range(peers)
    ]
    for copy in copies:
        copy.start()
    for copy in copies:
        copy.wait()


def join(parts, blocks, heads, size):
    peers, own, _ = parts.shape
    return pl.pallas_call(
        functools.partial(join_kernel, heads=heads, size=size),
        grid=(1,),
        in_specs=whole([parts]) + streamed(1),
        out_specs=streamed(1)[0],
        out_shape=jax.ShapeDtypeStruct(blocks.shape, BF),
        input_output_aliases={1: 0},
        scratch_shapes=[
            pltpu.VMEM((heads * own, size), BF),
            pltpu.SemaphoreType.DMA((peers,)),
        ],
        compiler_params=PARAMS,
        cost_estimate=lasting(20),
        name="join",
    )(parts, blocks)


def project_kernel(parts, out_weight, spread, *, heads, size):
    peers, packed, _ = spread.shape
    own = (parts.shape[1] - packed) // heads
    tokens = own * peers
    acc = unfold(jnp.sum(parts[:, :packed, :].astype(F32), axis=0), tokens)
    for h in range(heads):
        attended = jnp.concatenate(
            [parts[j, packed + h * own : packed + (h + 1) * own, :size] for j in range(peers)],
            axis=0,
        )
        acc = acc + dot_nt(attended, out_weight[:, h * size : (h + 1) * size])
    out = fold(acc).astype(BF)
    for j in range(peers):
        spread[j] = out


def project(parts, out_weight, packed, heads, size):
    members = parts.shape[0]
    out = jax.ShapeDtypeStruct((members, packed, AUX), BF)
    return pl.pallas_call(
        functools.partial(project_kernel, heads=heads, size=size),
        grid=(1,),
        in_specs=whole([parts, out_weight]),
        out_specs=whole([out])[0],
        out_shape=out,
        compiler_params=PARAMS,
        cost_estimate=lasting(20),
        name="project",
    )(parts, out_weight)


def load_units(weights, gates, ups, downs, sems, units):
    copies = []
    begin = 0
    for w in weights:
        for first in range(0, w.shape[0], 3 * units):
            trio = []
            for k, to in enumerate((gates, ups, downs)):
                copy = pltpu.make_async_copy(
                    w.at[pl.ds(first + k * units, units), :],
                    to.at[pl.ds(begin, units), :],
                    sems.at[len(copies), k],
                )
                copy.start()
                trio.append(copy)
            begin += units
            copies.append((begin, trio))
    return copies


def use_units(second, copies, gates, ups, downs, chunk=256):
    acc = None
    ready = 0
    waiting = list(copies)
    for first in range(0, gates.shape[0], chunk):
        while ready < first + chunk:
            ready, trio = waiting.pop(0)
            for copy in trio:
                copy.wait()
        span = slice(first, first + chunk)
        gate = dot_nt(second, gates[span, :])
        up = dot_nt(second, ups[span, :])
        hidden = (gate / (1.0 + jnp.exp(-gate)) * up).astype(BF)
        part = dot_nn(hidden, downs[span, :])
        acc = part if acc is None else acc + part
    return acc


def feed_kernel(spread, embedded, gain, *refs, count, units):
    weights = refs[:count]
    out, mixed, gates, ups, downs, sems = refs[count:]
    copies = load_units(weights, gates, ups, downs, sems, units)
    tokens = embedded.shape[0]
    peers, own, _ = out.shape
    added = jnp.concatenate([unfold(spread[j].astype(F32), tokens) for j in range(peers)], axis=1)
    rows = (embedded[...].astype(F32) + added).astype(BF)
    mixed[...] = rows
    wide = rows.astype(F32)
    factor = lax.rsqrt(jnp.mean(wide * wide, axis=-1, keepdims=True) + 1e-05)
    rows_norm = (wide * factor * gain[...]).astype(BF)
    acc = use_units(rows_norm, copies, gates, ups, downs)
    for j in range(peers):
        out[j] = acc[j * own : (j + 1) * own, :].astype(BF)


def unit_scratch(weights, units):
    width = weights[0].shape[1]
    rows = sum(w.shape[0] for w in weights)
    count = rows // (3 * units)
    return [pltpu.VMEM((rows // 3, width), BF)] * 3 + [pltpu.SemaphoreType.DMA((count, 3))]


def feed(spread, embedded, gain, weights, units):
    members = spread.shape[0]
    tokens, width = embedded.shape
    outs = [
        jax.ShapeDtypeStruct((members, tokens // members, width), BF),
        jax.ShapeDtypeStruct(embedded.shape, BF),
    ]
    return pl.pallas_call(
        functools.partial(feed_kernel, count=len(weights), units=units),
        grid=(1,),
        in_specs=whole([spread, embedded, gain]) + streamed(len(weights)),
        out_specs=whole(outs),
        out_shape=outs,
        scratch_shapes=unit_scratch(weights, units),
        compiler_params=PARAMS,
        cost_estimate=lasting(20),
        name="feed",
    )(spread, embedded, gain, *weights)


def pack_kernel(gate, up, down, ready, low, high):
    half = low.shape[0] // 3
    for k, part in enumerate((gate, up, down)):
        low[k * half : (k + 1) * half] = part[:half]
        high[k * half : (k + 1) * half] = part[half:]


def pack(gate, up, down, ready):
    units, width = gate.shape
    out = jax.ShapeDtypeStruct((3 * units // 2, width), gate.dtype)
    return pl.pallas_call(
        pack_kernel,
        grid=(1,),
        in_specs=whole([gate, up, down]) + streamed(1),
        out_specs=whole([out, out]),
        out_shape=[out, out],
        compiler_params=PARAMS,
        cost_estimate=cost(0, 1024),
        name="pack",
    )(gate, up, down, ready)


def pick_kernel(turns, rows, *refs):
    held = refs[:-1]
    out = refs[-1]
    for i in range(out.shape[0]):
        for n, ref in enumerate(held):

            @pl.when(turns[i] == n)
            def _():
                out[i] = ref[rows[i]].astype(F32)


def pick_states(turns, rows, held, count):
    shape = (count,) + held[0].shape[1:]
    out = jax.ShapeDtypeStruct(shape, F32)
    return pl.pallas_call(
        pick_kernel,
        grid=(1,),
        in_specs=scalars(2) + whole(held),
        out_specs=whole([out])[0],
        out_shape=out,
        compiler_params=PARAMS,
        name="pick",
    )(turns, rows, *held)


def local(
    draft_ids,
    lengths,
    current_slot,
    new_slot,
    accepted,
    embed_table,
    mixer_gain,
    query_weight,
    keyvalue_weight,
    key_cache,
    value_cache,
    attention_out,
    mamba_input,
    mamba_gate,
    state_proj,
    mamba_step,
    step_bias,
    decay_log,
    skip_gain,
    states,
    mamba_out,
    mlp_gain,
    gate_weight,
    up_weight,
    down_weight,
):
    members = lax.axis_size("tok")
    groups = lax.axis_size(REQ)
    group_index = lax.axis_index(REQ)
    member = lax.axis_index("tok")
    slots_dev, cache_dev, head_size = key_cache.shape
    draft_len = draft_ids.shape[1]
    width = embed_table.shape[1]
    query_heads = query_weight.shape[1] // head_size
    own = slots_dev * draft_len // members

    cores = CORES
    chips = groups // cores

    def turn(value, by):
        return lax.ppermute(
            value, REQ, [(g, (g + by * cores) % groups) for g in range(groups)]
        )

    def across(value):
        return lax.ppermute(value, REQ, [(g, g ^ 1) for g in range(groups)])

    def exchange(turn):
        keep, give, places, origin, most = fetch(
            turn, current_slot[None], draft_ids.T, embed_table, groups, members
        )
        came = lax.all_to_all(keep + across(give), ("z", "tok"), 0, 0, tiled=True)
        return came, places, origin, most

    def plane(rows):
        return lax.all_to_all(rows, "tok", 0, 0, tiled=True)

    came, places, origin, most = exchange(jnp.zeros((1,), jnp.int32))

    low, high = pack(gate_weight.T, up_weight.T, down_weight.T, places)
    near_z = [turn(low, 1), turn(high, -1)]
    handed = hand(origin, came, members)
    later = lax.optimization_barrier((low, high, handed))
    near_z += [turn(later[1], 1), turn(later[0], -1)]
    weights = [low, high] + near_z
    arrived = plane(handed)

    def more(carry):
        return carry[0][0] < most[0]

    def round_of(carry):
        at, rows = carry
        later, spots, froms, _ = exchange(at)
        return at + 1, place(plane(hand(froms, later, members)), spots, rows)

    _, extra = lax.while_loop(
        more, round_of, (jnp.ones((1,), jnp.int32), jnp.zeros((members * own, width), BF))
    )

    slot_owner = inverse_of(current_slot)
    local_owner = lax.dynamic_slice_in_dim(slot_owner, group_index * slots_dev, slots_dev)
    ints = jnp.concatenate(
        [jnp.take(lengths, local_owner), jnp.take(accepted, local_owner), member[None]]
    )
    reals = jnp.concatenate([step_bias, jnp.exp(decay_log), skip_gain])
    payload, embedded, normed = attend(
        ints,
        arrived,
        places,
        extra,
        mixer_gain[None],
        query_weight,
        keyvalue_weight,
        key_cache,
        value_cache,
    )
    parts = lax.all_to_all(payload, "tok", 0, 0, tiled=True)
    later = lax.optimization_barrier((near_z[0], near_z[1], payload))
    far = [turn(later[0], 1), turn(later[1], -1)]
    blocks, chosen = mamba(
        ints,
        reals,
        normed,
        mamba_input,
        mamba_gate,
        state_proj,
        mamba_step.T,
        states,
        mamba_out,
        members,
        query_heads * own,
    )
    joint = join(parts, blocks, query_heads, head_size)
    joined = lax.all_to_all(joint, "tok", 0, 0, tiled=True)
    *later, chosen, _ = lax.optimization_barrier((*weights, chosen, joint))
    weights += [across(w) for w in later]
    chosen = chosen[:, 0]
    pair = jnp.concatenate([chosen, across(chosen)], axis=0)
    joined, *_ = lax.optimization_barrier((joined, *far))
    folded = members * own * (width // members) // AUX
    spread = project(joined, attention_out.T, folded, query_heads, head_size)
    first, second, spread, pair, *_ = lax.optimization_barrier((*far, spread, pair, *weights[-6:]))
    far = [first, second]
    weights += far + [across(w) for w in far]
    added = lax.all_to_all(spread, "tok", 0, 0, tiled=True)
    half = gate_weight.shape[1] // 2
    mlp_part, mixed = feed(added, embedded, mlp_gain[None], weights, half)
    mlp_rows = lax.all_to_all(mlp_part, "tok", 0, 0, tiled=True)
    own_rows = lax.optimization_barrier(lax.dynamic_slice_in_dim(mixed, member * own, own))
    hidden_out = (own_rows.astype(F32) + jnp.sum(mlp_rows.astype(F32), axis=0)).astype(BF)

    incoming = inverse_of(new_slot)
    local_targets = lax.dynamic_slice_in_dim(incoming, group_index * slots_dev, slots_dev)
    sources = jnp.take(current_slot, local_targets)
    held = [pair] + [turn(pair, by) for by in range(1, chips)]
    source_group = sources // slots_dev
    turns = (group_index // cores - source_group // cores) % chips
    other_core = (source_group % cores) != (group_index % cores)
    rows = sources % slots_dev + jnp.where(other_core, slots_dev, 0)
    new_states = pick_states(turns, rows, held, slots_dev)[:, None]
    return (hidden_out, new_states)


def solution(mesh):
    groups, members = mesh.devices.shape
    devices = mesh.devices.reshape(groups // CORES, CORES, members)
    mesh = Mesh(devices, ("z", "core", "tok"))
    return jax.shard_map(
        local,
        mesh=mesh,
        in_specs=(
            P(),
            P(),
            P(),
            P(),
            P(),
            P(("z", "core", "tok"), None),
            P(),
            P(),
            P(),
            P(REQ, "tok", None),
            P(REQ, "tok", None),
            P(None, "tok"),
            P(None, "tok"),
            P(None, "tok"),
            P(),
            P(None, "tok"),
            P("tok"),
            P("tok"),
            P("tok"),
            P(REQ, "tok", None, None),
            P("tok", None),
            P(),
            P(None, ("z", "core", "tok")),
            P(None, ("z", "core", "tok")),
            P(None, ("z", "core", "tok")),
        ),
        out_specs=(P(("z", "core", "tok"), None), P(REQ, "tok", None, None)),
        check_vma=False,
    )
```

```python
import functools

import jax
import jax.numpy as jnp
from jax import lax
from jax.experimental import pallas as pl
from jax.experimental.pallas import tpu as pltpu
from jax.sharding import PartitionSpec as P

BF = jnp.bfloat16
F32 = jnp.float32
NEG = -1e30
AUX = 128
VMEM = 63 << 10


def inverse_of(mapping):
    places = jnp.arange(mapping.shape[0], dtype=jnp.int32)
    matches = mapping[None, :] == places[:, None]
    return jnp.sum(jnp.where(matches, places[None, :], 0), axis=1)


def dot_nn(a, b, precision=None):
    return lax.dot_general(
        a, b, (((1,), (0,)), ((), ())), precision=precision, preferred_element_type=F32
    )


def dot_nt(a, b, precision=None):
    return lax.dot_general(
        a, b, (((1,), (1,)), ((), ())), precision=precision, preferred_element_type=F32
    )


def dot_tn(a, b, precision=None):
    return lax.dot_general(
        a, b, (((0,), (0,)), ((), ())), precision=precision, preferred_element_type=F32
    )


HI = lax.Precision.HIGHEST


def cost(flops, moved, special=0):
    return pl.CostEstimate(flops=flops, bytes_accessed=moved, transcendentals=special)


def lasting(microseconds):
    return cost(int(microseconds * 1e9), 1024)


def whole(shapes):
    return [pl.BlockSpec(a.shape, lambda i, n=len(a.shape): (0,) * n) for a in shapes]


def near(count):
    return [pl.BlockSpec(memory_space=pltpu.VMEM)] * count


def streamed(count):
    return [pl.BlockSpec(memory_space=pltpu.HBM)] * count


def scalars(count):
    return [pl.BlockSpec(memory_space=pltpu.SMEM)] * count


PARAMS = pltpu.CompilerParams(vmem_limit_bytes=VMEM << 10)
SMALL = pltpu.CompilerParams(vmem_limit_bytes=8 << 20)


def fetch_kernel(
    turn, slots_row, ids_cols, table_far, payload, places, origin, most, table, sem, *, groups, members
):
    load = pltpu.make_async_copy(table_far, table, sem)
    load.start()
    drafts, requests = ids_cols.shape
    vocab = table.shape[0]
    count = requests * drafts // groups
    slots = requests // groups
    group = lax.axis_index("req")
    member = lax.axis_index("tok")
    me = group * members + member
    now = turn[0]
    sub = lax.broadcasted_iota(jnp.int32, (count, count), 0)
    lane = lax.broadcasted_iota(jnp.int32, (count, count), 1)
    sub_c = sub[:, :1]
    lane_r = lane[:1, :]
    ids = ids_cols[...]
    ids_hi = (ids // 256).astype(F32).astype(BF)
    ids_lo = (ids % 256).astype(F32).astype(BF)
    row_slot = lax.broadcasted_iota(jnp.int32, (count, requests), 0) // drafts
    token = lax.broadcasted_iota(jnp.int32, (count, drafts), 0) % drafts
    token_lane = lax.broadcasted_iota(jnp.int32, (count, drafts), 1)
    column = lax.broadcasted_iota(jnp.int32, (members, count), 0)
    local_iota = lax.broadcasted_iota(jnp.int32, (members, vocab), 1)
    own = count // members
    hots = []
    own_place = jnp.zeros((count, 1), jnp.int32)
    own_from = [jnp.zeros((1, count), jnp.int32)] * own
    peak = jnp.zeros((1, count), jnp.int32)
    for g in range(groups):
        pick = jnp.where(slots_row[...] == row_slot + g * slots, 1.0, 0.0).astype(BF)
        mixed_ids = dot_nt(pick, ids_hi) * 256.0 + dot_nt(pick, ids_lo)
        id_c = jnp.sum(
            jnp.where(token == token_lane, mixed_ids, 0.0), axis=1, keepdims=True
        ).astype(jnp.int32)
        id_r = jnp.sum(jnp.where(sub == lane, id_c, 0), axis=0, keepdims=True)
        same = id_c == id_r
        first_c = jnp.min(jnp.where(same, lane, count), axis=1, keepdims=True)
        first_r = jnp.min(jnp.where(same, sub, count), axis=0, keepdims=True)
        owner_c = id_c // vocab
        owner_r = id_r // vocab
        alike = owner_c == owner_r
        before_r = (first_c == sub_c) & alike & (sub < first_r)
        less_r = (first_c == sub_c) & (owner_c < owner_r)
        nth_r = jnp.sum(jnp.where(before_r, 1, 0), axis=0, keepdims=True)
        rank_r = nth_r + jnp.sum(jnp.where(less_r, 1, 0), axis=0, keepdims=True)
        peak = jnp.maximum(peak, nth_r // members + 1)
        before_c = (first_r == lane_r) & alike & (lane < first_c)
        less_c = (first_r == lane_r) & (owner_r < owner_c)
        nth_c = jnp.sum(jnp.where(before_c, 1, 0), axis=1, keepdims=True)
        rank_c = nth_c + jnp.sum(jnp.where(less_c, 1, 0), axis=1, keepdims=True)
        spot = (rank_c % members) * own + rank_c // members
        spot = jnp.where(nth_c // members == now, spot, -1)
        own_place = jnp.where(group == g, spot, own_place)
        sent_r = (first_r == lane_r) & (nth_r // members == now)
        asked = sent_r & (owner_r == me) & (rank_r % members == column)
        row = jnp.sum(jnp.where(asked, id_r % vocab + 1, 0), axis=1, keepdims=True) - 1
        hots.append(jnp.where(local_iota == row, 1.0, 0.0))
        for k in range(own):
            here = sent_r & (rank_r == k * members + member) & (group == g)
            own_from[k] = own_from[k] + jnp.where(here, owner_r + 1, 0)
    places[...] = jnp.broadcast_to(own_place, places.shape)
    for k in range(own):
        origin[k] = jnp.sum(own_from[k]) - 1
    most[0] = jnp.max(peak)
    hot = jnp.concatenate(hots, axis=0).astype(BF)
    load.wait()
    payload[...] = dot_nn(hot, table[...]).reshape(payload.shape).astype(BF)


def fetch(turn, slots_row, ids_cols, table, groups, members):
    count = ids_cols.size // groups
    outs = [
        jax.ShapeDtypeStruct((groups * members, table.shape[1] // AUX, AUX), BF),
        jax.ShapeDtypeStruct((count, AUX), jnp.int32),
        jax.ShapeDtypeStruct((count // members,), jnp.int32),
        jax.ShapeDtypeStruct((1,), jnp.int32),
    ]
    return pl.pallas_call(
        functools.partial(fetch_kernel, groups=groups, members=members),
        grid=(1,),
        in_specs=scalars(1) + whole([slots_row, ids_cols]) + streamed(1),
        out_specs=whole(outs[:2]) + scalars(2),
        out_shape=outs,
        scratch_shapes=[pltpu.VMEM(table.shape, table.dtype), pltpu.SemaphoreType.DMA],
        compiler_params=PARAMS,
        cost_estimate=cost(2 * groups * members * table.size, 2 * table.size),
        name="fetch",
    )(turn, slots_row, ids_cols, table)


def hand_kernel(origin, came, spread):
    peers, own, lines = spread.shape[0], origin.shape[0], came.shape[1]
    for k in range(own):
        source = origin[k]
        row = came[jnp.maximum(source, 0)]
        row = jnp.where(source >= 0, row.astype(F32), 0.0).astype(BF)
        for j in range(peers):
            spread[j, k * lines : (k + 1) * lines, :] = row


def hand(origin, came, members):
    own = origin.shape[0]
    out = jax.ShapeDtypeStruct((members, own * came.shape[1], AUX), BF)
    return pl.pallas_call(
        hand_kernel,
        in_specs=scalars(1) + near(1),
        out_specs=near(1)[0],
        out_shape=out,
        compiler_params=SMALL,
        cost_estimate=lasting(10),
        name="hand",
    )(origin, came)


def rows_of(arrived, places):
    count = places.shape[0]
    width = arrived.size // count
    slot = lax.broadcasted_iota(jnp.int32, (count, count), 1)
    hot = jnp.where(slot == places[:, :1], 1.0, 0.0).astype(BF)
    lines = arrived[...].astype(F32).reshape(count, width // AUX, AUX)
    return dot_nn(hot, lines.reshape(count, width).astype(BF))


def place_kernel(arrived, places, before, out):
    out[...] = (before[...].astype(F32) + rows_of(arrived, places)).astype(BF)


def place(arrived, places, before):
    return pl.pallas_call(
        place_kernel,
        grid=(1,),
        in_specs=whole([arrived, places, before]),
        out_specs=whole([before])[0],
        out_shape=jax.ShapeDtypeStruct(before.shape, BF),
        compiler_params=PARAMS,
        name="place",
    )(arrived, places, before)


def attend_kernel(
    ints,
    arrived,
    places,
    extra,
    gain,
    query_weight,
    keyvalue_weight,
    keys,
    values,
    payload,
    embedded,
    normed,
    query_in,
    keyvalue_in,
    keys_in,
    values_in,
    sems,
):
    moves = []
    third = query_weight.shape[0] // 3
    for k in range(3):
        span = pl.ds(k * third, third)
        moves.append((query_weight.at[span, :], query_in.at[span, :]))
    moves += [(keyvalue_weight, keyvalue_in), (keys, keys_in), (values, values_in)]
    copies = [pltpu.make_async_copy(a, b, sems.at[n]) for n, (a, b) in enumerate(moves)]
    for copy in copies:
        copy.start()
    slots, cache, size = keys.shape
    tokens = extra.shape[0]
    drafts = tokens // slots
    heads = query_weight.shape[1] // size
    own = payload.shape[1]
    rows_in = (rows_of(arrived, places) + extra[...].astype(F32)).astype(BF)
    embedded[...] = rows_in
    wide = rows_in.astype(F32)
    factor = lax.rsqrt(jnp.mean(wide * wide, axis=-1, keepdims=True) + 1e-05)
    rows_norm = (wide * factor * gain[...]).astype(BF)
    normed[...] = rows_norm
    queries = None
    for k in range(3):
        copies[k].wait()
        span = slice(k * third, (k + 1) * third)
        part = dot_nn(rows_norm[:, span], query_in[span, :])
        queries = part if queries is None else queries + part
    queries = queries.astype(BF)
    copies[3].wait()
    keyvalue = dot_nn(rows_norm, keyvalue_in[...]).astype(BF)
    copies[4].wait()
    copies[5].wait()
    member = ints[8]
    scale = size ** (-0.5)
    rows = heads * drafts
    position = lax.broadcasted_iota(jnp.int32, (rows, cache), 1) + member * cache
    token = lax.broadcasted_iota(jnp.int32, (rows, drafts), 0) % drafts
    other = lax.broadcasted_iota(jnp.int32, (rows, drafts), 1)
    seen = other <= jnp.where(member == 0, token, -1)
    lane = lax.broadcasted_iota(jnp.int32, (drafts, AUX), 1)
    for slot in range(slots):
        span = slice(slot * drafts, (slot + 1) * drafts)
        length = ints[slot]
        query = jnp.concatenate(
            [queries[span, h * size : (h + 1) * size] for h in range(heads)], axis=0
        )
        scores = dot_nt(query, keys_in[slot]) * scale
        scores = jnp.where(position < length, scores, NEG)
        draft_scores = dot_nt(query, keyvalue[span, :size]) * scale
        draft_scores = jnp.where(seen, draft_scores, NEG)
        top = jnp.maximum(
            jnp.max(scores, axis=-1, keepdims=True),
            jnp.max(draft_scores, axis=-1, keepdims=True),
        )
        probs = jnp.where(position < length, jnp.exp(scores - top), 0.0)
        draft_probs = jnp.where(seen, jnp.exp(draft_scores - top), 0.0)
        total = jnp.sum(probs, axis=-1, keepdims=True) + jnp.sum(
            draft_probs, axis=-1, keepdims=True
        )
        summed = dot_nn(probs.astype(BF), values_in[slot]) + dot_nn(
            draft_probs.astype(BF), keyvalue[span, size:]
        )
        top_a = top.astype(BF).astype(F32)
        top_b = (top - top_a).astype(BF).astype(F32)
        top_c = top - top_a - top_b
        total_a = total.astype(BF).astype(F32)
        total_b = total - total_a
        aux = jnp.zeros((drafts, AUX), F32)
        for k, piece in enumerate((top_a, top_b, top_c, total_a, total_b)):
            for h in range(heads):
                part = piece[h * drafts : (h + 1) * drafts]
                aux = jnp.where(lane == k * heads + h, part, aux)
        flat = jnp.concatenate(
            [summed[h * drafts : (h + 1) * drafts] for h in range(heads)] + [aux], axis=1
        ).astype(BF)
        for q in range(drafts // own):
            payload[slot * (drafts // own) + q] = flat[q * own : (q + 1) * own]


def attend(ints, arrived, places, extra, gain, query_weight, keyvalue_weight, keys, values):
    tokens, width = extra.shape
    members = arrived.shape[0]
    wide = query_weight.shape[1] + AUX
    far = (query_weight, keyvalue_weight, keys, values)
    outs = [
        jax.ShapeDtypeStruct((members, tokens // members, wide), BF),
        jax.ShapeDtypeStruct((tokens, width), BF),
        jax.ShapeDtypeStruct((tokens, width), BF),
    ]
    return pl.pallas_call(
        attend_kernel,
        grid=(1,),
        in_specs=scalars(1) + whole([arrived, places, extra, gain]) + streamed(4),
        out_specs=whole(outs),
        out_shape=outs,
        scratch_shapes=[pltpu.VMEM(a.shape, a.dtype) for a in far]
        + [pltpu.SemaphoreType.DMA((6,))],
        compiler_params=PARAMS,
        cost_estimate=lasting(20),
        name="attend",
    )(ints, arrived, places, extra, gain, query_weight, keyvalue_weight, keys, values)


def fold(block):
    half = block.shape[0] // 2
    rest = jnp.concatenate([block[:half, AUX:], block[half:, AUX:]], axis=1)
    return jnp.concatenate([block[:, :AUX], rest], axis=0)


def unfold(block, tokens):
    half = AUX // 2
    rest = jnp.concatenate([block[tokens:, :half], block[tokens:, half:]], axis=0)
    return jnp.concatenate([block[:tokens], rest], axis=1)


def mamba_kernel(
    ints,
    reals,
    normed,
    input_weight,
    gate_weight,
    state_proj,
    step_row,
    states,
    mamba_out,
    blocks,
    chosen,
    proj_in,
    input_in,
    gate_in,
    states_in,
    out_in,
    sems,
):
    moves = (
        (state_proj, proj_in),
        (input_weight, input_in),
        (gate_weight, gate_in),
        (states, states_in),
        (mamba_out, out_in),
    )
    copies = [pltpu.make_async_copy(a, b, sems.at[n]) for n, (a, b) in enumerate(moves)]
    for copy in copies:
        copy.start()
    slots = states.shape[0]
    tokens = normed.shape[0]
    drafts = tokens // slots
    rows = normed[...]
    step_in = (
        jnp.sum(rows.astype(F32) * step_row[...].astype(F32), axis=1, keepdims=True) + reals[0]
    )
    sizes = jnp.maximum(step_in, 0.0) + jnp.log1p(jnp.exp(-jnp.abs(step_in)))
    copies[0].wait()
    both = dot_nn(rows, proj_in[...])
    copies[1].wait()
    x_all = dot_nn(rows, input_in[...])
    copies[2].wait()
    z_all = dot_nn(rows, gate_in[...])
    copies[3].wait()
    state_size = both.shape[1] // 2
    row = lax.broadcasted_iota(jnp.int32, (drafts, drafts), 0)
    col = lax.broadcasted_iota(jnp.int32, (drafts, drafts), 1)
    rows_in = lax.broadcasted_iota(jnp.int32, (drafts, 1), 0)
    gated = []
    for slot in range(slots):
        span = slice(slot * drafts, (slot + 1) * drafts)
        accept = ints[4 + slot]
        size_t = sizes[span]
        size_row = jnp.sum(jnp.where(row == col, size_t, 0.0), axis=0, keepdims=True)
        log_decay = -reals[1] * jnp.sum(
            jnp.where(col <= row, size_row, 0.0), axis=1, keepdims=True
        )
        log_row = jnp.sum(jnp.where(row == col, log_decay, 0.0), axis=0, keepdims=True)
        between = jnp.exp(jnp.where(col <= row, log_decay - log_row, NEG))
        state_in = both[span, :state_size]
        state_read = both[span, state_size:]
        x = x_all[span]
        z = z_all[span]
        inputs = size_t * x
        start = states_in[slot, 0]
        weights = dot_nt(state_read, state_in, HI) * between
        readout = dot_nn(weights, inputs, HI) + jnp.exp(log_decay) * dot_nt(
            state_read, start, HI
        )
        readout = readout + reals[2] * x
        last = jnp.sum(jnp.where(rows_in == accept - 1, log_decay, 0.0), axis=0, keepdims=True)
        remain = jnp.exp(jnp.where(rows_in < accept, last - log_decay, NEG))
        chosen[slot, 0] = (
            jnp.exp(last) * start + dot_tn(remain * inputs, state_in, HI)
        ).astype(BF)
        gated.append((readout * (z / (1.0 + jnp.exp(-z)))).astype(BF))
    copies[4].wait()
    part = dot_nn(jnp.concatenate(gated, axis=0), out_in[...])
    share = part.shape[1] // blocks.shape[0]
    for j in range(blocks.shape[0]):
        block = fold(part[:, j * share : (j + 1) * share]).astype(BF)
        blocks[j, : block.shape[0]] = block
        blocks[j, block.shape[0] :] = jnp.zeros_like(blocks[j, block.shape[0] :])


def mamba(
    ints,
    reals,
    normed,
    input_weight,
    gate_weight,
    state_proj,
    step_row,
    states,
    mamba_out,
    members,
    room,
):
    tokens = normed.shape[0]
    share = mamba_out.shape[1] // members
    outs = [
        jax.ShapeDtypeStruct((members, tokens * share // AUX + room, AUX), BF),
        jax.ShapeDtypeStruct(states.shape, BF),
    ]
    far = (state_proj, input_weight, gate_weight, states, mamba_out)
    return pl.pallas_call(
        mamba_kernel,
        grid=(1,),
        in_specs=scalars(2)
        + whole([normed])
        + streamed(3)
        + whole([step_row])
        + streamed(2),
        out_specs=whole(outs),
        out_shape=outs,
        scratch_shapes=[pltpu.VMEM(a.shape, a.dtype) for a in far]
        + [pltpu.SemaphoreType.DMA((5,))],
        compiler_params=PARAMS,
        cost_estimate=lasting(8),
        name="mamba",
    )(ints, reals, normed, input_weight, gate_weight, state_proj, step_row, states, mamba_out)


def join_kernel(parts, blocks, payload, piece, sem, *, heads, size):
    peers, own, _ = parts.shape
    rows = heads * own
    aux = parts[:, :, heads * size : heads * size + AUX].astype(F32)
    get = lambda k: aux[:, :, k * heads : (k + 1) * heads]
    top = get(0) + get(1) + get(2)
    total = get(3) + get(4)
    factors = jnp.exp(top - jnp.max(top, axis=0, keepdims=True))
    factors = factors / jnp.sum(factors * total, axis=0, keepdims=True)
    for h in range(heads):
        value = parts[:, :, h * size : (h + 1) * size].astype(F32)
        summed = jnp.sum(factors[:, :, h : h + 1] * value, axis=0)
        piece[h * own : (h + 1) * own, :] = summed.astype(BF)
    first = payload.shape[1] - rows
    copies = [
        pltpu.make_async_copy(piece, payload.at[j, pl.ds(first, rows), :], sem.at[j])
        for j in range(peers)
    ]
    for copy in copies:
        copy.start()
    for copy in copies:
        copy.wait()


def join(parts, blocks, heads, size):
    peers, own, _ = parts.shape
    return pl.pallas_call(
        functools.partial(join_kernel, heads=heads, size=size),
        grid=(1,),
        in_specs=whole([parts]) + streamed(1),
        out_specs=streamed(1)[0],
        out_shape=jax.ShapeDtypeStruct(blocks.shape, BF),
        input_output_aliases={1: 0},
        scratch_shapes=[
            pltpu.VMEM((heads * own, size), BF),
            pltpu.SemaphoreType.DMA((peers,)),
        ],
        compiler_params=PARAMS,
        cost_estimate=lasting(20),
        name="join",
    )(parts, blocks)


def project_kernel(parts, out_weight, spread, *, heads, size):
    peers, packed, _ = spread.shape
    own = (parts.shape[1] - packed) // heads
    tokens = own * peers
    acc = unfold(jnp.sum(parts[:, :packed, :].astype(F32), axis=0), tokens)
    for h in range(heads):
        attended = jnp.concatenate(
            [parts[j, packed + h * own : packed + (h + 1) * own, :size] for j in range(peers)],
            axis=0,
        )
        acc = acc + dot_nt(attended, out_weight[:, h * size : (h + 1) * size])
    out = fold(acc).astype(BF)
    for j in range(peers):
        spread[j] = out


def project(parts, out_weight, packed, heads, size):
    members = parts.shape[0]
    out = jax.ShapeDtypeStruct((members, packed, AUX), BF)
    return pl.pallas_call(
        functools.partial(project_kernel, heads=heads, size=size),
        grid=(1,),
        in_specs=whole([parts, out_weight]),
        out_specs=whole([out])[0],
        out_shape=out,
        compiler_params=PARAMS,
        cost_estimate=lasting(20),
        name="project",
    )(parts, out_weight)


def load_units(weights, gates, ups, downs, sems, units):
    copies = []
    begin = 0
    for w in weights:
        for first in range(0, w.shape[0], 3 * units):
            trio = []
            for k, to in enumerate((gates, ups, downs)):
                copy = pltpu.make_async_copy(
                    w.at[pl.ds(first + k * units, units), :],
                    to.at[pl.ds(begin, units), :],
                    sems.at[len(copies), k],
                )
                copy.start()
                trio.append(copy)
            begin += units
            copies.append((begin, trio))
    return copies


def use_units(second, copies, gates, ups, downs, chunk=256):
    acc = None
    ready = 0
    waiting = list(copies)
    for first in range(0, gates.shape[0], chunk):
        while ready < first + chunk:
            ready, trio = waiting.pop(0)
            for copy in trio:
                copy.wait()
        span = slice(first, first + chunk)
        gate = dot_nt(second, gates[span, :])
        up = dot_nt(second, ups[span, :])
        hidden = (gate / (1.0 + jnp.exp(-gate)) * up).astype(BF)
        part = dot_nn(hidden, downs[span, :])
        acc = part if acc is None else acc + part
    return acc


def feed_kernel(spread, embedded, gain, *refs, count, units):
    weights = refs[:count]
    out, mixed, gates, ups, downs, sems = refs[count:]
    copies = load_units(weights, gates, ups, downs, sems, units)
    tokens = embedded.shape[0]
    peers, own, _ = out.shape
    added = jnp.concatenate([unfold(spread[j].astype(F32), tokens) for j in range(peers)], axis=1)
    rows = (embedded[...].astype(F32) + added).astype(BF)
    mixed[...] = rows
    wide = rows.astype(F32)
    factor = lax.rsqrt(jnp.mean(wide * wide, axis=-1, keepdims=True) + 1e-05)
    rows_norm = (wide * factor * gain[...]).astype(BF)
    acc = use_units(rows_norm, copies, gates, ups, downs)
    for j in range(peers):
        out[j] = acc[j * own : (j + 1) * own, :].astype(BF)


def unit_scratch(weights, units):
    width = weights[0].shape[1]
    rows = sum(w.shape[0] for w in weights)
    count = rows // (3 * units)
    return [pltpu.VMEM((rows // 3, width), BF)] * 3 + [pltpu.SemaphoreType.DMA((count, 3))]


def feed(spread, embedded, gain, weights, units):
    members = spread.shape[0]
    tokens, width = embedded.shape
    outs = [
        jax.ShapeDtypeStruct((members, tokens // members, width), BF),
        jax.ShapeDtypeStruct(embedded.shape, BF),
    ]
    return pl.pallas_call(
        functools.partial(feed_kernel, count=len(weights), units=units),
        grid=(1,),
        in_specs=whole([spread, embedded, gain]) + streamed(len(weights)),
        out_specs=whole(outs),
        out_shape=outs,
        scratch_shapes=unit_scratch(weights, units),
        compiler_params=PARAMS,
        cost_estimate=lasting(20),
        name="feed",
    )(spread, embedded, gain, *weights)


def pack_kernel(gate, up, down, ready, low, high):
    half = low.shape[0] // 3
    for k, part in enumerate((gate, up, down)):
        low[k * half : (k + 1) * half] = part[:half]
        high[k * half : (k + 1) * half] = part[half:]


def pack(gate, up, down, ready):
    units, width = gate.shape
    out = jax.ShapeDtypeStruct((3 * units // 2, width), gate.dtype)
    return pl.pallas_call(
        pack_kernel,
        grid=(1,),
        in_specs=whole([gate, up, down]) + streamed(1),
        out_specs=whole([out, out]),
        out_shape=[out, out],
        compiler_params=PARAMS,
        cost_estimate=cost(0, 1024),
        name="pack",
    )(gate, up, down, ready)


def pick_kernel(turns, rows, *refs):
    held = refs[:-1]
    out = refs[-1]
    for i in range(out.shape[0]):
        for n, ref in enumerate(held):

            @pl.when(turns[i] == n)
            def _():
                out[i] = ref[rows[i]].astype(F32)


def pick_states(turns, rows, held, count):
    shape = (count,) + held[0].shape[1:]
    out = jax.ShapeDtypeStruct(shape, F32)
    return pl.pallas_call(
        pick_kernel,
        grid=(1,),
        in_specs=scalars(2) + whole(held),
        out_specs=whole([out])[0],
        out_shape=out,
        compiler_params=PARAMS,
        name="pick",
    )(turns, rows, *held)


def local(
    draft_ids,
    lengths,
    current_slot,
    new_slot,
    accepted,
    embed_table,
    mixer_gain,
    query_weight,
    keyvalue_weight,
    key_cache,
    value_cache,
    attention_out,
    mamba_input,
    mamba_gate,
    state_proj,
    mamba_step,
    step_bias,
    decay_log,
    skip_gain,
    states,
    mamba_out,
    mlp_gain,
    gate_weight,
    up_weight,
    down_weight,
):
    members = lax.axis_size("tok")
    groups = lax.axis_size("req")
    group_index = lax.axis_index("req")
    member = lax.axis_index("tok")
    slots_dev, cache_dev, head_size = key_cache.shape
    draft_len = draft_ids.shape[1]
    width = embed_table.shape[1]
    query_heads = query_weight.shape[1] // head_size
    own = slots_dev * draft_len // members

    cores = 2
    chips = groups // cores

    def turn(value, by):
        return lax.ppermute(
            value, "req", [(g, (g + by * cores) % groups) for g in range(groups)]
        )

    def across(value):
        return lax.ppermute(value, "req", [(g, g ^ 1) for g in range(groups)])

    def exchange(turn):
        sent, places, origin, most = fetch(
            turn, current_slot[None], draft_ids.T, embed_table, groups, members
        )
        came = lax.all_to_all(sent, ("req", "tok"), 0, 0, tiled=True)
        return came, places, origin, most

    def plane(rows):
        return lax.all_to_all(rows, "tok", 0, 0, tiled=True)

    came, places, origin, most = exchange(jnp.zeros((1,), jnp.int32))

    low, high = pack(gate_weight.T, up_weight.T, down_weight.T, places)
    near_z = [turn(low, 1), turn(high, -1)]
    handed = hand(origin, came, members)
    later = lax.optimization_barrier((low, high, handed))
    near_z += [turn(later[1], 1), turn(later[0], -1)]
    weights = [low, high] + near_z
    arrived = plane(handed)

    def more(carry):
        return carry[0][0] < most[0]

    def round_of(carry):
        at, rows = carry
        later, spots, froms, _ = exchange(at)
        return at + 1, place(plane(hand(froms, later, members)), spots, rows)

    _, extra = lax.while_loop(
        more, round_of, (jnp.ones((1,), jnp.int32), jnp.zeros((members * own, width), BF))
    )

    slot_owner = inverse_of(current_slot)
    local_owner = lax.dynamic_slice_in_dim(slot_owner, group_index * slots_dev, slots_dev)
    ints = jnp.concatenate(
        [jnp.take(lengths, local_owner), jnp.take(accepted, local_owner), member[None]]
    )
    reals = jnp.concatenate([step_bias, jnp.exp(decay_log), skip_gain])
    payload, embedded, normed = attend(
        ints,
        arrived,
        places,
        extra,
        mixer_gain[None],
        query_weight,
        keyvalue_weight,
        key_cache,
        value_cache,
    )
    parts = lax.all_to_all(payload, "tok", 0, 0, tiled=True)
    later = lax.optimization_barrier((near_z[0], near_z[1], payload))
    far = [turn(later[0], 1), turn(later[1], -1)]
    blocks, chosen = mamba(
        ints,
        reals,
        normed,
        mamba_input,
        mamba_gate,
        state_proj,
        mamba_step.T,
        states,
        mamba_out,
        members,
        query_heads * own,
    )
    joint = join(parts, blocks, query_heads, head_size)
    joined = lax.all_to_all(joint, "tok", 0, 0, tiled=True)
    *later, chosen, _ = lax.optimization_barrier((*weights, chosen, joint))
    weights += [across(w) for w in later]
    chosen = chosen[:, 0]
    pair = jnp.concatenate([chosen, across(chosen)], axis=0)
    joined, *_ = lax.optimization_barrier((joined, *far))
    folded = members * own * (width // members) // AUX
    spread = project(joined, attention_out.T, folded, query_heads, head_size)
    first, second, spread, pair, *_ = lax.optimization_barrier((*far, spread, pair, *weights[-6:]))
    far = [first, second]
    weights += far + [across(w) for w in far]
    added = lax.all_to_all(spread, "tok", 0, 0, tiled=True)
    half = gate_weight.shape[1] // 2
    mlp_part, mixed = feed(added, embedded, mlp_gain[None], weights, half)
    mlp_rows = lax.all_to_all(mlp_part, "tok", 0, 0, tiled=True)
    own_rows = lax.optimization_barrier(lax.dynamic_slice_in_dim(mixed, member * own, own))
    hidden_out = (own_rows.astype(F32) + jnp.sum(mlp_rows.astype(F32), axis=0)).astype(BF)

    incoming = inverse_of(new_slot)
    local_targets = lax.dynamic_slice_in_dim(incoming, group_index * slots_dev, slots_dev)
    sources = jnp.take(current_slot, local_targets)
    held = [pair] + [turn(pair, by) for by in range(1, chips)]
    source_group = sources // slots_dev
    turns = (group_index // cores - source_group // cores) % chips
    other_core = (source_group % cores) != (group_index % cores)
    rows = sources % slots_dev + jnp.where(other_core, slots_dev, 0)
    new_states = pick_states(turns, rows, held, slots_dev)[:, None]
    return (hidden_out, new_states)


def solution(mesh):
    return jax.shard_map(
        local,
        mesh=mesh,
        in_specs=(
            P(),
            P(),
            P(),
            P(),
            P(),
            P(("req", "tok"), None),
            P(),
            P(),
            P(),
            P("req", "tok", None),
            P("req", "tok", None),
            P(None, "tok"),
            P(None, "tok"),
            P(None, "tok"),
            P(),
            P(None, "tok"),
            P("tok"),
            P("tok"),
            P("tok"),
            P("req", "tok", None, None),
            P("tok", None),
            P(),
            P(None, ("req", "tok")),
            P(None, ("req", "tok")),
            P(None, ("req", "tok")),
        ),
        out_specs=(P(("req", "tok"), None), P("req", "tok", None, None)),
        check_vma=False,
    )
```
